32 devices in a mesh: dp: 8 (over z, y), tensor: 4 (over x, core).
Axes of the slice: x: 2, y: 2, z: 4, core: 2. Of those that a mesh axis runs over, the one named last changes fastest.
Arguments:
- block_input: bfloat16 [8192, 1536], P('dp'), may hold values from -6 to 6
- segments: int32 [8192], P('dp'), may hold values from 0 to 31, never falling along the last dimension, each value on 1 to 2048 neighbouring positions
- positions: int32 [8192], P('dp'), may hold values from 0 to 1023
- norm1_gain: float32 [1536], P('dp'), may hold values from 0.5 to 1.5
- q_norm_gain: float32 [64], P('dp'), may hold values from 0.5 to 1.5
- k_norm_gain: float32 [64], P('dp'), may hold values from 0.5 to 1.5
- w_q: float32 [1536, 1536], P('dp', 'tensor'), may hold values from -0.15625 to 0.15625
- w_k: float32 [1536, 512], P('dp', 'tensor'), may hold values from -0.15625 to 0.15625
- w_v: float32 [1536, 512], P('dp', 'tensor'), may hold values from -0.15625 to 0.15625
- w_o: float32 [1536, 1536], P('tensor', 'dp'), may hold values from -0.625 to 0.625
- norm2_gain: float32 [1536], P('dp'), may hold values from 0.5 to 1.5
- w_gate: float32 [1536, 6912], P('dp', 'tensor'), may hold values from -0.15625 to 0.15625
- w_up: float32 [1536, 6912], P('dp', 'tensor'), may hold values from -0.15625 to 0.15625
- w_down: float32 [6912, 1536], P('tensor', 'dp'), may hold values from -0.078125 to 0.078125
- cotangent: bfloat16 [8192, 1536], P('dp'), may hold values from -6 to 6
Outputs:
- block_output: bfloat16 [8192, 1536], P('dp')
- input_grad: float32 [8192, 1536], P('dp')
- norm1_gain_grad: float32 [1536], P('dp')
- q_norm_gain_grad: float32 [64], P('dp')
- k_norm_gain_grad: float32 [64], P('dp')
- w_q_grad: float32 [1536, 1536], P('dp', 'tensor')
- w_k_grad: float32 [1536, 512], P('dp', 'tensor')
- w_v_grad: float32 [1536, 512], P('dp', 'tensor')
- w_o_grad: float32 [1536, 1536], P('tensor', 'dp')
- norm2_gain_grad: float32 [1536], P('dp')
- w_gate_grad: float32 [1536, 6912], P('dp', 'tensor')
- w_up_grad: float32 [1536, 6912], P('dp', 'tensor')
- w_down_grad: float32 [6912, 1536], P('tensor', 'dp')
The draws below stay inside these ranges and needn't reach their ends.
Inputs may be any that keep to these rules, and one draw needn't show every extreme that they name: `segments`: segment numbers never fall along the tokens; a document holds at most 2048 tokens, and some document holds exactly that many; a document that runs across the end of a 1024-token sequence is attended only within each sequence.
All inputs are finite; a program needn't handle non-finite values.
Results may differ from the reference program's by a relative error of at most 0.014.
The reference program's roundings to bfloat16 on the way count: a program that leaves them out, or rounds other values in their place, can miss the bound.
Values may be sent and summed in bfloat16 or wider, within the bound.
A program may use at most 192 MiB of HBM per device.

```python
import math
import jax
import jax.numpy as jnp
import numpy as np
from jax import lax

D = 1536
HEADS = 24
KV = 8
HD = 64
FF = 6912
SEQ = 1024
TOKENS = 8192
DOCS = 32
N_DP = 8


def with_ends(values, own_key, low, largest):
    index_at = [jax.random.randint(jax.random.fold_in(own_key, axis), (), 0, length) for axis, length in enumerate(values.shape)]
    main_axis = values.shape.index(max(values.shape))
    beside = index_at[:main_axis] + [(index_at[main_axis] + 1) % values.shape[main_axis]] + index_at[main_axis + 1:]
    return values.at[tuple(index_at)].set(low).at[tuple(beside)].set(largest)


def block_scale(key, dims, split, low, top_value):
    def one(dim, parts):
        steps = jax.random.uniform(jax.random.fold_in(jax.random.fold_in(key, 6), dim), (parts,), jnp.float32, low / len(split), top_value / len(split))
        return jnp.repeat(jnp.exp(steps), dims[dim] // parts).reshape((-1,) + (1,) * (len(dims) - dim - 1))

    level = one(*split[0])
    for cut in split[1:]:
        level = level * one(*cut)
    return level


def length_profile(amount, total, reach, slope):
    portions = [(1 << 20) // math.isqrt(grade ** slope) + 1 for grade in range(2, amount + 1)]
    rest, counts = total - reach - (amount - 1), [1] * (amount - 1)
    while rest > 0:
        candidates = [i for i in range(amount - 1) if counts[i] < reach]
        whole, budget = sum([portions[i] for i in candidates]), rest
        for i in candidates:
            addition = min(reach - counts[i], max(1, budget * portions[i] // whole), rest)
            counts[i] = counts[i] + addition
            rest = rest - addition
    return np.array([reach] + counts)


def ragged(rng, number_of, total, limit, slope):
    if number_of == 2:
        one = jax.random.randint(rng, (), max(1, total - limit), min(limit, total - 1) + 1)
        return jnp.stack([one, total - one])
    lengths = jnp.asarray(length_profile(number_of, total, limit, slope), jnp.int32)
    couples = (number_of - 1) // 2
    source_of, receiver = lengths[1:1 + 2 * couples:2], lengths[2:2 + 2 * couples:2]
    margin = jnp.minimum(source_of - 1, limit - receiver)
    passed = jax.random.randint(jax.random.fold_in(rng, 1), (couples,), 0, 1 << 20) % (margin + 1)
    lengths = lengths.at[1:1 + 2 * couples:2].set(source_of - passed).at[2:2 + 2 * couples:2].set(receiver + passed)
    return lengths[jax.random.permutation(jax.random.fold_in(rng, 2), number_of)]


def centred(stream_key, dims, spread, bound, shards=(), kind=jnp.bfloat16):
    entries = spread * jax.random.normal(stream_key, dims, jnp.float32)
    if shards:
        entries = entries * block_scale(stream_key, dims, shards, -0.22, 0.18)
    return jnp.clip(entries, -bound, bound).astype(kind)


def setup_inputs(seed: int = 0) -> dict:
    seeds = jax.random.split(jax.random.key(seed), 16)
    return {
        "block_input": centred(seeds[0], (TOKENS, D), 1.0, 6.0, ((0, 8),)),
        "segments": jnp.searchsorted(jnp.cumsum(ragged(seeds[1], DOCS, TOKENS, 2 * SEQ, 2)), jnp.arange(TOKENS), side="right").astype(jnp.int32),
        "positions": with_ends(jax.random.randint(seeds[2], (TOKENS,), 0, SEQ), jax.random.fold_in(seeds[2], 1), 0, SEQ - 1).astype(jnp.int32),
        "norm1_gain": jnp.clip(1.0 + 0.1 * jax.random.normal(seeds[3], (D,), jnp.float32), 0.5, 1.5),
        "q_norm_gain": jnp.clip(1.0 + 0.1 * jax.random.normal(seeds[4], (HD,), jnp.float32), 0.5, 1.5),
        "k_norm_gain": jnp.clip(1.0 + 0.1 * jax.random.normal(seeds[5], (HD,), jnp.float32), 0.5, 1.5),
        "w_q": centred(seeds[6], (D, HEADS * HD), D ** -0.5, 0.15625, ((0, 8), (1, 4)), jnp.float32),
        "w_k": centred(seeds[7], (D, KV * HD), D ** -0.5, 0.15625, ((0, 8), (1, 4)), jnp.float32),
        "w_v": centred(seeds[8], (D, KV * HD), D ** -0.5, 0.15625, ((0, 8), (1, 4)), jnp.float32),
        "w_o": centred(seeds[9], (HEADS * HD, D), (HEADS * HD // 16) ** -0.5, 0.625, ((0, 4), (1, 8)), jnp.float32),
        "norm2_gain": jnp.clip(1.0 + 0.1 * jax.random.normal(seeds[10], (D,), jnp.float32), 0.5, 1.5),
        "w_gate": centred(seeds[11], (D, FF), D ** -0.5, 0.15625, ((0, 8), (1, 4)), jnp.float32),
        "w_up": centred(seeds[12], (D, FF), D ** -0.5, 0.15625, ((0, 8), (1, 4)), jnp.float32),
        "w_down": centred(seeds[13], (FF, D), FF ** -0.5, 0.078125, ((0, 4), (1, 8)), jnp.float32),
        "cotangent": centred(seeds[14], (TOKENS, D), 1.0, 6.0, ((0, 8),)),
    }


EPSILON = 1e-05
ROPE_BASE = 1000000.0
MASKED = -1e+30
HIGHEST_PREC = lax.Precision.HIGHEST

@jax.custom_vjp
def low(v):
    return lax.optimization_barrier(v.astype(jnp.bfloat16)).astype(jnp.float32)

@jax.custom_vjp
def low_back(v):
    return v

def low_keep(v):
    return (low(v), None)

def low_pass(kept, grad):
    return (grad,)

def back_keep(v):
    return (v, None)

def back_low(kept, grad):
    return (low(grad),)
low.defvjp(low_keep, low_pass)
low_back.defvjp(back_keep, back_low)

def norm_rows(values, gain):
    return values * lax.rsqrt(lax.optimization_barrier(jnp.mean(values * values, axis=-1, keepdims=True)) + EPSILON) * gain

def rotate(values, positions):
    half_dim = values.shape[-1] // 2
    frequency = ROPE_BASE ** (-jnp.arange(half_dim, dtype=jnp.float32) * 2.0 / values.shape[-1])
    angles = positions.astype(jnp.float32)[:, None] * frequency[None, :]
    cosine = jnp.cos(angles)[:, None, :]
    sine = jnp.sin(angles)[:, None, :]
    first_half = values[..., :half_dim]
    second_half = values[..., half_dim:]
    return jnp.concatenate([first_half * cosine - second_half * sine, second_half * cosine + first_half * sine], axis=-1)

def block_forward(rows_in, allowed, positions, params):
    norm1_gain, q_norm_gain, k_norm_gain, w_q, w_k, w_v, w_o, norm2_gain, w_gate, w_up, w_down = params
    seq_len = rows_in.shape[0]
    normed = low(norm_rows(rows_in, low(norm1_gain)))
    query = low_back(jnp.dot(normed, low(w_q), precision=HIGHEST_PREC)).reshape(seq_len, HEADS, HD)
    keyed = low_back(jnp.dot(normed, low(w_k), precision=HIGHEST_PREC)).reshape(seq_len, KV, HD)
    valued = low(low_back(jnp.dot(normed, low(w_v), precision=HIGHEST_PREC))).reshape(seq_len, KV, HD)
    query_ready = low(rotate(norm_rows(query, low(q_norm_gain)), positions)).reshape(seq_len, KV, HEADS // KV, HD)
    key_ready = low(rotate(norm_rows(keyed, low(k_norm_gain)), positions))
    raw_scores = jnp.einsum('qkgd,skd->kgqs', query_ready, key_ready, precision=HIGHEST_PREC)
    scores = low_back(raw_scores * HD ** (-0.5))
    logits = jnp.where(allowed[None, None], scores, MASKED)
    maxima = lax.optimization_barrier(jnp.max(logits, axis=-1, keepdims=True))
    expo_terms = jnp.exp(logits - maxima)
    probs_soft = expo_terms / lax.optimization_barrier(jnp.sum(expo_terms, axis=-1, keepdims=True))
    context = jnp.einsum('kgqs,skd->qkgd', low(probs_soft), valued, precision=HIGHEST_PREC)
    context = low(low_back(context.reshape(seq_len, HEADS * HD)))
    residual = rows_in + low_back(jnp.dot(context, low(w_o), precision=HIGHEST_PREC))
    normed_two = low(norm_rows(residual, low(norm2_gain)))
    gated = low_back(jnp.dot(normed_two, low(w_gate), precision=HIGHEST_PREC))
    upward = low_back(jnp.dot(normed_two, low(w_up), precision=HIGHEST_PREC))
    inner_act = low(gated * jax.nn.sigmoid(gated) * upward)
    return residual + low_back(jnp.dot(inner_act, low(w_down), precision=HIGHEST_PREC))

def reference(block_input, segments, positions, norm1_gain, q_norm_gain, k_norm_gain, w_q, w_k, w_v, w_o, norm2_gain, w_gate, w_up, w_down, cotangent):
    params = (norm1_gain, q_norm_gain, k_norm_gain, w_q, w_k, w_v, w_o, norm2_gain, w_gate, w_up, w_down)
    rows_all = block_input.astype(jnp.float32).reshape(N_DP, SEQ, D)
    cot_all = cotangent.astype(jnp.float32).reshape(N_DP, SEQ, D)
    seg_all = segments.reshape(N_DP, SEQ)
    pos_all = positions.reshape(N_DP, SEQ)
    order_ids = jnp.arange(SEQ, dtype=jnp.int32)
    causal = order_ids[:, None] >= order_ids[None, :]

    def one_sequence(totals, item):
        seq_rows, seg_rows, pos_rows, cot_rows = item
        allowed = causal & (seg_rows[:, None] == seg_rows[None, :])

        def forward(rows_in, weights):
            return block_forward(rows_in, allowed, pos_rows, weights)
        outputs, pull = jax.vjp(forward, seq_rows, params)
        grad_rows, grad_params = pull(cot_rows)
        totals = jax.tree.map(lambda total_sum, fresh_sum: total_sum + fresh_sum, totals, grad_params)
        return (totals, (outputs.astype(jnp.bfloat16), grad_rows))
    zeros_init = jax.tree.map(jnp.zeros_like, params)
    totals, (out_rows, grad_in) = lax.scan(one_sequence, zeros_init, (rows_all, seg_all, pos_all, cot_all))
    return (out_rows.reshape(TOKENS, D), grad_in.reshape(TOKENS, D), totals[0], totals[1], totals[2], totals[3], totals[4], totals[5], totals[6], totals[7], totals[8], totals[9], totals[10])
```

```python
import functools

import jax
import jax.numpy as jnp
from jax import lax
from jax.experimental import pallas as pl
from jax.experimental.pallas import tpu as pltpu
from jax.sharding import PartitionSpec as P

EPSILON = 1e-05
ROPE_BASE = 1000000.0
MASKED = -1e30


def rotation_tables(positions, head_dim):
    half_dim = head_dim // 2
    frequency = ROPE_BASE ** (-jnp.arange(half_dim, dtype=jnp.float32) * 2.0 / head_dim)
    angles = positions.astype(jnp.float32)[:, None] * frequency[None, :]
    return (jnp.cos(angles)[:, None, :], jnp.sin(angles)[:, None, :])


def rotate(values, cosine, sine):
    half_dim = values.shape[-1] // 2
    first_half = values[..., :half_dim]
    second_half = values[..., half_dim:]
    return jnp.concatenate(
        [first_half * cosine - second_half * sine, second_half * cosine + first_half * sine],
        axis=-1,
    )


def rotate_back(grads, cosine, sine):
    half_dim = grads.shape[-1] // 2
    first_half = grads[..., :half_dim]
    second_half = grads[..., half_dim:]
    return jnp.concatenate(
        [first_half * cosine + second_half * sine, second_half * cosine - first_half * sine],
        axis=-1,
    )


def norm_forward(values, gain):
    inverse = lax.rsqrt(jnp.mean(values * values, axis=-1, keepdims=True) + EPSILON)
    return (values * inverse * gain, inverse)


def norm_backward(values, inverse, gain, grad_out):
    scaled = grad_out * gain
    inner_mean = jnp.mean(scaled * values, axis=-1, keepdims=True)
    return inverse * scaled - values * (inverse * inverse * inverse) * inner_mean


def matmul(left_op, right_op):
    return jnp.dot(left_op, right_op, preferred_element_type=jnp.float32)


def matmul_tn(left_op, right_op):
    return lax.dot_general(
        left_op, right_op, (((0,), (0,)), ((), ())), preferred_element_type=jnp.float32
    )


def matmul_nt(left_op, right_op):
    return lax.dot_general(
        left_op, right_op, (((1,), (1,)), ((), ())), preferred_element_type=jnp.float32
    )


def place(parts, places, rows):
    count = len(parts)
    width = parts[0].shape[1]

    def kernel(*refs):
        ins, out, sems = refs[:count], refs[count], refs[count + 1]
        copies = []
        for index, (ref, spot) in enumerate(zip(ins, places())):
            start = pl.multiple_of(spot * rows, 16)
            copies.append(
                pltpu.make_async_copy(ref, out.at[pl.ds(start, rows), :], sems.at[index])
            )
        for copy in copies:
            copy.start()
        for copy in copies:
            copy.wait()

    size = count * rows * width * 2
    return pl.pallas_call(
        kernel,
        out_shape=jax.ShapeDtypeStruct((count * rows, width), parts[0].dtype),
        in_specs=[pl.BlockSpec(memory_space=pl.ANY)] * count,
        out_specs=pl.BlockSpec(memory_space=pl.ANY),
        scratch_shapes=[pltpu.SemaphoreType.DMA((count,))],
        cost_estimate=pl.CostEstimate(flops=0, bytes_accessed=2 * size, transcendentals=0),
    )(*parts)


class Ring:
    def __init__(self, count):
        self.count = count
        self.depth = count // 2
        self.flip = [(d, d ^ 1) for d in range(count)]

    def hop(self, values, step):
        pairs = [
            (d, ((d // 2 + step) % self.depth) * 2 + d % 2) for d in range(self.count)
        ]
        return lax.ppermute(values, "dp", pairs)

    def swap(self, values):
        return lax.ppermute(values, "dp", self.flip)

    def gather(self, shard):
        column = [shard] + [self.hop(shard, step) for step in range(1, self.depth)]
        beside = [self.swap(piece) for piece in column]

        def places():
            me = lax.axis_index("dp")
            far, near = me // 2, me % 2
            rows = [lax.rem(far + self.depth - step, self.depth) * 2 for step in range(self.depth)]
            return [row + near for row in rows] + [row + 1 - near for row in rows]

        return place(column + beside, places, shard.shape[0])

    def scatter(self, partial):
        me = lax.axis_index("dp")
        far, near = me // 2, me % 2
        rows = partial.shape[0] // self.count
        total = None
        for step in list(range(1, self.depth)) + [0]:
            there = lax.rem(far + step, self.depth) * 2
            out = lax.dynamic_slice_in_dim(partial, (there + 1 - near) * rows, rows, 0)
            came = self.swap(out).astype(jnp.float32)
            keep = lax.dynamic_slice_in_dim(partial, (there + near) * rows, rows, 0)
            both = keep.astype(jnp.float32) + came
            if step:
                arrived = self.hop(both.astype(jnp.bfloat16), step).astype(jnp.float32)
            else:
                arrived = both
            total = arrived if total is None else total + arrived
        return total


def tensor_sum(partial, count):
    if count != 4:
        return lax.psum(partial.astype(jnp.bfloat16), "tensor")
    me = lax.axis_index("tensor")
    core = lax.rem(me, 2)
    half = partial.shape[0] // 2
    mate = [(t, t ^ 1) for t in range(count)]
    across = [(t, t ^ 2) for t in range(count)]
    out = lax.dynamic_slice_in_dim(partial, (1 - core) * half, half, 0).astype(jnp.bfloat16)
    keep = lax.dynamic_slice_in_dim(partial, core * half, half, 0)
    chip = (keep + lax.ppermute(out, "tensor", mate).astype(jnp.float32)).astype(jnp.bfloat16)
    other = lax.ppermute(chip, "tensor", across)
    mine = (chip.astype(jnp.float32) + other.astype(jnp.float32)).astype(jnp.bfloat16)
    theirs = lax.ppermute(mine, "tensor", mate)
    first = jnp.where(core == 0, mine, theirs)
    second = jnp.where(core == 0, theirs, mine)
    return jnp.concatenate([first, second], axis=0)


def block_logits(query_part, key_part, segments, first_row, last_row, scale):
    raw_scores = (
        jnp.einsum("qkgd,skd->kgqs", query_part, key_part, preferred_element_type=jnp.float32)
        * scale
    )
    row_ids = jnp.arange(first_row, last_row)
    col_ids = jnp.arange(last_row)
    allowed = (segments[first_row:last_row][:, None] == segments[:last_row][None, :]) & (
        row_ids[:, None] >= col_ids[None, :]
    )
    return jnp.where(allowed[None, None], raw_scores, MASKED)


def attention_forward(query_b, key_b, value_b, segments, scale):
    seq_len = query_b.shape[0]
    block_rows = min(512, seq_len)
    pieces = []
    logsums = []
    for block_index in range(seq_len // block_rows):
        first_row = block_index * block_rows
        last_row = first_row + block_rows
        logits = block_logits(
            query_b[first_row:last_row], key_b[:last_row], segments, first_row, last_row, scale
        )
        maxima = jnp.max(logits, axis=-1, keepdims=True)
        expo_terms = jnp.exp(logits - maxima)
        totals = jnp.sum(expo_terms, axis=-1, keepdims=True)
        probs_low = (expo_terms / totals).astype(jnp.bfloat16)
        pieces.append(
            jnp.einsum(
                "kgqs,skd->qkgd", probs_low, value_b[:last_row], preferred_element_type=jnp.float32
            )
        )
        logsums.append(maxima + jnp.log(totals))
    return (jnp.concatenate(pieces, axis=0), logsums)


def attention_backward(query_b, key_b, value_b, grad_context, logsums, segments, scale):
    seq_len = query_b.shape[0]
    block_rows = min(512, seq_len)
    grad_query = []
    grad_key = jnp.zeros(key_b.shape, jnp.float32)
    grad_value = jnp.zeros(value_b.shape, jnp.float32)
    for block_index in range(seq_len // block_rows):
        first_row = block_index * block_rows
        last_row = first_row + block_rows
        query_part = query_b[first_row:last_row]
        grad_part = grad_context[first_row:last_row]
        logits = block_logits(query_part, key_b[:last_row], segments, first_row, last_row, scale)
        probs_soft = jnp.exp(logits - logsums[block_index])
        grad_probs = jnp.einsum(
            "qkgd,skd->kgqs", grad_part, value_b[:last_row], preferred_element_type=jnp.float32
        )
        row_inner = jnp.sum(probs_soft * grad_probs, axis=-1, keepdims=True)
        grad_scores = (probs_soft * (grad_probs - row_inner)).astype(jnp.bfloat16)
        grad_query.append(
            jnp.einsum(
                "kgqs,skd->qkgd", grad_scores, key_b[:last_row], preferred_element_type=jnp.float32
            )
            * scale
        )
        grad_key = grad_key.at[:last_row].add(
            jnp.einsum(
                "kgqs,qkgd->skd", grad_scores, query_part, preferred_element_type=jnp.float32
            )
            * scale
        )
        grad_value = grad_value.at[:last_row].add(
            jnp.einsum(
                "kgqs,qkgd->skd",
                probs_soft.astype(jnp.bfloat16),
                grad_part,
                preferred_element_type=jnp.float32,
            )
        )
    return (jnp.concatenate(grad_query, axis=0), grad_key, grad_value)


def shards(
    block_input,
    segments,
    positions,
    norm1_gain,
    q_norm_gain,
    k_norm_gain,
    w_q,
    w_k,
    w_v,
    w_o,
    norm2_gain,
    w_gate,
    w_up,
    w_down,
    cotangent,
    *,
    n_dp,
    n_tensor,
):
    ring = Ring(n_dp)
    bf16 = jnp.bfloat16
    rows = w_q.shape[0]
    q_cols, kv_cols, ff_cols = w_q.shape[1], w_k.shape[1], w_gate.shape[1]
    small_gain = q_norm_gain.shape[0]

    def column(gain):
        return jnp.pad(gain.astype(bf16), (0, rows - gain.shape[0]))[:, None]

    gains = jnp.concatenate(
        [column(norm1_gain), column(norm2_gain), column(q_norm_gain), column(k_norm_gain)], axis=1
    )
    gains = jnp.pad(gains, ((0, 0), (0, 124)))
    pack_attn = jnp.concatenate(
        [w_q.astype(bf16), w_k.astype(bf16), w_v.astype(bf16), w_o.T.astype(bf16), gains], axis=1
    )
    pack_gates = jnp.concatenate([w_gate.astype(bf16), w_up.astype(bf16)], axis=1)
    pack_down = w_down.T.astype(bf16)
    full_attn = ring.gather(pack_attn)
    full_gates = ring.gather(pack_gates)
    full_down = ring.gather(pack_down)

    qkv_cols = q_cols + 2 * kv_cols
    weight_qkv = full_attn[:, :qkv_cols]
    weight_ot = full_attn[:, qkv_cols : qkv_cols + q_cols]
    gain_block = full_attn[:, qkv_cols + q_cols : qkv_cols + q_cols + 4].astype(jnp.float32).T
    gain_one, gain_two = gain_block[0], gain_block[1]
    gain_query = gain_block[2].reshape(n_dp, rows)[:, :small_gain].reshape(-1)
    gain_key = gain_block[3].reshape(n_dp, rows)[:, :small_gain].reshape(-1)

    seq_len = block_input.shape[0]
    head_dim = gain_query.shape[0]
    local_heads = q_cols // head_dim
    local_kv = kv_cols // head_dim
    group_size = local_heads // local_kv
    scale = head_dim ** (-0.5)
    cosine, sine = rotation_tables(positions, head_dim)
    rows_in = block_input.astype(jnp.float32)
    normed, inverse_one = norm_forward(rows_in, gain_one)
    normed_b = normed.astype(bf16)
    qkv = matmul(normed_b, weight_qkv)
    query = qkv[:, :q_cols].reshape(seq_len, local_heads, head_dim)
    keyed = qkv[:, q_cols : q_cols + kv_cols].reshape(seq_len, local_kv, head_dim)
    value_b = qkv[:, q_cols + kv_cols :].astype(bf16).reshape(seq_len, local_kv, head_dim)
    query_normed, query_inverse = norm_forward(query, gain_query)
    key_normed, key_inverse = norm_forward(keyed, gain_key)
    query_b = (
        rotate(query_normed, cosine, sine)
        .astype(bf16)
        .reshape(seq_len, local_kv, group_size, head_dim)
    )
    key_b = rotate(key_normed, cosine, sine).astype(bf16)
    context, logsums = attention_forward(query_b, key_b, value_b, segments, scale)
    context_b = context.reshape(seq_len, local_heads * head_dim).astype(bf16)
    attn_total = tensor_sum(matmul_nt(context_b, weight_ot), n_tensor)
    residual = rows_in + attn_total.astype(jnp.float32)
    normed_two, inverse_two = norm_forward(residual, gain_two)
    normed_two_b = normed_two.astype(bf16)
    weight_gate = full_gates[:, :ff_cols]
    weight_up = full_gates[:, ff_cols:]
    gated = matmul(normed_two_b, weight_gate)
    upward = matmul(normed_two_b, weight_up)
    sigmoid_gate = jax.nn.sigmoid(gated)
    inner_b = (gated * sigmoid_gate * upward).astype(bf16)
    grad_down = ring.scatter(matmul_tn(cotangent, inner_b).astype(bf16)).T
    mlp_total = tensor_sum(matmul_nt(inner_b, full_down), n_tensor)
    output_rows = (residual + mlp_total.astype(jnp.float32)).astype(bf16)
    grad_out = cotangent.astype(jnp.float32)
    grad_inner = matmul(cotangent, full_down)
    grad_up_b = (grad_inner * gated * sigmoid_gate).astype(bf16)
    grad_gate_b = (
        grad_inner * upward * sigmoid_gate * (1.0 + gated * (1.0 - sigmoid_gate))
    ).astype(bf16)
    grad_gate_w = ring.scatter(matmul_tn(normed_two_b, grad_gate_b).astype(bf16))
    grad_up_w = ring.scatter(matmul_tn(normed_two_b, grad_up_b).astype(bf16))
    grad_normed_two = tensor_sum(
        matmul_nt(grad_gate_b, weight_gate) + matmul_nt(grad_up_b, weight_up), n_tensor
    ).astype(jnp.float32)
    grad_gain_two = jnp.sum(grad_normed_two * residual * inverse_two, axis=0)
    grad_residual = grad_out + norm_backward(residual, inverse_two, gain_two, grad_normed_two)
    grad_res_b = grad_residual.astype(bf16)
    grad_out_w = ring.scatter(matmul_tn(grad_res_b, context_b).astype(bf16)).T
    grad_context = (
        matmul(grad_res_b, weight_ot).astype(bf16).reshape(seq_len, local_kv, group_size, head_dim)
    )
    grad_query, grad_key, grad_value = attention_backward(
        query_b, key_b, value_b, grad_context, logsums, segments, scale
    )
    grad_query = rotate_back(grad_query.reshape(seq_len, local_heads, head_dim), cosine, sine)
    grad_key = rotate_back(grad_key, cosine, sine)
    grad_gain_q = jnp.sum(grad_query * query * query_inverse, axis=(0, 1))
    grad_gain_k = jnp.sum(grad_key * keyed * key_inverse, axis=(0, 1))
    grad_q_low = (
        norm_backward(query, query_inverse, gain_query, grad_query)
        .astype(bf16)
        .reshape(seq_len, local_heads * head_dim)
    )
    grad_k_low = (
        norm_backward(keyed, key_inverse, gain_key, grad_key)
        .astype(bf16)
        .reshape(seq_len, local_kv * head_dim)
    )
    grad_v_low = grad_value.astype(bf16).reshape(seq_len, local_kv * head_dim)
    grad_low = jnp.concatenate([grad_q_low, grad_k_low, grad_v_low], axis=1)
    grad_qkv = ring.scatter(matmul_tn(normed_b, grad_low).astype(bf16))
    grad_normed = tensor_sum(matmul_nt(grad_low, weight_qkv), n_tensor).astype(jnp.float32)
    grad_gain_one = jnp.sum(grad_normed * rows_in * inverse_one, axis=0)
    grad_input = grad_residual + norm_backward(rows_in, inverse_one, gain_one, grad_normed)
    share = 1.0 / n_tensor
    small = lax.psum(
        jnp.concatenate([grad_gain_one * share, grad_gain_two * share, grad_gain_q, grad_gain_k]),
        ("dp", "tensor"),
    )
    me = lax.axis_index("dp")
    width = gain_one.shape[0]

    def own(start, size):
        return lax.dynamic_slice_in_dim(small, start + me * size, size, 0)

    return (
        output_rows,
        grad_input,
        own(0, rows),
        own(2 * width, small_gain),
        own(2 * width + head_dim, small_gain),
        grad_qkv[:, :q_cols],
        grad_qkv[:, q_cols : q_cols + kv_cols],
        grad_qkv[:, q_cols + kv_cols :],
        grad_out_w,
        own(width, rows),
        grad_gate_w,
        grad_up_w,
        grad_down,
    )


def solution(mesh):
    placed = (
        P("dp", None),
        P("dp"),
        P("dp"),
        P("dp"),
        P("dp"),
        P("dp"),
        P("dp", "tensor"),
        P("dp", "tensor"),
        P("dp", "tensor"),
        P("tensor", "dp"),
        P("dp"),
        P("dp", "tensor"),
        P("dp", "tensor"),
        P("tensor", "dp"),
        P("dp", None),
    )
    return jax.shard_map(
        functools.partial(shards, n_dp=mesh.shape["dp"], n_tensor=mesh.shape["tensor"]),
        mesh=mesh,
        in_specs=placed,
        out_specs=(
            P("dp", None),
            P("dp", None),
            P("dp"),
            P("dp"),
            P("dp"),
            P("dp", "tensor"),
            P("dp", "tensor"),
            P("dp", "tensor"),
            P("tensor", "dp"),
            P("dp"),
            P("dp", "tensor"),
            P("dp", "tensor"),
            P("tensor", "dp"),
        ),
        check_vma=False,
    )
```

```python
import functools

import jax
import jax.numpy as jnp
from jax import lax
from jax.experimental import pallas as pl
from jax.experimental.pallas import tpu as pltpu
from jax.sharding import PartitionSpec as P

EPSILON = 1e-05
ROPE_BASE = 1000000.0
MASKED = -1e30


MESH = pl.DeviceIdType.MESH
NEAR = 2
HALF = 64
LANES = 128
HIGHEST = lax.Precision.HIGHEST
BF16 = jnp.bfloat16
F32 = jnp.float32


def whole_block():
    return pl.BlockSpec(memory_space=pltpu.VMEM)


def in_place():
    return pl.BlockSpec(memory_space=pl.ANY)


def remote(src, dst, send, recv, dp, tensor):
    return pltpu.make_async_remote_copy(
        src_ref=src,
        dst_ref=dst,
        send_sem=send,
        recv_sem=recv,
        device_id=(dp, tensor),
        device_id_type=MESH,
    )


def dot_nn(left, right):
    return jnp.dot(left, right, preferred_element_type=F32)


def dot_nt(left, right):
    return lax.dot_general(left, right, (((1,), (1,)), ((), ())), preferred_element_type=F32)


def dot_tn(left, right):
    return lax.dot_general(left, right, (((0,), (0,)), ((), ())), preferred_element_type=F32)


class Place:
    def __init__(self, count):
        self.count = count
        self.depth = count // NEAR
        self.me = lax.axis_index("dp")
        self.tensor = lax.axis_index("tensor")
        self.far = self.me // NEAR
        self.near = lax.rem(self.me, NEAR)
        self.core = lax.rem(self.tensor, 2)
        self.mate = self.tensor + 1 - 2 * self.core
        self.across = lax.rem(self.tensor + 2, 4)
        self.beside = self.me + 1 - 2 * self.near

    def ahead(self, step):
        return lax.rem(self.far + step, self.depth)

    def behind(self, step):
        return lax.rem(self.far + self.depth - step, self.depth)

    def greet(self, everyone, tensor):
        barrier = pltpu.get_barrier_semaphore()
        peers = []
        if everyone:
            peers += [(lax.rem(self.me + d, self.count), self.tensor) for d in range(1, self.count)]
        else:
            peers += [
                (self.ahead(step) * NEAR + self.near, self.tensor) for step in range(1, self.depth)
            ]
            peers.append((self.beside, self.tensor))
        if tensor:
            peers += [(self.me, self.mate), (self.me, self.across)]
        for peer in peers:
            pl.semaphore_signal(barrier, 1, device_id=peer, device_id_type=MESH)
        pl.semaphore_wait(barrier, len(peers))


class Gather:
    def __init__(self, place, shard, full, sems):
        self.place, self.shard, self.full = place, shard, full
        self.rows = shard.shape[0]
        late = self.late_rows(self.rows)
        self.cuts = [(0, self.rows - late)] + ([(self.rows - late, late)] if late else [])
        self.zsend, self.zrecv, self.ysend, self.yrecv, self.own = sems
        self.sent = []

    @staticmethod
    def late_rows(rows):
        return rows // 6 // 16 * 16

    @staticmethod
    def sems(count):
        depth = count // NEAR
        dma = pltpu.SemaphoreType.DMA
        return [dma((2, depth - 1, 3)), dma((2, depth - 1, 3)), dma((2 * depth - 1, 2)), dma((2 * depth - 1, 2)), dma]

    def spot(self, block, cut):
        start, size = self.cuts[cut]
        return self.full.at[pl.ds(pl.multiple_of(block * self.rows + start, 16), size), :]

    def mine(self, cut):
        start, size = self.cuts[cut]
        return self.shard.at[pl.ds(start, size), :]

    def block(self, way, step, other):
        far = self.place.far - step if way == 0 else self.place.far + step
        return far * NEAR + (1 - self.place.near if other else self.place.near)

    def valid(self, way, step):
        return self.place.far >= step if way == 0 else self.place.far + step < self.place.depth

    def emit(self, copy, when):
        if when is None:
            copy.start()
        else:
            pl.when(when)(copy.start)
        self.sent.append((copy, when))

    def along(self, way, step, cut, other, valid=None):
        place = self.place
        if step >= place.depth - 1:
            return
        more = place.far < place.depth - 1 if way == 0 else place.far > 0
        spot = self.spot(self.block(way, step, other), cut)
        goal = place.me + (NEAR if way == 0 else -NEAR)
        self.emit(
            remote(
                self.mine(cut) if step == 0 and not other else spot, spot,
                self.zsend.at[way, step, cut + other], self.zrecv.at[way, step, cut + other], goal, place.tensor,
            ),
            more if valid is None else more & valid,
        )

    def over(self, way, step, cut, valid=None):
        place = self.place
        spot = self.spot(self.block(way, step, 0), cut)
        slot = step if way == 0 else step + place.depth - 1
        self.emit(
            remote(
                self.mine(cut) if step == 0 else spot, spot,
                self.ysend.at[slot, cut], self.yrecv.at[slot, cut], place.beside, place.tensor,
            ),
            valid,
        )

    def came_over(self, way, step, cut):
        place = self.place
        spot = self.spot(self.block(way, step, 1), cut)
        slot = step if way == 0 else step + place.depth - 1
        copy = remote(
            spot, spot, self.ysend.at[slot, cut], self.yrecv.at[slot, cut], place.beside, place.tensor
        )
        if step == 0:
            copy.wait_recv()
        else:
            pl.when(self.valid(way, step))(copy.wait_recv)

    def start(self):
        place = self.place
        self.local = pltpu.make_async_copy(
            self.shard, self.full.at[pl.ds(pl.multiple_of(place.me * self.rows, 16), self.rows), :], self.own
        )
        self.local.start()
        for cut in reversed(range(len(self.cuts))):
            self.over(0, 0, cut)
        for cut in range(len(self.cuts)):
            for way in range(2):
                self.along(way, 0, cut, 0)

    def steps(self):
        place = self.place
        if len(self.cuts) > 1:
            self.came_over(0, 0, 1)
            for way in range(2):
                self.along(way, 0, 1, 1)
            yield
        for step in range(1, place.depth):
            for cut in range(len(self.cuts)):
                for other in range(cut + 1):
                    for way in range(2):
                        valid = self.valid(way, step)
                        spot = self.spot(self.block(way, step, other), cut)
                        copy = remote(
                            spot, spot, self.zsend.at[way, step - 1, cut + other],
                            self.zrecv.at[way, step - 1, cut + other], place.me, place.tensor,
                        )
                        pl.when(valid)(copy.wait_recv)
                        self.along(way, step, cut, other, valid)
                        if cut == 0:
                            self.over(way, step, cut, valid)
                        yield

    def finish(self):
        self.came_over(0, 0, 0)
        for step in range(1, self.place.depth):
            for way in range(2):
                self.came_over(way, step, 0)
        self.local.wait()

    def settle(self):
        for copy, when in self.sent:
            if when is None:
                copy.wait_send()
            else:
                pl.when(when)(copy.wait_send)


class TensorSum:
    def __init__(self, place, part, total, tiles, scratch):
        self.place, self.part, self.total, self.tiles = place, part, total, tiles
        self.tile = part.shape[0] // tiles
        self.half = self.tile // 2
        self.near, self.chip, self.far, self.sems = scratch
        self.sent = []

    @staticmethod
    def scratch(rows, width, tiles, kind):
        half = (rows // 2, width)
        return [
            pltpu.VMEM(half, kind), pltpu.VMEM(half, BF16), pltpu.VMEM(half, BF16), pltpu.SemaphoreType.DMA((6, tiles))
        ]

    def half_rows(self, index, which):
        return pl.ds(pl.multiple_of(index * self.tile + which * self.half, 16), self.half)

    def slot(self, index):
        return pl.ds(index * self.half, self.half)

    def send_core(self, index):
        place = self.place
        copy = remote(
            self.part.at[self.half_rows(index, 1 - place.core), :], self.near.at[self.slot(index), :],
            self.sems.at[0, index], self.sems.at[1, index], place.me, place.mate,
        )
        copy.start()
        self.sent.append(copy)

    def send_across(self, index):
        place = self.place
        spot = self.near.at[self.slot(index), :]
        remote(spot, spot, self.sems.at[0, index], self.sems.at[1, index], place.me, place.mate).wait_recv()
        mine = self.part[self.half_rows(index, place.core), :].astype(F32)
        self.chip[self.slot(index), :] = (mine + self.near[self.slot(index), :].astype(F32)).astype(BF16)
        copy = remote(
            self.chip.at[self.slot(index), :], self.far.at[self.slot(index), :],
            self.sems.at[2, index], self.sems.at[3, index], place.me, place.across,
        )
        copy.start()
        self.sent.append(copy)

    def send_back(self, index):
        place = self.place
        spot = self.far.at[self.slot(index), :]
        remote(spot, spot, self.sems.at[2, index], self.sems.at[3, index], place.me, place.across).wait_recv()
        both = self.chip[self.slot(index), :].astype(F32) + self.far[self.slot(index), :].astype(F32)
        rows = self.half_rows(index, place.core)
        self.total[rows, :] = both.astype(self.total.dtype)
        copy = remote(
            self.total.at[rows, :], self.total.at[rows, :],
            self.sems.at[4, index], self.sems.at[5, index], place.me, place.mate,
        )
        copy.start()
        self.sent.append(copy)

    def finish(self, index):
        place = self.place
        spot = self.total.at[self.half_rows(index, 1 - place.core), :]
        remote(spot, spot, self.sems.at[4, index], self.sems.at[5, index], place.me, place.mate).wait_recv()

    def settle(self):
        for copy in self.sent:
            copy.wait_send()


def lane_ids(width=LANES):
    return lax.broadcasted_iota(jnp.int32, (1, width), 1)


def head_mean(values):
    row = lax.broadcasted_iota(jnp.int32, (LANES, LANES), 0)
    col = lax.broadcasted_iota(jnp.int32, (LANES, LANES), 1)
    groups = jnp.where(row // HALF == col // HALF, 1.0 / HALF, 0.0).astype(F32)
    return jnp.dot(values, groups, precision=HIGHEST, preferred_element_type=F32)


def turn(values, cosine, sine):
    ahead = pltpu.roll(values, LANES - HALF // 2, 1)
    back = pltpu.roll(values, HALF // 2, 1)
    first = lax.rem(lane_ids(), HALF) < HALF // 2
    return values * cosine + jnp.where(first, ahead, back) * sine


def bias_block(seg_col, seg_row, bias, first, tile):
    last = first + tile
    rows = lax.broadcasted_iota(jnp.int32, (tile, last), 0) + first
    cols = lax.broadcasted_iota(jnp.int32, (tile, last), 1)
    allowed = (seg_col[pl.ds(first, tile), :] == seg_row[:, pl.ds(0, last)]) & (rows >= cols)
    bias[:, pl.ds(0, last)] = jnp.where(allowed, 0.0, MASKED)


def forward_kernel(count, *refs):
    (
        x_ref, seg_col, seg_row, cos_ref, sin_ref, gain_ref, pack_attn, pack_gates,
        full_attn, full_gates, n1_ref, qk_ref, qm_ref, kb_ref, vb_ref, lse_ref, ctx_ref, h_ref, n2_ref,
        gains_out,
        w0, bias, gain_slots, part, total, tmp_near, tmp_chip, tmp_far, sum_sems, gain_send, gain_recv, out_sem,
        *gather_sems,
    ) = refs
    place = Place(count)
    seq, width = x_ref.shape
    q_cols = ctx_ref.shape[1]
    kv_cols = kb_ref.shape[1]
    pairs = q_cols // LANES
    group = (q_cols // HALF) // (kv_cols // HALF)
    tile = seq // 4
    place.greet(True, True)
    first = Gather(place, pack_attn, w0, gather_sems[:5])
    second = Gather(place, pack_gates, full_gates, gather_sems[5:])
    gain_copies = []
    for step in range(1, count):
        copy = remote(
            gain_ref, gain_slots.at[step], gain_send.at[step], gain_recv.at[step],
            lax.rem(place.me + step, count), place.tensor,
        )
        copy.start()
        gain_copies.append(copy)
    first.start()
    for qb in range(4):
        bias_block(seg_col, seg_row, bias.at[qb], qb * tile, tile)
    gains = gain_ref[...]
    for copy in gain_copies:
        copy.wait_recv()
    for step in range(1, count):
        gains = gains + gain_slots[step]
    gains_out[...] = gains
    for _ in first.steps():
        pass
    second.start()
    moves = second.steps()
    g1 = gains_out[pl.ds(0, 1), :]
    g2 = gains_out[pl.ds(1, 1), :]

    def norm_one(index, carry):
        rows = pl.ds(pl.multiple_of(index * LANES, LANES), LANES)
        x = x_ref[rows, :].astype(F32)
        inverse = lax.rsqrt(jnp.mean(x * x, axis=1, keepdims=True) + EPSILON)
        n1_ref[rows, :] = (x * inverse * g1).astype(BF16)
        return carry

    lax.fori_loop(0, seq // LANES, norm_one, 0)
    first.finish()
    save = pltpu.make_async_copy(w0, full_attn, out_sem)
    save.start()
    gq = gains_out[pl.ds(2, 1), pl.ds(0, LANES)]
    gk = gains_out[pl.ds(3, 1), pl.ds(0, LANES)]
    lanes = lane_ids()

    def project(index, carry):
        rows = pl.ds(pl.multiple_of(index * tile, tile), tile)
        qkv = dot_nn(n1_ref[rows, :], w0[:, pl.ds(0, q_cols + 2 * kv_cols)])
        qk_ref[rows, :] = qkv[:, : q_cols + kv_cols]
        vb_ref[rows, :] = qkv[:, q_cols + kv_cols :].astype(BF16)
        cosine, sine = cos_ref[rows, :], sin_ref[rows, :]
        for pair in range(pairs + 1):
            raw = qkv[:, pair * LANES : (pair + 1) * LANES]
            inverse = lax.rsqrt(head_mean(raw * raw) + EPSILON)
            turned = turn(raw * inverse * (gk if pair == pairs else gq), cosine, sine)
            if pair == pairs:
                kb_ref[rows, :] = turned.astype(BF16)
                continue
            swapped = pltpu.roll(turned, HALF, 1)
            for side in range(2):
                head = 2 * pair + side
                kv = head // group
                keep = (turned if side == kv else swapped).astype(BF16) * 0.125
                qm_ref[head, rows, :] = jnp.where(lanes // HALF == kv, keep, jnp.zeros_like(keep))
        return carry

    lax.fori_loop(0, 4, project, 0)
    next(moves, None)

    for qb in range(4):
        last = (qb + 1) * tile
        rows = pl.ds(qb * tile, tile)

        def attend(pair, carry, last=last, rows=rows, qb=qb):
            halves, sums = [], []
            for side in range(2):
                head = 2 * pair + side
                kv = head // group
                logits = dot_nt(qm_ref[head, rows, :], kb_ref[pl.ds(0, last), :]) + bias[qb, :, pl.ds(0, last)]
                top = jnp.max(logits, axis=1, keepdims=True)
                expo = jnp.exp(logits - top)
                total = jnp.sum(expo, axis=1, keepdims=True)
                probs = (expo * (1.0 / total)).astype(BF16)
                got = dot_nn(probs, vb_ref[pl.ds(0, last), :])
                halves.append(jnp.where(kv == side, got, pltpu.roll(got, HALF, 1)))
                sums.append(top + jnp.log(total))
            ctx_ref[rows, pl.ds(pl.multiple_of(pair * LANES, LANES), LANES)] = jnp.where(
                lanes < HALF, halves[0], halves[1]
            ).astype(BF16)
            carry = jnp.where(lanes == 2 * pair, sums[0], carry)
            return jnp.where(lanes == 2 * pair + 1, sums[1], carry)

        lse_ref[rows, :] = lax.fori_loop(0, pairs, attend, jnp.zeros((tile, LANES), F32))
        next(moves, None)
        next(moves, None)

    summed = TensorSum(place, part, total, 4, (tmp_near, tmp_chip, tmp_far, sum_sems))
    for index in range(4):
        rows = pl.ds(index * tile, tile)
        part[rows, :] = dot_nt(
            ctx_ref[rows, :], w0[:, pl.ds(q_cols + 2 * kv_cols, q_cols)]
        )
        summed.send_core(index)
    for index in range(4):
        summed.send_across(index)
    next(moves, None)
    for index in range(4):
        summed.send_back(index)
        next(moves, None)
    for index in range(4):
        summed.finish(index)

        def norm_two(sub, carry, index=index):
            rows = pl.ds(pl.multiple_of(index * tile + sub * LANES, LANES), LANES)
            h = x_ref[rows, :].astype(F32) + total[rows, :]
            h_ref[rows, :] = h
            inverse = lax.rsqrt(jnp.mean(h * h, axis=1, keepdims=True) + EPSILON)
            n2_ref[rows, :] = (h * inverse * g2).astype(BF16)
            return carry

        lax.fori_loop(0, tile // LANES, norm_two, 0)
        next(moves, None)
    for _ in moves:
        pass
    second.finish()
    save.wait()
    for copy in gain_copies:
        copy.wait_send()
    first.settle()
    second.settle()
    summed.settle()


def forward_call(count, x, seg_col, seg_row, cosine, sine, gains, pack_attn, pack_gates):
    seq, width = x.shape
    rows = pack_attn.shape[0]
    shape = jax.ShapeDtypeStruct
    q_cols, kv_cols = 384, LANES
    outs = [
        shape((count * rows, pack_attn.shape[1]), BF16),
        shape((count * rows, pack_gates.shape[1]), BF16),
        shape((seq, width), BF16),
        shape((seq, q_cols + kv_cols), F32),
        shape((q_cols // HALF, seq, LANES), BF16),
        shape((seq, LANES), BF16),
        shape((seq, LANES), BF16),
        shape((seq, LANES), F32),
        shape((seq, q_cols), BF16),
        shape((seq, width), F32),
        shape((seq, width), BF16),
        shape(gains.shape, F32),
    ]
    dma = pltpu.SemaphoreType.DMA
    return pl.pallas_call(
        functools.partial(forward_kernel, count),
        out_shape=outs,
        in_specs=[whole_block()] * 6 + [in_place()] * 2,
        out_specs=[in_place()] * 2 + [whole_block()] * 10,
        scratch_shapes=[
            pltpu.VMEM((count * rows, pack_attn.shape[1]), BF16),
            pltpu.VMEM((4, seq // 4, seq), F32),
            pltpu.VMEM((count,) + gains.shape, F32),
            pltpu.VMEM((seq, width), F32),
            pltpu.VMEM((seq, width), F32),
            *TensorSum.scratch(seq, width, 4, F32),
            dma((count,)),
            dma((count,)),
            dma,
            *Gather.sems(count),
            *Gather.sems(count),
        ],
        compiler_params=pltpu.CompilerParams(
            collective_id=1, has_side_effects=True, vmem_limit_bytes=60 << 20
        ),
    )(x, seg_col, seg_row, cosine, sine, gains, pack_attn, pack_gates)


class Scatter:
    def __init__(self, place, partial, result, scratch):
        self.place, self.partial, self.result = place, partial, result
        self.rows = partial.shape[0] // place.count
        self.late = Gather.late_rows(self.rows)
        self.early = self.rows - self.late
        self.over_in, self.far_in, self.far_late, self.late_in = scratch[:4]
        self.zsend, self.zrecv, self.ysend, self.yrecv, self.lsend, self.lrecv = scratch[4:]
        self.sent = []

    @staticmethod
    def scratch(count, rows, width):
        depth = count // NEAR
        late = Gather.late_rows(rows)
        early = rows - late
        dma = pltpu.SemaphoreType.DMA
        return [
            pltpu.VMEM((depth, early, width), BF16),
            pltpu.VMEM((depth + 1, early, width), BF16),
            pltpu.VMEM((2, depth + 1, max(late, 16), width), BF16),
            pltpu.VMEM((max(late, 16), width), BF16),
            dma((2, depth - 1, 3)),
            dma((2, depth - 1, 3)),
            dma((2 * depth - 1,)),
            dma((2 * depth - 1,)),
            dma,
            dma,
        ]

    def spot(self, far, other, late):
        near = 1 - self.place.near if other else self.place.near
        start = (far * NEAR + near) * self.rows + (self.early if late else 0)
        return pl.ds(pl.multiple_of(start, 16), self.late if late else self.early)

    def valid(self, way, step):
        return self.place.far + step < self.place.depth if way == 0 else self.place.far >= step

    def fed(self, way):
        return self.place.far > 0 if way == 0 else self.place.far < self.place.depth - 1

    def goal(self, way, step):
        return self.place.far + step if way == 0 else self.place.far - step

    def slot(self, way, step):
        return step if way == 0 else step + self.place.depth - 1

    def emit(self, copy, when=None):
        if when is None:
            copy.start()
        else:
            pl.when(when)(copy.start)
        self.sent.append((copy, when))

    def over(self, far, slot):
        place = self.place
        return remote(
            self.partial.at[self.spot(far, True, False), :], self.over_in.at[far],
            self.ysend.at[slot], self.yrecv.at[slot], place.beside, place.tensor,
        )

    def start(self):
        place = self.place
        for step in reversed(range(1, place.depth)):
            for way in range(2):
                self.emit(self.over(self.goal(way, step), self.slot(way, step)), self.valid(way, step))
        self.emit(self.over(place.far, 0))

    def add(self, spot, sources):
        size = sources[0].shape[0]
        part = 32 if size % 32 == 0 else 16

        def body(index, carry):
            start = pl.multiple_of(index * part, 16)
            rows = pl.ds(pl.multiple_of(spot.start + start, 16), part)
            total = self.partial[rows, :].astype(F32)
            for source in sources:
                total = total + source[pl.ds(start, part), :].astype(F32)
            self.partial[rows, :] = total.astype(BF16)
            return carry

        lax.fori_loop(0, size // part, body, 0)

    def incoming(self, way, step, item):
        place = self.place
        index = place.depth if way == 1 and step == 0 else self.goal(way, step)
        return self.far_in.at[index] if item == 0 else self.far_late.at[item - 1, index]

    def wait_far(self, way, step, item):
        place = self.place
        into = self.incoming(way, step, item)
        remote(
            into, into, self.zsend.at[way, step, item], self.zrecv.at[way, step, item], place.me, place.tensor
        ).wait_recv()
        return into

    def pass_on(self, way, step, item):
        place = self.place
        far = self.goal(way, step)
        spot = self.spot(far, item == 2, item > 0)
        if item == 0:
            copy = self.over(far, self.slot(way, step))
            pl.when(self.valid(way, step))(copy.wait_recv)
        base = [self.over_in.at[far]] if item == 0 else []
        valid = self.valid(way, step)
        if step < place.depth - 1:

            @pl.when(valid & self.fed(way))
            def _():
                self.add(spot, base + [self.wait_far(way, step, item)])

        if base:

            @pl.when(valid & jnp.logical_not(self.fed(way)))
            def _():
                self.add(spot, base)

        index = place.depth if way == 1 and step == 1 else far
        into = self.far_in.at[index] if item == 0 else self.far_late.at[item - 1, index]
        self.emit(
            remote(
                self.partial.at[spot, :], into,
                self.zsend.at[way, step - 1, item], self.zrecv.at[way, step - 1, item],
                place.me + (NEAR if way == 0 else -NEAR), place.tensor,
            ),
            valid,
        )

    def steps(self):
        place = self.place
        for step in reversed(range(1, place.depth)):
            for item in ((1, 2) if self.late else ()):
                for way in range(2):
                    self.pass_on(way, step, item)
                yield
            for way in range(2):
                self.pass_on(way, step, 0)
                yield
        far = place.far
        if self.late:
            for item in (2, 1):
                spot = self.spot(far, item == 2, True)
                for way in range(2):

                    @pl.when(self.fed(way))
                    def _(way=way, item=item, spot=spot):
                        self.add(spot, [self.wait_far(way, 0, item)])

                if item == 2:
                    copy = remote(
                        self.partial.at[spot, :], self.late_in, self.lsend, self.lrecv, place.beside, place.tensor
                    )
                    self.emit(copy)
            yield
        self.over(far, 0).wait_recv()
        spot = self.spot(far, False, False)
        self.add(spot, [self.over_in.at[far]])
        yield
        for way in range(2):

            @pl.when(self.fed(way))
            def _(way=way, spot=spot):
                self.add(spot, [self.wait_far(way, 0, 0)])

        own = self.spot(far, False, False)
        self.result[pl.ds(0, self.early), :] = self.partial[own, :].astype(F32)
        yield
        if self.late:
            copy.wait_recv()
            own = self.spot(far, False, True)
            self.result[pl.ds(self.early, self.late), :] = (
                self.partial[own, :].astype(F32) + self.late_in[...].astype(F32)
            )
        yield

    def settle(self):
        for copy, when in self.sent:
            if when is None:
                copy.wait_send()
            else:
                pl.when(when)(copy.wait_send)


def drain(*moves):
    for one in moves:
        for _ in one:
            pass


def ahead(moves, count=1):
    for _ in range(count):
        next(moves, None)


def blocks(total, size, body):
    def step(index, carry):
        body(pl.multiple_of(index * size, size))
        return carry

    lax.fori_loop(0, total // size, step, 0)


def mlp_kernel(count, *refs):
    (
        n2_ref, cot_ref, gates_hbm, pack_down,
        first_out, second_out, dn2_ref, part_ref, down_ref,
        w1, w2, ab, hid, partial, load_sem, save_sems, *rest,
    ) = refs
    place = Place(count)
    seq, width = n2_ref.shape
    both = w1.shape[1]
    even = both // (2 * LANES)
    split = first_out.shape[1]
    lanes = lane_ids()
    place.greet(False, False)
    gather = Gather(place, pack_down, w2, rest[:5])
    scatter = Scatter(place, partial, down_ref, rest[5:])
    load = pltpu.make_async_copy(gates_hbm, w1, load_sem)
    load.start()
    gather.start()
    moves = gather.steps()
    load.wait()

    def gate_up(index, carry):
        cols = pl.ds(pl.multiple_of(index * 2 * LANES, 2 * LANES), 2 * LANES)
        got = dot_nn(n2_ref[...], w1[:, cols])
        gate, up = got[:, :LANES], got[:, LANES:]
        sig = jax.nn.sigmoid(gate)
        act = gate * sig
        hid[:, pl.ds(pl.multiple_of(index * LANES, LANES), LANES)] = (act * up).astype(BF16)
        slope = up * sig * (1.0 + gate * (1.0 - sig))
        ab[:, cols] = jnp.concatenate([slope, act], axis=1).astype(BF16)
        return carry

    third = even // 3
    for piece in range(3):
        lax.fori_loop(piece * third, even if piece == 2 else (piece + 1) * third, gate_up, 0)
        ahead(moves, 2)
    tail = pl.ds(2 * even * LANES, LANES)
    got = dot_nn(n2_ref[...], w1[:, tail])
    up = pltpu.roll(got, HALF, 1)
    sig = jax.nn.sigmoid(got)
    act = got * sig
    hid[:, pl.ds(even * LANES, LANES)] = jnp.where(lanes < HALF, act * up, 0.0).astype(BF16)
    slope = up * sig * (1.0 + got * (1.0 - sig))
    ab[:, tail] = jnp.where(lanes < HALF, slope, pltpu.roll(act, HALF, 1)).astype(BF16)
    ahead(moves, 2)

    def down_grad(start):
        partial[pl.ds(start, 384), :] = dot_tn(cot_ref[:, pl.ds(start, 384)], hid[...]).astype(BF16)

    blocks(width, 384, down_grad)
    scatter.start()
    sums = scatter.steps()
    drain(moves)
    ahead(sums, 4)
    gather.finish()

    def inner_grad(index, carry):
        got = dot_nn(cot_ref[...], w2[:, pl.ds(pl.multiple_of(index * 2 * LANES, 2 * LANES), 2 * LANES)])
        for side in range(2):
            piece = got[:, side * LANES : (side + 1) * LANES]
            cols = pl.ds(pl.multiple_of(index * 4 * LANES + side * 2 * LANES, 2 * LANES), 2 * LANES)
            ab[:, cols] = (ab[:, cols].astype(F32) * jnp.concatenate([piece, piece], axis=1)).astype(BF16)
        return carry

    lax.fori_loop(0, even // 2, inner_grad, 0)
    got = dot_nn(cot_ref[...], w2[:, pl.ds((even - 1) * LANES, 2 * LANES)])
    piece = got[:, :LANES]
    cols = pl.ds(2 * (even - 1) * LANES, 2 * LANES)
    ab[:, cols] = (ab[:, cols].astype(F32) * jnp.concatenate([piece, piece], axis=1)).astype(BF16)
    piece = got[:, LANES:]
    piece = jnp.where(lanes < HALF, piece, pltpu.roll(piece, HALF, 1))
    ab[:, tail] = (ab[:, tail].astype(F32) * piece).astype(BF16)
    ahead(sums, 2)

    def normed_grad(start):
        dn2_ref[:, pl.ds(start, 256)] = dot_nt(ab[...], w1[pl.ds(start, 256), :]).astype(dn2_ref.dtype)

    blocks(width, 256, normed_grad)
    ahead(sums, 2)

    def output_part(start):
        part_ref[:, pl.ds(start, 256)] = dot_nt(hid[...], w2[pl.ds(start, 256), :]).astype(BF16)

    blocks(width, 256, output_part)
    ahead(sums, 2)

    def gates_grad(start):
        rows = pl.ds(start, 384)
        for low, high in ((0, split), (split, both)):
            w1[rows, pl.ds(low, high - low)] = dot_tn(
                n2_ref[:, pl.ds(start, 384)], ab[:, pl.ds(low, high - low)]
            ).astype(BF16)

    blocks(width, 384, gates_grad)
    saves = [
        pltpu.make_async_copy(w1.at[:, pl.ds(0, split)], first_out, save_sems.at[0]),
        pltpu.make_async_copy(w1.at[:, pl.ds(split, both - split)], second_out, save_sems.at[1]),
    ]
    for save in saves:
        save.start()
    drain(sums)
    for save in saves:
        save.wait()
    gather.settle()
    scatter.settle()


def mlp_call(count, n2, cot, full_gates, pack_down):
    seq, width = n2.shape
    rows, down = pack_down.shape
    both = full_gates.shape[1]
    split = 14 * LANES
    shape = jax.ShapeDtypeStruct
    dma = pltpu.SemaphoreType.DMA
    return pl.pallas_call(
        functools.partial(mlp_kernel, count),
        out_shape=[
            shape((width, split), BF16),
            shape((width, both - split), BF16),
            shape((seq, width), BF16),
            shape((seq, width), BF16),
            shape((rows, down), F32),
        ],
        in_specs=[whole_block()] * 2 + [in_place()] * 2,
        out_specs=[in_place()] * 2 + [whole_block()] * 3,
        scratch_shapes=[
            pltpu.VMEM((width, both), BF16),
            pltpu.VMEM((width, down), BF16),
            pltpu.VMEM((seq, both), BF16),
            pltpu.VMEM((seq, down), BF16),
            pltpu.VMEM((width, down), BF16),
            dma,
            dma((2,)),
            *Gather.sems(count),
            *Scatter.scratch(count, rows, down),
        ],
        compiler_params=pltpu.CompilerParams(
            collective_id=2, has_side_effects=True, vmem_limit_bytes=61 << 20
        ),
    )(n2, cot, full_gates, pack_down)


def middle_kernel(count, *refs):
    (
        part_in, dn2_ref, h_ref, cot_ref, w0_ref, ctx_ref, gain_ref,
        gates_ref, dh_ref, dm_ref, dwo_ref, small_ref,
        partial, dhb, near, chip, far, sum_sems, load_sem, *rest,
    ) = refs
    place = Place(count)
    seq, width = dn2_ref.shape
    q_cols = ctx_ref.shape[1]
    heads = q_cols // HALF
    group = heads // 2
    tile = seq // 4
    lanes = lane_ids()
    load = pltpu.make_async_copy(part_in, partial, load_sem)
    load.start()
    place.greet(False, True)
    scatter = Scatter(place, partial, gates_ref, rest)
    summed = TensorSum(place, dn2_ref, dh_ref, 4, (near, chip, far, sum_sems))
    for index in range(4):
        summed.send_core(index)
    load.wait()
    scatter.start()
    sums = scatter.steps()
    for index in range(4):
        summed.send_across(index)
    ahead(sums, 2)
    for index in range(4):
        summed.send_back(index)
        ahead(sums, 1)
    g2 = gain_ref[pl.ds(1, 1), :]
    summed.settle()
    gain_sum = jnp.zeros((8, width), F32)
    for index in range(4):
        summed.finish(index)

        def residual_grad(sub, carry, index=index):
            rows = pl.ds(pl.multiple_of(index * tile + sub * 64, 64), 64)
            grad = dh_ref[rows, :]
            h = h_ref[rows, :]
            inverse = lax.rsqrt(jnp.mean(h * h, axis=1, keepdims=True) + EPSILON)
            scaled = grad * g2
            inner = jnp.mean(scaled * h, axis=1, keepdims=True)
            dh = cot_ref[rows, :].astype(F32) + inverse * scaled - h * (inverse * inverse * inverse * inner)
            dh_ref[rows, :] = dh
            dhb[rows, :] = dh.astype(BF16)
            return carry + jnp.sum((grad * h * inverse).reshape(8, 8, width), axis=0)

        gain_sum = lax.fori_loop(0, tile // 64, residual_grad, gain_sum)
        rows = pl.ds(index * tile, tile)
        dctx = dot_nn(dhb[rows, :], w0_ref[:, pl.ds(w0_ref.shape[1] - q_cols, q_cols)])
        for pair in range(heads // 2):
            value = dctx[:, pair * LANES : (pair + 1) * LANES]
            swapped = pltpu.roll(value, HALF, 1)
            for side in range(2):
                head = 2 * pair + side
                keep = value if side == head // group else swapped
                dm_ref[head, rows, :] = jnp.where(lanes // HALF == head // group, keep, 0.0).astype(BF16)
        ahead(sums, 1)
    small_ref[...] = gain_sum

    def out_grad(start):
        dwo_ref[pl.ds(start, 384), :] = dot_tn(dhb[:, pl.ds(start, 384)], ctx_ref[...]).astype(BF16)

    blocks(width, 384, out_grad)
    drain(sums)
    scatter.settle()


def middle_call(count, part, dn2, h, cot, w0, ctx, gains):
    seq, width = dn2.shape
    q_cols = ctx.shape[1]
    rows = width // count
    shape = jax.ShapeDtypeStruct
    dma = pltpu.SemaphoreType.DMA
    return pl.pallas_call(
        functools.partial(middle_kernel, count),
        out_shape=[
            shape((rows, part.shape[1]), F32),
            shape((seq, width), F32),
            shape((q_cols // HALF, seq, LANES), BF16),
            shape((width, q_cols), BF16),
            shape((8, width), F32),
        ],
        in_specs=[in_place()] + [whole_block()] * 6,
        out_specs=[whole_block()] * 5,
        scratch_shapes=[
            pltpu.VMEM(part.shape, BF16),
            pltpu.VMEM((seq, width), BF16),
            *TensorSum.scratch(seq, width, 4, BF16),
            dma,
            *Scatter.scratch(count, rows, part.shape[1]),
        ],
        compiler_params=pltpu.CompilerParams(
            collective_id=3, has_side_effects=True, vmem_limit_bytes=61 << 20
        ),
    )(part, dn2, h, cot, w0, ctx, gains)


def last_kernel(count, *refs):
    (
        part_in, dwo_in, mlp_ref, dm_ref, qm_ref, kb_ref, vb_ref, lse_ref, qk_ref, cos_ref, sin_ref,
        seg_col, seg_row, n1_ref, w0_ref, gain_ref,
        gates_ref, out_ref, qkv_ref, dn1_ref, mlp_total, small_ref,
        partial, partial_o, partial_qkv, bias, dk, dv, dlow, part1,
        near1, chip1, far1, sems1, near2, chip2, far2, sems2, load_sems, *rest,
    ) = refs
    place = Place(count)
    seq, width = n1_ref.shape
    kv_cols = kb_ref.shape[1]
    q_cols = qk_ref.shape[1] - kv_cols
    pairs = q_cols // LANES
    group = (q_cols // HALF) // (kv_cols // HALF)
    tile = seq // 4
    lanes = lane_ids()
    loads = [
        pltpu.make_async_copy(part_in, partial, load_sems.at[0]),
        pltpu.make_async_copy(dwo_in, partial_o, load_sems.at[1]),
    ]
    for load in loads:
        load.start()
    place.greet(False, True)
    third = len(rest) // 3
    scatter = Scatter(place, partial, gates_ref, rest[:third])
    scatter_o = Scatter(place, partial_o, out_ref, rest[third : 2 * third])
    scatter_qkv = Scatter(place, partial_qkv, qkv_ref, rest[2 * third :])
    summed = TensorSum(place, mlp_ref, mlp_total, 4, (near1, chip1, far1, sems1))
    for index in range(4):
        summed.send_core(index)
    for load in loads:
        load.wait()
    scatter.start()
    scatter_o.start()
    sums, sums_o = scatter.steps(), scatter_o.steps()
    for index in range(4):
        summed.send_across(index)
    dk[...] = jnp.zeros_like(dk)
    dv[...] = jnp.zeros_like(dv)
    gq = gain_ref[pl.ds(2, 1), pl.ds(0, LANES)]
    gk = gain_ref[pl.ds(3, 1), pl.ds(0, LANES)]

    def head_back(grad, raw, cosine, sine, gain):
        back = turn(grad, cosine, -sine)
        inverse = lax.rsqrt(head_mean(raw * raw) + EPSILON)
        scaled = back * gain
        inner = head_mean(scaled * raw)
        low = inverse * scaled - raw * (inverse * inverse * inverse * inner)
        return low.astype(BF16), jnp.sum((back * raw * inverse).reshape(-1, 8, LANES), axis=0)

    gain_q = jnp.zeros((8, LANES), F32)
    for qb in range(4):
        last = (qb + 1) * tile
        rows = pl.ds(qb * tile, tile)
        bias_block(seg_col, seg_row, bias, qb * tile, tile)

        def attend_back(pair, carry, last=last, rows=rows):
            keys = pl.ds(0, last)
            sides = []
            for side in range(2):
                head = 2 * pair + side
                kv = head // group
                query, grad = qm_ref[head, rows, :], dm_ref[head, rows, :]
                logsum = jnp.sum(jnp.where(lanes == head, lse_ref[rows, :], 0.0), axis=1, keepdims=True)
                logits = dot_nt(query, kb_ref[keys, :]) + bias[:, keys]
                probs = jnp.exp(logits - logsum)
                dprob = dot_nt(grad, vb_ref[keys, :])
                inner = jnp.sum(probs * dprob, axis=1, keepdims=True)
                ds = (probs * (dprob - inner)).astype(BF16)
                got = dot_nn(ds, kb_ref[keys, :]) * 0.125
                sides.append(jnp.where(kv == side, got, pltpu.roll(got, HALF, 1)))
                dk[keys, :] += dot_tn(ds, query)
                dv[keys, :] += dot_tn(probs.astype(BF16), grad)
            cols = pl.ds(pl.multiple_of(pair * LANES, LANES), LANES)
            low, terms = head_back(
                jnp.where(lanes < HALF, sides[0], sides[1]), qk_ref[rows, cols], cos_ref[rows, :], sin_ref[rows, :], gq
            )
            dlow[rows, cols] = low
            return carry + terms

        gain_q = lax.fori_loop(0, pairs, attend_back, gain_q)
        summed.send_back(qb)
        ahead(sums, 2)
        ahead(sums_o, 1)
    gain_k = jnp.zeros((8, LANES), F32)
    for qb in range(4):
        rows = pl.ds(qb * tile, tile)
        low, terms = head_back(
            dk[rows, :], qk_ref[rows, pl.ds(q_cols, LANES)], cos_ref[rows, :], sin_ref[rows, :], gk
        )
        dlow[rows, pl.ds(q_cols, LANES)] = low
        dlow[rows, pl.ds(q_cols + LANES, LANES)] = dv[rows, :].astype(BF16)
        gain_k = gain_k + terms
    small_ref[pl.ds(0, 8), :] = gain_q
    small_ref[pl.ds(8, 8), :] = gain_k
    final = TensorSum(place, part1, dn1_ref, 4, (near2, chip2, far2, sems2))
    for index in range(4):
        rows = pl.ds(index * tile, tile)
        part1[rows, :] = dot_nt(dlow[rows, :], w0_ref[:, pl.ds(0, dlow.shape[1])]).astype(BF16)
        final.send_core(index)
    ahead(sums, 1)
    for index in range(4):
        final.send_across(index)

    def qkv_grad(start):
        partial_qkv[pl.ds(start, 384), :] = dot_tn(n1_ref[:, pl.ds(start, 384)], dlow[...]).astype(BF16)

    blocks(width, 384, qkv_grad)
    scatter_qkv.start()
    sums_qkv = scatter_qkv.steps()
    drain(sums, sums_o)
    for index in range(4):
        final.send_back(index)
        ahead(sums_qkv, 2)
    for index in range(4):
        summed.finish(index)
        final.finish(index)
        ahead(sums_qkv, 2)
    drain(sums_qkv)
    for one in (scatter, scatter_o, scatter_qkv, summed, final):
        one.settle()


def last_call(count, part, dwo, mlp, dm, qm, kb, vb, lse, qk, cosine, sine, seg_col, seg_row, n1, w0, gains):
    seq, width = n1.shape
    rows = width // count
    q_cols = dwo.shape[1]
    low = qk.shape[1] + LANES
    shape = jax.ShapeDtypeStruct
    dma = pltpu.SemaphoreType.DMA
    return pl.pallas_call(
        functools.partial(last_kernel, count),
        out_shape=[
            shape((rows, part.shape[1]), F32),
            shape((rows, q_cols), F32),
            shape((rows, low), F32),
            shape((seq, width), BF16),
            shape((seq, width), BF16),
            shape((16, LANES), F32),
        ],
        in_specs=[in_place()] * 2 + [whole_block()] * 14,
        out_specs=[whole_block()] * 6,
        scratch_shapes=[
            pltpu.VMEM(part.shape, BF16),
            pltpu.VMEM(dwo.shape, BF16),
            pltpu.VMEM((width, low), BF16),
            pltpu.VMEM((seq // 4, seq), F32),
            pltpu.VMEM((seq, LANES), F32),
            pltpu.VMEM((seq, LANES), F32),
            pltpu.VMEM((seq, low), BF16),
            pltpu.VMEM((seq, width), BF16),
            *TensorSum.scratch(seq, width, 4, BF16),
            *TensorSum.scratch(seq, width, 4, BF16),
            dma((2,)),
            *Scatter.scratch(count, rows, part.shape[1]),
            *Scatter.scratch(count, rows, q_cols),
            *Scatter.scratch(count, rows, low),
        ],
        compiler_params=pltpu.CompilerParams(
            collective_id=4, has_side_effects=True, vmem_limit_bytes=61 << 20
        ),
    )(part, dwo, mlp, dm, qm, kb, vb, lse, qk, cosine, sine, seg_col, seg_row, n1, w0, gains)


def rotation_tables(positions, head_dim):
    half_dim = head_dim // 2
    frequency = ROPE_BASE ** (-jnp.arange(half_dim, dtype=jnp.float32) * 2.0 / head_dim)
    angles = positions.astype(jnp.float32)[:, None] * frequency[None, :]
    return (jnp.cos(angles)[:, None, :], jnp.sin(angles)[:, None, :])


def lay(gate, up):
    rows, cols = gate.shape
    even = cols // LANES * LANES
    pairs = jnp.stack(
        [gate[:, :even].reshape(rows, -1, LANES), up[:, :even].reshape(rows, -1, LANES)], axis=2
    ).reshape(rows, 2 * even)
    return jnp.concatenate([pairs, gate[:, even:], up[:, even:]], axis=1)


def unlay(both):
    rows, cols = both.shape
    even = cols // 2 // LANES * LANES
    pairs = both[:, : 2 * even].reshape(rows, -1, 2, LANES)
    rest = both[:, 2 * even :]
    size = rest.shape[1] // 2
    return (
        jnp.concatenate([pairs[:, :, 0].reshape(rows, even), rest[:, :size]], axis=1),
        jnp.concatenate([pairs[:, :, 1].reshape(rows, even), rest[:, size:]], axis=1),
    )


def spread(gain, me, width):
    full = jnp.zeros((width,), F32)
    return lax.dynamic_update_slice(full, gain.astype(BF16).astype(F32), (me * gain.shape[0],))


def gain_rows(norm1_gain, norm2_gain, q_gain, k_gain, count):
    me = lax.axis_index("dp")
    width = norm1_gain.shape[0] * count
    head = q_gain.shape[0] * count
    rows = [spread(norm1_gain, me, width), spread(norm2_gain, me, width)]
    for gain in (q_gain, k_gain):
        one = spread(gain, me, head)
        rows.append(jnp.pad(jnp.concatenate([one, one]), (0, width - 2 * head)))
    return jnp.pad(jnp.stack(rows), ((0, 4), (0, 0)))


def rotation_lanes(positions):
    cosine, sine = rotation_tables(positions, HALF)
    cosine, sine = cosine[:, 0], sine[:, 0]
    return (
        jnp.concatenate([cosine] * 4, axis=1),
        jnp.concatenate([-sine, sine, -sine, sine], axis=1),
    )


def shards(
    block_input,
    segments,
    positions,
    norm1_gain,
    q_norm_gain,
    k_norm_gain,
    w_q,
    w_k,
    w_v,
    w_o,
    norm2_gain,
    w_gate,
    w_up,
    w_down,
    cotangent,
    *,
    n_dp,
    n_tensor,
):
    rows = w_q.shape[0]
    q_cols, kv_cols, ff_cols = w_q.shape[1], w_k.shape[1], w_gate.shape[1]
    small_gain = q_norm_gain.shape[0]
    head_dim = small_gain * n_dp
    seg_col, seg_row = segments[:, None], segments[None, :]
    gains = gain_rows(norm1_gain, norm2_gain, q_norm_gain, k_norm_gain, n_dp)
    pack_attn = jnp.concatenate(
        [w_q.astype(BF16), w_k.astype(BF16), w_v.astype(BF16), w_o.T.astype(BF16)], axis=1
    )
    pack_gates = lay(w_gate.astype(BF16), w_up.astype(BF16))
    pack_down = jnp.pad(w_down.T.astype(BF16), ((0, 0), (0, -ff_cols % LANES)))
    cosine, sine = rotation_lanes(positions)
    w0, w1, n1, qk, qm, kb, vb, lse, ctx, h, n2, gains = forward_call(
        n_dp, block_input, seg_col, seg_row, cosine, sine, gains, pack_attn, pack_gates
    )
    first, second, dn2, mlp, down = mlp_call(n_dp, n2, cotangent, w1, pack_down)
    gates_one, dh, dm, dwo, small_two = middle_call(n_dp, first, dn2, h, cotangent, w0, ctx, gains)
    gates_two, grad_o, grad_qkv, dn1, mlp_total, small_heads = last_call(
        n_dp, second, dwo, mlp, dm, qm, kb, vb, lse, qk, cosine, sine, seg_col, seg_row, n1, w0, gains
    )
    output_rows = (h + mlp_total.astype(F32)).astype(BF16)
    x = block_input.astype(F32)
    grad = dn1.astype(F32)
    inverse = lax.rsqrt(jnp.mean(x * x, axis=-1, keepdims=True) + EPSILON)
    scaled = grad * gains[0]
    inner = jnp.mean(scaled * x, axis=-1, keepdims=True)
    grad_input = dh + inverse * scaled - x * (inverse * inverse * inverse) * inner
    grad_gain_one = jnp.sum(grad * x * inverse, axis=0)
    share = 1.0 / n_tensor
    heads = small_heads.reshape(2, 8, 2, head_dim).sum(axis=(1, 2))
    small = lax.psum(
        jnp.concatenate([grad_gain_one * share, small_two.sum(axis=0) * share, heads[0], heads[1]]),
        ("dp", "tensor"),
    )
    me = lax.axis_index("dp")
    width = block_input.shape[1]

    def own(start, size):
        return lax.dynamic_slice_in_dim(small, start + me * size, size, 0)

    grad_gate, grad_up = unlay(jnp.concatenate([gates_one, gates_two], axis=1))
    return (
        output_rows,
        grad_input,
        own(0, rows),
        own(2 * width, small_gain),
        own(2 * width + head_dim, small_gain),
        grad_qkv[:, :q_cols],
        grad_qkv[:, q_cols : q_cols + kv_cols],
        grad_qkv[:, q_cols + kv_cols :],
        grad_o.T,
        own(width, rows),
        grad_gate,
        grad_up,
        down[:, :ff_cols].T,
    )


def solution(mesh):
    placed = (
        P("dp", None),
        P("dp"),
        P("dp"),
        P("dp"),
        P("dp"),
        P("dp"),
        P("dp", "tensor"),
        P("dp", "tensor"),
        P("dp", "tensor"),
        P("tensor", "dp"),
        P("dp"),
        P("dp", "tensor"),
        P("dp", "tensor"),
        P("tensor", "dp"),
        P("dp", None),
    )
    return jax.shard_map(
        functools.partial(shards, n_dp=mesh.shape["dp"], n_tensor=mesh.shape["tensor"]),
        mesh=mesh,
        in_specs=placed,
        out_specs=(
            P("dp", None),
            P("dp", None),
            P("dp"),
            P("dp"),
            P("dp"),
            P("dp", "tensor"),
            P("dp", "tensor"),
            P("dp", "tensor"),
            P("tensor", "dp"),
            P("dp"),
            P("dp", "tensor"),
            P("dp", "tensor"),
            P("tensor", "dp"),
        ),
        check_vma=False,
    )
```

```python
import functools

import jax
import jax.numpy as jnp
from jax import lax
from jax.experimental import pallas as pl
from jax.experimental.pallas import tpu as pltpu
from jax.sharding import PartitionSpec as P

EPSILON = 1e-05
ROPE_BASE = 1000000.0
MASKED = -1e30


MESH = pl.DeviceIdType.MESH
NEAR = 2
HALF = 64
LANES = 128
HIGHEST = lax.Precision.HIGHEST
BF16 = jnp.bfloat16
F32 = jnp.float32


def whole_block():
    return pl.BlockSpec(memory_space=pltpu.VMEM)


def in_place():
    return pl.BlockSpec(memory_space=pl.ANY)


def remote(src, dst, send, recv, dp, tensor):
    return pltpu.make_async_remote_copy(
        src_ref=src,
        dst_ref=dst,
        send_sem=send,
        recv_sem=recv,
        device_id=(dp, tensor),
        device_id_type=MESH,
    )


def begin(src, dst, sem):
    copy = pltpu.make_async_copy(src, dst, sem)
    copy.start()
    return copy


def dot_nn(left, right):
    return jnp.dot(left, right, preferred_element_type=F32)


def dot_nt(left, right):
    return lax.dot_general(left, right, (((1,), (1,)), ((), ())), preferred_element_type=F32)


def dot_tn(left, right):
    return lax.dot_general(left, right, (((0,), (0,)), ((), ())), preferred_element_type=F32)


class Place:
    def __init__(self, count):
        self.count = count
        self.depth = count // NEAR
        self.me = lax.axis_index("dp")
        self.tensor = lax.axis_index("tensor")
        self.far = self.me // NEAR
        self.near = lax.rem(self.me, NEAR)
        self.core = lax.rem(self.tensor, 2)
        self.mate = self.tensor + 1 - 2 * self.core
        self.across = lax.rem(self.tensor + 2, 4)
        self.beside = self.me + 1 - 2 * self.near

    def ahead(self, step):
        return lax.rem(self.far + step, self.depth)

    def behind(self, step):
        return lax.rem(self.far + self.depth - step, self.depth)

    def greet(self, everyone, tensor):
        barrier = pltpu.get_barrier_semaphore()
        peers = []
        if everyone:
            peers += [(lax.rem(self.me + d, self.count), self.tensor) for d in range(1, self.count)]
        else:
            peers += [
                (self.ahead(step) * NEAR + self.near, self.tensor) for step in range(1, self.depth)
            ]
            peers.append((self.beside, self.tensor))
        if tensor:
            peers += [(self.me, lax.rem(self.tensor + t, 4)) for t in range(1, 4)]
        for peer in peers:
            pl.semaphore_signal(barrier, 1, device_id=peer, device_id_type=MESH)
        pl.semaphore_wait(barrier, len(peers))


class Gather:
    def __init__(self, place, shard, full, late, sems):
        self.place, self.shard, self.full = place, shard, full
        self.rows = shard.shape[0]
        self.cuts = [(0, self.rows - late)] + ([(self.rows - late, late)] if late else [])
        self.zsend, self.zrecv, self.ysend, self.yrecv, self.own = sems
        self.sent = []

    @staticmethod
    def sems(count):
        depth = count // NEAR
        dma = pltpu.SemaphoreType.DMA
        return [dma((2, depth - 1, 3)), dma((2, depth - 1, 3)), dma((2 * depth - 1, 2)), dma((2 * depth - 1, 2)), dma]

    def spot(self, block, cut):
        start, size = self.cuts[cut]
        return self.full.at[pl.ds(pl.multiple_of(block * self.rows + start, 16), size), :]

    def mine(self, cut):
        start, size = self.cuts[cut]
        return self.shard.at[pl.ds(start, size), :]

    def block(self, way, step, other):
        far = self.place.far - step if way == 0 else self.place.far + step
        return far * NEAR + (1 - self.place.near if other else self.place.near)

    def valid(self, way, step):
        return self.place.far >= step if way == 0 else self.place.far + step < self.place.depth

    def emit(self, make):
        copy, when = make()
        if when is None:
            copy.start()
        else:
            pl.when(when)(copy.start)
        self.sent.append(make)

    def along(self, way, step, cut, other):
        place = self.place
        if step >= place.depth - 1:
            return

        def make():
            more = place.far < place.depth - 1 if way == 0 else place.far > 0
            spot = self.spot(self.block(way, step, other), cut)
            copy = remote(
                self.mine(cut) if step == 0 and not other else spot, spot,
                self.zsend.at[way, step, cut + other], self.zrecv.at[way, step, cut + other],
                place.me + (NEAR if way == 0 else -NEAR), place.tensor,
            )
            return copy, more if step == 0 else more & self.valid(way, step)

        self.emit(make)

    def crossing(self, way, step, cut, other):
        place = self.place
        spot = self.spot(self.block(way, step, other), cut)
        slot = step if way == 0 else step + place.depth - 1
        return remote(
            self.mine(cut) if step == 0 and not other else spot, spot,
            self.ysend.at[slot, cut], self.yrecv.at[slot, cut], place.beside, place.tensor,
        ), (self.valid(way, step) if step else None)

    def over(self, way, step, cut):
        self.emit(lambda: self.crossing(way, step, cut, 0))

    def came_over(self, way, step, cut):
        copy, when = self.crossing(way, step, cut, 1)
        if when is None:
            copy.wait_recv()
        else:
            pl.when(when)(copy.wait_recv)

    def start(self):
        place = self.place
        self.local = lambda: pltpu.make_async_copy(
            self.shard, self.full.at[pl.ds(pl.multiple_of(place.me * self.rows, 16), self.rows), :], self.own
        )
        self.local().start()
        for cut in reversed(range(len(self.cuts))):
            self.over(0, 0, cut)
        for cut in range(len(self.cuts)):
            for way in range(2):
                self.along(way, 0, cut, 0)

    def steps(self):
        place = self.place
        if len(self.cuts) > 1:
            self.came_over(0, 0, 1)
            for way in range(2):
                self.along(way, 0, 1, 1)
            yield
        for step in range(1, place.depth):
            for cut in range(len(self.cuts)):
                for other in range(cut + 1):
                    for way in range(2):
                        spot = self.spot(self.block(way, step, other), cut)
                        copy = remote(
                            spot, spot, self.zsend.at[way, step - 1, cut + other],
                            self.zrecv.at[way, step - 1, cut + other], place.me, place.tensor,
                        )
                        pl.when(self.valid(way, step))(copy.wait_recv)
                        self.along(way, step, cut, other)
                        if cut == 0:
                            self.over(way, step, cut)
                    yield

    def finish(self):
        self.came_over(0, 0, 0)
        for step in range(1, self.place.depth):
            for way in range(2):
                self.came_over(way, step, 0)
        self.local().wait()

    def settle(self):
        for make in self.sent:
            copy, when = make()
            if when is None:
                copy.wait_send()
            else:
                pl.when(when)(copy.wait_send)


def late_share(rows, share):
    return int(rows * share) // 16 * 16


class TensorSum:
    def __init__(self, place, part, total, tiles, scratch):
        self.place, self.part, self.total, self.tiles = place, part, total, tiles
        self.tile = part.shape[0] // tiles
        self.half = self.tile // 2
        self.near, self.chip, self.far, self.sems = scratch
        self.sent = []

    @staticmethod
    def scratch(rows, width, tiles, kind):
        half = (rows // 2, width)
        return [
            pltpu.VMEM(half, kind), pltpu.VMEM(half, BF16), pltpu.VMEM(half, BF16), pltpu.SemaphoreType.DMA((6, tiles))
        ]

    def half_rows(self, index, which):
        return pl.ds(pl.multiple_of(index * self.tile + which * self.half, 16), self.half)

    def slot(self, index):
        return pl.ds(index * self.half, self.half)

    def core_copy(self, index):
        place = self.place
        return remote(
            self.part.at[self.half_rows(index, 1 - place.core), :], self.near.at[self.slot(index), :],
            self.sems.at[0, index], self.sems.at[1, index], place.me, place.mate,
        )

    def across_copy(self, index):
        place = self.place
        return remote(
            self.chip.at[self.slot(index), :], self.far.at[self.slot(index), :],
            self.sems.at[2, index], self.sems.at[3, index], place.me, place.across,
        )

    def back_copy(self, index, which):
        place = self.place
        rows = self.half_rows(index, which)
        return remote(
            self.total.at[rows, :], self.total.at[rows, :],
            self.sems.at[4, index], self.sems.at[5, index], place.me, place.mate,
        )

    def send_core(self, index):
        self.core_copy(index).start()
        self.sent.append(lambda: self.core_copy(index))

    def send_across(self, index):
        place = self.place
        self.core_copy(index).wait_recv()
        mine = self.part[self.half_rows(index, place.core), :].astype(F32)
        self.chip[self.slot(index), :] = (mine + self.near[self.slot(index), :].astype(F32)).astype(BF16)
        self.across_copy(index).start()
        self.sent.append(lambda: self.across_copy(index))

    def send_back(self, index):
        place = self.place
        self.across_copy(index).wait_recv()
        both = self.chip[self.slot(index), :].astype(F32) + self.far[self.slot(index), :].astype(F32)
        self.total[self.half_rows(index, place.core), :] = both.astype(self.total.dtype)
        self.back_copy(index, place.core).start()

    def finish(self, index):
        self.back_copy(index, 1 - self.place.core).wait_recv()
        self.back_copy(index, self.place.core).wait_send()

    def steps(self):
        for index in range(2):
            self.send_across(index)
            yield
        for index in range(self.tiles):
            self.send_back(index)
            if index + 2 < self.tiles:
                self.send_across(index + 2)
            yield

    def settle(self):
        for make in self.sent:
            make().wait_send()


def lane_ids(width=LANES):
    return lax.broadcasted_iota(jnp.int32, (1, width), 1)


def head_mean(values):
    row = lax.broadcasted_iota(jnp.int32, (LANES, LANES), 0)
    col = lax.broadcasted_iota(jnp.int32, (LANES, LANES), 1)
    groups = jnp.where(row // HALF == col // HALF, 1.0 / HALF, 0.0).astype(F32)
    return jnp.dot(values, groups, precision=HIGHEST, preferred_element_type=F32)


def turn(values, cosine, sine):
    ahead = pltpu.roll(values, LANES - HALF // 2, 1)
    back = pltpu.roll(values, HALF // 2, 1)
    first = lax.rem(lane_ids(), HALF) < HALF // 2
    return values * cosine + jnp.where(first, ahead, back) * sine


def bias_block(seg_col, seg_row, bias, first, tile):
    last = first + tile
    rows = lax.broadcasted_iota(jnp.int32, (tile, last), 0) + first
    cols = lax.broadcasted_iota(jnp.int32, (tile, last), 1)
    allowed = (seg_col[pl.ds(first, tile), :] == seg_row[:, pl.ds(0, last)]) & (rows >= cols)
    bias[:, pl.ds(0, last)] = jnp.where(allowed, 0.0, MASKED)


def drain(*moves):
    for one in moves:
        for _ in one:
            pass


def ahead(moves, count=1):
    for _ in range(count):
        next(moves, None)


def polled(count, body, *polls):
    def step(index, carry):
        body(index)
        for at in range(count):
            due = [(moves, times[at]) for moves, times in polls if at in times]
            if due:

                @pl.when(index == at)
                def _(due=due):
                    for moves, times in due:
                        ahead(moves, times)

        return carry

    lax.fori_loop(0, count, step, 0)


def every(count, times=1, first=0):
    return {index: times for index in range(first, count)}


def blocks(total, size, body):
    def step(index, carry):
        body(pl.multiple_of(index * size, size))
        return carry

    lax.fori_loop(0, total // size, step, 0)


def forward_kernel(count, *refs):
    (
        x_hbm, seg_col, seg_row, cos_ref, sin_ref, gain_ref, pack_attn, pack_gates,
        full_attn, full_gates, n1_out, qk_out, qm_out, kb_out, vb_out, lse_out, ctx_out, h_out, n2_out, gains_out,
        x_ref, w0, n1_ref, qk_ref, qm_ref, kb_ref, vb_ref, lse_ref, ctx_ref, h_ref, n2_ref,
        bias, gain_slots, part, total, tmp_near, tmp_chip, tmp_far, sum_sems, gain_send, gain_recv, copy_sems,
        *gather_sems,
    ) = refs
    place = Place(count)
    seq, width = x_ref.shape
    q_cols = ctx_ref.shape[1]
    kv_cols = kb_ref.shape[1]
    pairs = q_cols // LANES
    group = (q_cols // HALF) // (kv_cols // HALF)
    tile = seq // 4
    load = begin(x_hbm, x_ref, copy_sems.at[0])
    place.greet(True, True)
    first = Gather(place, pack_attn, w0, late_share(pack_attn.shape[0], 1 / 6), gather_sems[:5])
    second = Gather(place, pack_gates, full_gates, late_share(pack_gates.shape[0], 1 / 6), gather_sems[5:])
    gain_copies = []
    for step in range(1, count):
        copy = remote(
            gain_ref, gain_slots.at[step], gain_send.at[step], gain_recv.at[step],
            lax.rem(place.me + step, count), place.tensor,
        )
        copy.start()
        gain_copies.append(copy)
    first.start()
    for qb in range(4):
        bias_block(seg_col, seg_row, bias.at[qb], qb * tile, tile)
    gains = gain_ref[...]
    for copy in gain_copies:
        copy.wait_recv()
    for step in range(1, count):
        gains = gains + gain_slots[step]
    gains_out[...] = gains
    moves_first = first.steps()
    ahead(moves_first, 2)
    g1 = gains_out[pl.ds(0, 1), :]
    g2 = gains_out[pl.ds(1, 1), :]
    load.wait()

    def norm_one(index, carry):
        rows = pl.ds(pl.multiple_of(index * LANES, LANES), LANES)
        x = x_ref[rows, :].astype(F32)
        inverse = lax.rsqrt(jnp.mean(x * x, axis=1, keepdims=True) + EPSILON)
        n1_ref[rows, :] = (x * inverse * g1).astype(BF16)
        return carry

    lax.fori_loop(0, seq // LANES, norm_one, 0)
    saves = [begin(n1_ref, n1_out, copy_sems.at[1])]
    drain(moves_first)
    second.start()
    moves = second.steps()
    first.finish()
    saves.append(begin(w0, full_attn, copy_sems.at[2]))
    gq = gains_out[pl.ds(2, 1), pl.ds(0, LANES)]
    gk = gains_out[pl.ds(3, 1), pl.ds(0, LANES)]
    lanes = lane_ids()

    def project(index, carry):
        rows = pl.ds(pl.multiple_of(index * tile, tile), tile)
        qkv = dot_nn(n1_ref[rows, :], w0[:, pl.ds(0, q_cols + 2 * kv_cols)])
        qk_ref[rows, :] = qkv[:, : q_cols + kv_cols]
        vb_ref[rows, :] = qkv[:, q_cols + kv_cols :].astype(BF16)
        cosine, sine = cos_ref[rows, :], sin_ref[rows, :]
        for pair in range(pairs + 1):
            raw = qkv[:, pair * LANES : (pair + 1) * LANES]
            inverse = lax.rsqrt(head_mean(raw * raw) + EPSILON)
            turned = turn(raw * inverse * (gk if pair == pairs else gq), cosine, sine)
            if pair == pairs:
                kb_ref[rows, :] = turned.astype(BF16)
                continue
            swapped = pltpu.roll(turned, HALF, 1)
            for side in range(2):
                head = 2 * pair + side
                kv = head // group
                keep = (turned if side == kv else swapped).astype(BF16) * 0.125
                qm_ref[head, rows, :] = jnp.where(lanes // HALF == kv, keep, jnp.zeros_like(keep))
        return carry

    lax.fori_loop(0, 4, project, 0)
    for index, (src, dst) in enumerate(((qk_ref, qk_out), (qm_ref, qm_out), (kb_ref, kb_out), (vb_ref, vb_out))):
        saves.append(begin(src, dst, copy_sems.at[3 + index]))
    next(moves, None)

    for qb in range(4):
        last = (qb + 1) * tile
        rows = pl.ds(qb * tile, tile)

        def attend(pair, carry, last=last, rows=rows, qb=qb):
            halves, sums = [], []
            for side in range(2):
                head = 2 * pair + side
                kv = head // group
                logits = dot_nt(qm_ref[head, rows, :], kb_ref[pl.ds(0, last), :]) + bias[qb, :, pl.ds(0, last)]
                top = jnp.max(logits, axis=1, keepdims=True)
                expo = jnp.exp(logits - top)
                summed = jnp.sum(expo, axis=1, keepdims=True)
                probs = (expo * (1.0 / summed)).astype(BF16)
                got = dot_nn(probs, vb_ref[pl.ds(0, last), :])
                halves.append(jnp.where(kv == side, got, pltpu.roll(got, HALF, 1)))
                sums.append(top + jnp.log(summed))
            ctx_ref[rows, pl.ds(pl.multiple_of(pair * LANES, LANES), LANES)] = jnp.where(
                lanes < HALF, halves[0], halves[1]
            ).astype(BF16)
            carry = jnp.where(lanes == 2 * pair, sums[0], carry)
            return jnp.where(lanes == 2 * pair + 1, sums[1], carry)

        lse_ref[rows, :] = lax.fori_loop(0, pairs, attend, jnp.zeros((tile, LANES), F32))
        next(moves, None)
    saves.append(begin(lse_ref, lse_out, copy_sems.at[7]))
    saves.append(begin(ctx_ref, ctx_out, copy_sems.at[8]))

    summed = TensorSum(place, part, total, 4, (tmp_near, tmp_chip, tmp_far, sum_sems))
    for index in range(4):
        rows = pl.ds(index * tile, tile)
        part[rows, :] = dot_nt(ctx_ref[rows, :], w0[:, pl.ds(q_cols + 2 * kv_cols, q_cols)])
        summed.send_core(index)
    summed.send_across(0)
    summed.send_across(1)
    next(moves, None)
    for index in range(4):
        summed.send_back(index)
        if index < 2:
            summed.send_across(index + 2)
        next(moves, None)
        summed.finish(index)

        def norm_two(sub, carry, index=index):
            rows = pl.ds(pl.multiple_of(index * tile + sub * LANES, LANES), LANES)
            h = x_ref[rows, :].astype(F32) + total[rows, :]
            h_ref[rows, :] = h
            inverse = lax.rsqrt(jnp.mean(h * h, axis=1, keepdims=True) + EPSILON)
            n2_ref[rows, :] = (h * inverse * g2).astype(BF16)
            return carry

        lax.fori_loop(0, tile // LANES, norm_two, 0)
        next(moves, None)
    saves.append(begin(h_ref, h_out, copy_sems.at[9]))
    saves.append(begin(n2_ref, n2_out, copy_sems.at[10]))
    drain(moves)
    second.finish()
    for save in saves:
        save.wait()
    for copy in gain_copies:
        copy.wait_send()
    first.settle()
    second.settle()
    summed.settle()


def forward_call(count, x, seg_col, seg_row, cosine, sine, gains, pack_attn, pack_gates):
    seq, width = x.shape
    rows = pack_attn.shape[0]
    q_cols, kv_cols = 384, LANES
    kept = [
        ((seq, width), BF16),
        ((seq, q_cols + kv_cols), F32),
        ((q_cols // HALF, seq, LANES), BF16),
        ((seq, LANES), BF16),
        ((seq, LANES), BF16),
        ((seq, LANES), F32),
        ((seq, q_cols), BF16),
        ((seq, width), F32),
        ((seq, width), BF16),
    ]
    attn = ((count * rows, pack_attn.shape[1]), BF16)
    outs = [attn, ((count * rows, pack_gates.shape[1]), BF16), *kept, (gains.shape, F32)]
    dma = pltpu.SemaphoreType.DMA
    return pl.pallas_call(
        functools.partial(forward_kernel, count),
        out_shape=[jax.ShapeDtypeStruct(*out) for out in outs],
        in_specs=[in_place()] + [whole_block()] * 5 + [in_place()] * 2,
        out_specs=[in_place()] * 11 + [whole_block()],
        scratch_shapes=[
            pltpu.VMEM((seq, width), BF16),
            pltpu.VMEM(*attn),
            *[pltpu.VMEM(*one) for one in kept],
            pltpu.VMEM((4, seq // 4, seq), F32),
            pltpu.VMEM((count,) + gains.shape, F32),
            pltpu.VMEM((seq, width), F32),
            pltpu.VMEM((seq, width), F32),
            *TensorSum.scratch(seq, width, 4, F32),
            dma((count,)),
            dma((count,)),
            dma((11,)),
            *Gather.sems(count),
            *Gather.sems(count),
        ],
        compiler_params=pltpu.CompilerParams(
            collective_id=1, has_side_effects=True, vmem_limit_bytes=61 << 20
        ),
    )(x, seg_col, seg_row, cosine, sine, gains, pack_attn, pack_gates)


class Scatter:
    def __init__(self, place, partial, result, late, scratch):
        self.place, self.partial, self.result = place, partial, result
        self.rows = partial.shape[0] // place.count
        self.late = late
        early = self.rows - late
        half = (early // 2 + 15) // 16 * 16
        self.cuts = [(0, half), (half, early - half)] if early > half else [(0, early)]
        self.tail = (early, late)
        self.over_in, self.far_in, self.far_other, self.late_in = scratch[:4]
        self.zsend, self.zrecv, self.ysend, self.yrecv, self.lsend, self.lrecv = scratch[4:]
        self.sent = []
        depth = place.depth
        orders = [
            sorted(range(depth), key=lambda goal, far=far: (-abs(goal - far), -goal)) for far in range(depth)
        ]
        self.goals = []
        for index in range(depth):
            goal = jnp.int32(0)
            for far in range(depth):
                goal = goal + orders[far][index] * (place.far == far).astype(jnp.int32)
            self.goals.append(goal)
        self.pieces = [(index, cut) for index in range(depth) for cut in range(len(self.cuts))]

    @staticmethod
    def scratch(count, rows, width, late):
        depth = count // NEAR
        dma = pltpu.SemaphoreType.DMA
        return [
            pltpu.VMEM((depth, rows - late, width), BF16),
            pltpu.VMEM((depth + 2, rows, width), BF16),
            pltpu.VMEM((depth + 2, max(late, 16), width), BF16),
            pltpu.VMEM((max(late, 16), width), BF16),
            dma((depth - 1, 4)),
            dma((depth + 2, 4)),
            dma((depth, 2)),
            dma((depth, 2)),
            dma,
            dma,
        ]

    def spot(self, goal, other, start, size):
        near = 1 - self.place.near if other else self.place.near
        return pl.ds(pl.multiple_of((goal * NEAR + near) * self.rows + start, 16), size)

    def over(self, number):
        place = self.place
        index, cut = self.pieces[number]
        start, size = self.cuts[cut]
        return remote(
            self.partial.at[self.spot(self.goals[index], True, start, size), :],
            self.over_in.at[index, pl.ds(start, size), :],
            self.ysend.at[index, cut], self.yrecv.at[index, cut], place.beside, place.tensor,
        )

    def cross(self, number):
        if number < len(self.pieces):
            self.over(number).start()
            self.sent.append(lambda: self.over(number))

    def start(self):
        for number in range(len(self.cuts)):
            self.cross(number)

    def add(self, spot, sources):
        size = sources[0].shape[0]
        part = 32 if size % 32 == 0 else 16

        def body(index, carry):
            start = pl.multiple_of(index * part, 16)
            rows = pl.ds(pl.multiple_of(spot.start + start, 16), part)
            total = self.partial[rows, :].astype(F32)
            for source in sources:
                total = total + source[pl.ds(start, part), :].astype(F32)
            self.partial[rows, :] = total.astype(BF16)
            return carry

        lax.fori_loop(0, size // part, body, 0)

    def item(self, item):
        return (0, *self.cuts[item]) if item < 2 else (item - 2, *self.tail)

    def into(self, slot, item):
        other, start, size = self.item(item)
        return self.far_other.at[slot] if other else self.far_in.at[slot, pl.ds(start, size), :]

    def wait_far(self, slot, item):
        place = self.place
        into = self.into(slot, item)
        remote(
            into, into, self.zsend.at[0, item], self.zrecv.at[slot, item], place.me, place.tensor
        ).wait_recv()
        return into

    def hop(self, index, item):
        place = self.place
        goal = self.goals[index]
        sign = 2 * (goal > place.far).astype(jnp.int32) - 1
        ends = ((goal - place.far) * sign == 1).astype(jnp.int32)
        slot = goal + ends * (place.depth + (1 - sign) // 2 - goal)
        return remote(
            self.partial.at[self.spot(goal, *self.item(item)), :], self.into(slot, item),
            self.zsend.at[index, item], self.zrecv.at[slot, item], place.me + sign * NEAR, place.tensor,
        )

    def arrived(self, index, cut):
        number = index * len(self.cuts) + cut
        self.over(number).wait_recv()
        self.cross(number + len(self.cuts))
        start, size = self.cuts[cut]
        return self.over_in.at[index, pl.ds(start, size), :]

    def pass_on(self, index, item):
        place = self.place
        goal = self.goals[index]
        up = goal > place.far
        fed = (up & (place.far > 0)) | (jnp.logical_not(up) & (place.far < place.depth - 1))
        spot = self.spot(goal, *self.item(item))
        base = [self.arrived(index, item)] if item < 2 else []

        @pl.when(fed)
        def _():
            self.add(spot, base + [self.wait_far(goal, item)])

        if base:

            @pl.when(jnp.logical_not(fed))
            def _():
                self.add(spot, base)

        self.hop(index, item).start()
        self.sent.append(lambda: self.hop(index, item))

    def close(self, item):
        place = self.place
        spot = self.spot(place.far, *self.item(item))
        for way, comes in enumerate((place.far > 0, place.far < place.depth - 1)):

            @pl.when(comes)
            def _(way=way):
                self.add(spot, [self.wait_far(place.depth + way, item)])

    def last(self):
        place = self.place
        return remote(
            self.partial.at[self.spot(place.far, True, *self.tail), :], self.late_in,
            self.lsend, self.lrecv, place.beside, place.tensor,
        )

    def steps(self):
        place = self.place
        for index in range(place.depth - 1):
            if self.late:
                self.pass_on(index, 2)
                self.pass_on(index, 3)
                yield
            for cut in range(len(self.cuts)):
                self.pass_on(index, cut)
                yield
        if self.late:
            self.close(3)
            self.last().start()
            self.sent.append(self.last)
            self.close(2)
            yield
        for cut, (start, size) in enumerate(self.cuts):
            own = self.spot(place.far, 0, start, size)
            self.add(own, [self.arrived(place.depth - 1, cut)])
            self.close(cut)
            self.result[pl.ds(start, size), :] = self.partial[own, :].astype(F32)
            yield
        if self.late:
            start, size = self.tail
            self.last().wait_recv()
            self.result[pl.ds(start, size), :] = (
                self.partial[self.spot(place.far, 0, start, size), :].astype(F32) + self.late_in[...].astype(F32)
            )
            yield

    def settle(self):
        for make in self.sent:
            make().wait_send()


def mlp_kernel(count, share, *refs):
    (
        n2_hbm, cot_hbm, gates_hbm, pack_down,
        first_out, second_out, dn2_out, part_out, down_ref,
        n2_ref, cot_ref, dn2_part, dn2_ref, w1, w2, ab, hid, partial, near, chip, far, sum_sems, copy_sems, *rest,
    ) = refs
    place = Place(count)
    seq, width = n2_ref.shape
    both = w1.shape[1]
    even = both // (2 * LANES)
    split = first_out.shape[1]
    tile = seq // 4
    lanes = lane_ids()
    loads = [
        begin(src, dst, copy_sems.at[index])
        for index, (src, dst) in enumerate(((n2_hbm, n2_ref), (gates_hbm, w1), (cot_hbm, cot_ref)))
    ]
    place.greet(False, True)
    late = late_share(pack_down.shape[0], share)
    gather = Gather(place, pack_down, w2, late, rest[:5])
    scatter = Scatter(place, partial, down_ref, late, rest[5:])
    summed = TensorSum(place, dn2_part, dn2_ref, 4, (near, chip, far, sum_sems))
    gather.start()
    moves, sums, tensor = gather.steps(), scatter.steps(), summed.steps()
    loads[0].wait()
    loads[1].wait()

    def gate_up(index):
        cols = pl.ds(pl.multiple_of(index * 2 * LANES, 2 * LANES), 2 * LANES)
        got = dot_nn(n2_ref[...], w1[:, cols])
        gate, up = got[:, :LANES], got[:, LANES:]
        sig = jax.nn.sigmoid(gate)
        act = gate * sig
        hid[:, pl.ds(pl.multiple_of(index * LANES, LANES), LANES)] = (act * up).astype(BF16)
        slope = up * sig * (1.0 + gate * (1.0 - sig))
        ab[:, cols] = jnp.concatenate([slope, act], axis=1).astype(BF16)

    polled(even, gate_up, (moves, {8: 1, 12: 1}))
    tail = pl.ds(2 * even * LANES, LANES)
    got = dot_nn(n2_ref[...], w1[:, tail])
    up = pltpu.roll(got, HALF, 1)
    sig = jax.nn.sigmoid(got)
    act = got * sig
    hid[:, pl.ds(even * LANES, LANES)] = jnp.where(lanes < HALF, act * up, 0.0).astype(BF16)
    slope = up * sig * (1.0 + got * (1.0 - sig))
    ab[:, tail] = jnp.where(lanes < HALF, slope, pltpu.roll(act, HALF, 1)).astype(BF16)
    loads[2].wait()

    def down_grad(index):
        rows = pl.ds(pl.multiple_of(index * 384, 384), 384)
        partial[rows, :] = dot_tn(cot_ref[:, rows], hid[...]).astype(BF16)

    polled(width // 384, down_grad, (moves, {1: 1, 3: 1}))
    scatter.start()
    drain(moves)
    ahead(sums, 3)
    gather.finish()

    def inner_grad(index):
        got = dot_nn(cot_ref[...], w2[:, pl.ds(pl.multiple_of(index * 2 * LANES, 2 * LANES), 2 * LANES)])
        for side in range(2):
            piece = got[:, side * LANES : (side + 1) * LANES]
            cols = pl.ds(pl.multiple_of(index * 4 * LANES + side * 2 * LANES, 2 * LANES), 2 * LANES)
            ab[:, cols] = (ab[:, cols].astype(F32) * jnp.concatenate([piece, piece], axis=1)).astype(BF16)

    polled(even // 2, inner_grad, (sums, {2: 1, 5: 1}))
    got = dot_nn(cot_ref[...], w2[:, pl.ds((even - 1) * LANES, 2 * LANES)])
    piece = got[:, :LANES]
    cols = pl.ds(2 * (even - 1) * LANES, 2 * LANES)
    ab[:, cols] = (ab[:, cols].astype(F32) * jnp.concatenate([piece, piece], axis=1)).astype(BF16)
    piece = got[:, LANES:]
    piece = jnp.where(lanes < HALF, piece, pltpu.roll(piece, HALF, 1))
    ab[:, tail] = (ab[:, tail].astype(F32) * piece).astype(BF16)

    def normed_grad(index):
        rows = pl.ds(pl.multiple_of(index * tile, tile), tile)
        dn2_part[rows, :] = dot_nt(ab[rows, :], w1[...]).astype(BF16)
        for at in range(4):

            @pl.when(index == at)
            def _(at=at):
                summed.send_core(at)
                if at:
                    ahead(sums, 1)
                    ahead(tensor, 1)

    lax.fori_loop(0, 4, lambda index, carry: (normed_grad(index), carry)[1], 0)

    def output_part(index):
        rows = pl.ds(pl.multiple_of(index * 256, 256), 256)
        cot_ref[:, rows] = dot_nt(hid[...], w2[rows, :]).astype(BF16)

    polled(width // 256, output_part, (sums, {2: 1, 5: 1}), (tensor, {5: 1}))
    saves = [begin(cot_ref, part_out, copy_sems.at[4])]

    def gates_grad(index):
        rows = pl.ds(pl.multiple_of(index * 384, 384), 384)
        for low, high in ((0, split), (split, both)):
            w1[rows, pl.ds(low, high - low)] = dot_tn(n2_ref[:, rows], ab[:, pl.ds(low, high - low)]).astype(BF16)

    polled(width // 384, gates_grad, (sums, every(4)), (tensor, {1: 1, 3: 1}))
    saves.append(begin(w1.at[:, pl.ds(0, split)], first_out, copy_sems.at[5]))
    saves.append(begin(w1.at[:, pl.ds(split, both - split)], second_out, copy_sems.at[6]))
    drain(tensor, sums)
    for index in range(4):
        summed.finish(index)
    saves.append(begin(dn2_ref, dn2_out, copy_sems.at[3]))
    for save in saves:
        save.wait()
    gather.settle()
    scatter.settle()
    summed.settle()


def mlp_call(count, n2, cot, full_gates, pack_down, share=1 / 6):
    seq, width = n2.shape
    rows, down = pack_down.shape
    both = full_gates.shape[1]
    split = 14 * LANES
    shape = jax.ShapeDtypeStruct
    dma = pltpu.SemaphoreType.DMA
    return pl.pallas_call(
        functools.partial(mlp_kernel, count, share),
        out_shape=[
            shape((width, split), BF16),
            shape((width, both - split), BF16),
            shape((seq, width), BF16),
            shape((seq, width), BF16),
            shape((rows, down), F32),
        ],
        in_specs=[in_place()] * 4,
        out_specs=[in_place()] * 4 + [whole_block()],
        scratch_shapes=[
            *[pltpu.VMEM((seq, width), BF16)] * 4,
            pltpu.VMEM((width, both), BF16),
            pltpu.VMEM((width, down), BF16),
            pltpu.VMEM((seq, both), BF16),
            pltpu.VMEM((seq, down), BF16),
            pltpu.VMEM((width, down), BF16),
            *TensorSum.scratch(seq, width, 4, BF16),
            dma((7,)),
            *Gather.sems(count),
            *Scatter.scratch(count, rows, down, late_share(rows, share)),
        ],
        compiler_params=pltpu.CompilerParams(
            collective_id=2, has_side_effects=True, vmem_limit_bytes=61 << 20
        ),
    )(n2, cot, full_gates, pack_down)


def middle_kernel(count, *refs):
    (
        part_in, dn2_hbm, h_hbm, cot_hbm, w0_hbm, ctx_hbm, gain_ref,
        dh_out, dm_out, dwo_out, gates_ref, small_ref,
        partial, dn2_ref, h_ref, cot_ref, wo, ctx_ref, dh_ref, dm_ref, dwo_ref, dhb, copy_sems, *rest,
    ) = refs
    place = Place(count)
    seq, width = dn2_ref.shape
    q_cols = ctx_ref.shape[1]
    heads = q_cols // HALF
    group = heads // 2
    tile = seq // 4
    lanes = lane_ids()
    loads = [
        begin(src, dst, copy_sems.at[index])
        for index, (src, dst) in enumerate(
            (
                (part_in, partial), (dn2_hbm, dn2_ref), (h_hbm, h_ref), (cot_hbm, cot_ref),
                (w0_hbm.at[:, pl.ds(w0_hbm.shape[1] - q_cols, q_cols)], wo), (ctx_hbm, ctx_ref),
            )
        )
    ]
    place.greet(False, False)
    scatter = Scatter(place, partial, gates_ref, late_share(gates_ref.shape[0], 1 / 6), rest)
    loads[0].wait()
    scatter.start()
    sums = scatter.steps()
    g2 = gain_ref[pl.ds(1, 1), :]
    for load in loads[1:]:
        load.wait()
    small_ref[...] = jnp.zeros_like(small_ref)

    def residual_grad(index, carry):
        rows = pl.ds(pl.multiple_of(index * 64, 64), 64)
        grad = dn2_ref[rows, :].astype(F32)
        h = h_ref[rows, :]
        inverse = lax.rsqrt(jnp.mean(h * h, axis=1, keepdims=True) + EPSILON)
        scaled = grad * g2
        inner = jnp.mean(scaled * h, axis=1, keepdims=True)
        dh = cot_ref[rows, :].astype(F32) + inverse * scaled - h * (inverse * inverse * inverse * inner)
        dh_ref[rows, :] = dh
        dhb[rows, :] = dh.astype(BF16)
        return carry + jnp.sum((grad * h * inverse).reshape(8, 8, width), axis=0)

    def back(index):
        small_ref[...] += lax.fori_loop(
            index * (tile // 64), (index + 1) * (tile // 64), residual_grad, jnp.zeros((8, width), F32)
        )
        rows = pl.ds(pl.multiple_of(index * tile, tile), tile)
        dctx = dot_nn(dhb[rows, :], wo[...])
        for pair in range(heads // 2):
            value = dctx[:, pair * LANES : (pair + 1) * LANES]
            swapped = pltpu.roll(value, HALF, 1)
            for side in range(2):
                head = 2 * pair + side
                keep = value if side == head // group else swapped
                dm_ref[head, rows, :] = jnp.where(lanes // HALF == head // group, keep, 0.0).astype(BF16)

    polled(4, back, (sums, {1: 1, 2: 1, 3: 1}))
    saves = [begin(dh_ref, dh_out, copy_sems.at[6]), begin(dm_ref, dm_out, copy_sems.at[7])]

    def out_grad(index):
        rows = pl.ds(pl.multiple_of(index * 384, 384), 384)
        dwo_ref[rows, :] = dot_tn(dhb[:, rows], ctx_ref[...]).astype(BF16)

    polled(width // 384, out_grad, (sums, {1: 1, 3: 1}))
    saves.append(begin(dwo_ref, dwo_out, copy_sems.at[8]))
    drain(sums)
    for save in saves:
        save.wait()
    scatter.settle()


def middle_call(count, part, dn2, h, cot, w0, ctx, gains):
    seq, width = dn2.shape
    q_cols = ctx.shape[1]
    rows = width // count
    shape = jax.ShapeDtypeStruct
    dma = pltpu.SemaphoreType.DMA
    return pl.pallas_call(
        functools.partial(middle_kernel, count),
        out_shape=[
            shape((seq, width), F32),
            shape((q_cols // HALF, seq, LANES), BF16),
            shape((width, q_cols), BF16),
            shape((rows, part.shape[1]), F32),
            shape((8, width), F32),
        ],
        in_specs=[in_place()] * 6 + [whole_block()],
        out_specs=[in_place()] * 3 + [whole_block()] * 2,
        scratch_shapes=[
            pltpu.VMEM(part.shape, BF16),
            pltpu.VMEM((seq, width), BF16),
            pltpu.VMEM((seq, width), F32),
            pltpu.VMEM((seq, width), BF16),
            pltpu.VMEM((width, q_cols), BF16),
            pltpu.VMEM((seq, q_cols), BF16),
            pltpu.VMEM((seq, width), F32),
            pltpu.VMEM((q_cols // HALF, seq, LANES), BF16),
            pltpu.VMEM((width, q_cols), BF16),
            pltpu.VMEM((seq, width), BF16),
            dma((9,)),
            *Scatter.scratch(count, rows, part.shape[1], late_share(rows, 1 / 6)),
        ],
        compiler_params=pltpu.CompilerParams(
            collective_id=3, has_side_effects=True, vmem_limit_bytes=61 << 20
        ),
    )(part, dn2, h, cot, w0, ctx, gains)


def last_kernel(count, *refs):
    (
        part_in, dwo_in, dm_hbm, qm_hbm, kb_hbm, vb_hbm, lse_hbm, qk_hbm, n1_hbm, w0_hbm, x_hbm, dh_hbm,
        cos_ref, sin_ref, seg_col, seg_row, gain_ref, two_ref,
        grad_out, gates_ref, out_ref, qkv_ref, small_ref,
        partial, partial_o, dm_ref, qm_ref, kb_ref, vb_ref, lse_ref, qk_ref, n1_ref, wqkv, x_ref, dh_ref,
        partial_qkv, bias, dk, dv, dlow, part, dn1_ref, small, slots, head_slots,
        near, chip, far, sum_sems, small_send, small_recv, copy_sems, *rest,
    ) = refs
    place = Place(count)
    seq, width = n1_ref.shape
    kv_cols = kb_ref.shape[1]
    q_cols = qk_ref.shape[1] - kv_cols
    pairs = q_cols // LANES
    group = (q_cols // HALF) // (kv_cols // HALF)
    tile = seq // 4
    quarter = width // 4
    lanes = lane_ids()
    sources = (
        (part_in, partial), (dwo_in, partial_o), (qm_hbm, qm_ref), (kb_hbm, kb_ref), (lse_hbm, lse_ref),
        (dm_hbm, dm_ref), (vb_hbm, vb_ref), (qk_hbm, qk_ref),
        (w0_hbm.at[:, pl.ds(0, wqkv.shape[1])], wqkv), (n1_hbm, n1_ref), (x_hbm, x_ref), (dh_hbm, dh_ref),
    )
    loads = [begin(src, dst, copy_sems.at[index]) for index, (src, dst) in enumerate(sources)]
    place.greet(True, True)
    third = len(rest) // 3
    late = late_share(gates_ref.shape[0], 1 / 6)
    scatter = Scatter(place, partial, gates_ref, late, rest[:third])
    scatter_o = Scatter(place, partial_o, out_ref, late, rest[third : 2 * third])
    scatter_qkv = Scatter(place, partial_qkv, qkv_ref, late, rest[2 * third :])
    final = TensorSum(place, part, dn1_ref, 4, (near, chip, far, sum_sems))
    for load in loads[:2]:
        load.wait()
    scatter.start()
    sums, sums_o = scatter.steps(), scatter_o.steps()
    dk[...] = jnp.zeros_like(dk)
    dv[...] = jnp.zeros_like(dv)
    gq = gain_ref[pl.ds(2, 1), pl.ds(0, LANES)]
    gk = gain_ref[pl.ds(3, 1), pl.ds(0, LANES)]
    for load in loads[2:9]:
        load.wait()

    def head_back(grad, raw, cosine, sine, gain):
        back = turn(grad, cosine, -sine)
        inverse = lax.rsqrt(head_mean(raw * raw) + EPSILON)
        scaled = back * gain
        inner = head_mean(scaled * raw)
        low = inverse * scaled - raw * (inverse * inverse * inverse * inner)
        return low.astype(BF16), jnp.sum((back * raw * inverse).reshape(-1, 8, LANES), axis=0)

    gain_q = jnp.zeros((8, LANES), F32)
    gain_k = jnp.zeros((8, LANES), F32)
    for qb in reversed(range(4)):
        last = (qb + 1) * tile
        rows = pl.ds(qb * tile, tile)
        bias_block(seg_col, seg_row, bias, qb * tile, tile)

        def attend_back(pair, carry, last=last, rows=rows):
            keys = pl.ds(0, last)
            sides = []
            for side in range(2):
                head = 2 * pair + side
                kv = head // group
                query, grad = qm_ref[head, rows, :], dm_ref[head, rows, :]
                logsum = jnp.sum(jnp.where(lanes == head, lse_ref[rows, :], 0.0), axis=1, keepdims=True)
                logits = dot_nt(query, kb_ref[keys, :]) + bias[:, keys]
                probs = jnp.exp(logits - logsum)
                dprob = dot_nt(grad, vb_ref[keys, :])
                inner = jnp.sum(probs * dprob, axis=1, keepdims=True)
                ds = (probs * (dprob - inner)).astype(BF16)
                got = dot_nn(ds, kb_ref[keys, :]) * 0.125
                sides.append(jnp.where(kv == side, got, pltpu.roll(got, HALF, 1)))
                dk[keys, :] += dot_tn(ds, query)
                dv[keys, :] += dot_tn(probs.astype(BF16), grad)
            cols = pl.ds(pl.multiple_of(pair * LANES, LANES), LANES)
            low, terms = head_back(
                jnp.where(lanes < HALF, sides[0], sides[1]), qk_ref[rows, cols], cos_ref[rows, :], sin_ref[rows, :], gq
            )
            dlow[rows, cols] = low
            return carry + terms

        gain_q = lax.fori_loop(0, pairs, attend_back, gain_q)
        low, terms = head_back(
            dk[rows, :], qk_ref[rows, pl.ds(q_cols, LANES)], cos_ref[rows, :], sin_ref[rows, :], gk
        )
        dlow[rows, pl.ds(q_cols, LANES)] = low
        dlow[rows, pl.ds(q_cols + LANES, LANES)] = dv[rows, :].astype(BF16)
        gain_k = gain_k + terms
        part[rows, :] = dot_nt(dlow[rows, :], wqkv[...]).astype(BF16)
        final.send_core(qb)
        ahead(sums, 3)
        final.send_across(qb)
        if qb < 3:
            final.send_back(qb + 1)
        if qb == 1:
            scatter_o.start()
    mine = head_slots.at[place.tensor]
    mine[...] = jnp.concatenate([gain_q, gain_k], axis=0)
    head_copies = []
    for step in range(1, 4):
        copy = remote(
            mine, mine, small_send.at[step - 1], small_recv.at[step - 1], place.me, lax.rem(place.tensor + step, 4)
        )
        copy.start()
        head_copies.append(copy)
    for load in loads[9:]:
        load.wait()

    def qkv_grad(start):
        partial_qkv[pl.ds(start, 384), :] = dot_tn(n1_ref[:, pl.ds(start, 384)], dlow[...]).astype(BF16)

    blocks(width, 384, qkv_grad)
    scatter_qkv.start()
    sums_qkv = scatter_qkv.steps()
    for step, copy in enumerate(head_copies):
        whose = head_slots.at[lax.rem(place.tensor + 3 - step, 4)]
        remote(whose, whose, small_send.at[step], small_recv.at[step], place.me, place.tensor).wait_recv()
    heads = head_slots[0] + head_slots[1] + head_slots[2] + head_slots[3]
    ahead(sums_o, 2)
    g1 = gain_ref[pl.ds(0, 1), :]
    gain_one = jnp.zeros((8, width), F32)
    saves = []
    for index in reversed(range(4)):
        if index == 0:
            final.send_back(0)
        ahead(sums, 1)
        ahead(sums_o, 1)
        ahead(sums_qkv, 1)
        final.finish(index)

        def input_grad(sub, carry, index=index):
            rows = pl.ds(pl.multiple_of(index * tile + sub * 64, 64), 64)
            grad = dn1_ref[rows, :].astype(F32)
            x = x_ref[rows, :].astype(F32)
            inverse = lax.rsqrt(jnp.mean(x * x, axis=1, keepdims=True) + EPSILON)
            scaled = grad * g1
            inner = jnp.mean(scaled * x, axis=1, keepdims=True)
            dh_ref[rows, :] = dh_ref[rows, :] + inverse * scaled - x * (inverse * inverse * inverse * inner)
            return carry + jnp.sum((grad * x * inverse).reshape(8, 8, width), axis=0)

        gain_one = lax.fori_loop(0, tile // 64, input_grad, gain_one)
        rows = pl.ds(index * tile, tile)
        saves.append(begin(dh_ref.at[rows, :], grad_out.at[rows, :], copy_sems.at[index]))
    one = jnp.sum(gain_one, axis=0, keepdims=True)
    two = jnp.sum(two_ref[...], axis=0, keepdims=True)
    small[...] = jnp.zeros_like(small)
    for index in range(4):
        cols = slice(index * quarter, (index + 1) * quarter)
        small[pl.ds(index, 1), pl.ds(0, quarter)] = one[:, cols]
        small[pl.ds(4 + index, 1), pl.ds(0, quarter)] = two[:, cols]
    small[pl.ds(0, 1), pl.ds(quarter, LANES)] = jnp.sum(heads[:8], axis=0, keepdims=True)
    small[pl.ds(1, 1), pl.ds(quarter, LANES)] = jnp.sum(heads[8:], axis=0, keepdims=True)
    small_copies = []
    for step in range(1, count):
        copy = remote(
            small, slots.at[step], small_send.at[2 + step], small_recv.at[2 + step],
            lax.rem(place.me + step, count), place.tensor,
        )
        copy.start()
        small_copies.append(copy)
    drain(sums, sums_o, sums_qkv)
    total = small[...]
    for copy in small_copies:
        copy.wait_recv()
    for step in range(1, count):
        total = total + slots[step]
    small_ref[...] = total
    for save in saves:
        save.wait()
    for copy in head_copies + small_copies:
        copy.wait_send()
    for each in (scatter, scatter_o, scatter_qkv, final):
        each.settle()


def last_call(count, part, dwo, dm, qm, kb, vb, lse, qk, n1, w0, x, dh, cosine, sine, seg_col, seg_row, gains, two):
    seq, width = n1.shape
    rows = width // count
    q_cols = dwo.shape[1]
    low = qk.shape[1] + LANES
    shape = jax.ShapeDtypeStruct
    dma = pltpu.SemaphoreType.DMA
    loaded = [part, dwo, dm, qm, kb, vb, lse, qk, n1, jax.ShapeDtypeStruct((width, low), BF16), x, dh]
    small = (8, width // 4 + LANES)
    return pl.pallas_call(
        functools.partial(last_kernel, count),
        out_shape=[
            shape((seq, width), F32),
            shape((rows, part.shape[1]), F32),
            shape((rows, q_cols), F32),
            shape((rows, low), F32),
            shape(small, F32),
        ],
        in_specs=[in_place()] * 12 + [whole_block()] * 6,
        out_specs=[in_place()] + [whole_block()] * 4,
        scratch_shapes=[
            *[pltpu.VMEM(one.shape, one.dtype) for one in loaded],
            pltpu.VMEM((width, low), BF16),
            pltpu.VMEM((seq // 4, seq), F32),
            pltpu.VMEM((seq, LANES), F32),
            pltpu.VMEM((seq, LANES), F32),
            pltpu.VMEM((seq, low), BF16),
            pltpu.VMEM((seq, width), BF16),
            pltpu.VMEM((seq, width), BF16),
            pltpu.VMEM(small, F32),
            pltpu.VMEM((count,) + small, F32),
            pltpu.VMEM((4, 16, LANES), F32),
            *TensorSum.scratch(seq, width, 4, BF16),
            dma((count + 2,)),
            dma((count + 2,)),
            dma((12,)),
            *Scatter.scratch(count, rows, part.shape[1], late_share(rows, 1 / 6)),
            *Scatter.scratch(count, rows, q_cols, late_share(rows, 1 / 6)),
            *Scatter.scratch(count, rows, low, late_share(rows, 1 / 6)),
        ],
        compiler_params=pltpu.CompilerParams(
            collective_id=4, has_side_effects=True, vmem_limit_bytes=61 << 20
        ),
    )(part, dwo, dm, qm, kb, vb, lse, qk, n1, w0, x, dh, cosine, sine, seg_col, seg_row, gains, two)


def rotation_tables(positions, head_dim):
    half_dim = head_dim // 2
    frequency = ROPE_BASE ** (-jnp.arange(half_dim, dtype=jnp.float32) * 2.0 / head_dim)
    angles = positions.astype(jnp.float32)[:, None] * frequency[None, :]
    return (jnp.cos(angles)[:, None, :], jnp.sin(angles)[:, None, :])


def lay(gate, up):
    rows, cols = gate.shape
    even = cols // LANES * LANES
    pairs = jnp.stack(
        [gate[:, :even].reshape(rows, -1, LANES), up[:, :even].reshape(rows, -1, LANES)], axis=2
    ).reshape(rows, 2 * even)
    return jnp.concatenate([pairs, gate[:, even:], up[:, even:]], axis=1)


def unlay(both):
    rows, cols = both.shape
    even = cols // 2 // LANES * LANES
    pairs = both[:, : 2 * even].reshape(rows, -1, 2, LANES)
    rest = both[:, 2 * even :]
    size = rest.shape[1] // 2
    return (
        jnp.concatenate([pairs[:, :, 0].reshape(rows, even), rest[:, :size]], axis=1),
        jnp.concatenate([pairs[:, :, 1].reshape(rows, even), rest[:, size:]], axis=1),
    )


def spread(gain, me, width):
    full = jnp.zeros((width,), F32)
    return lax.dynamic_update_slice(full, lax.reduce_precision(gain, 8, 7), (me * gain.shape[0],))


def gain_rows(norm1_gain, norm2_gain, q_gain, k_gain, count):
    me = lax.axis_index("dp")
    width = norm1_gain.shape[0] * count
    head = q_gain.shape[0] * count
    rows = [spread(norm1_gain, me, width), spread(norm2_gain, me, width)]
    for gain in (q_gain, k_gain):
        one = spread(gain, me, head)
        rows.append(jnp.pad(jnp.concatenate([one, one]), (0, width - 2 * head)))
    return jnp.pad(jnp.stack(rows), ((0, 4), (0, 0)))


def rotation_lanes(positions):
    cosine, sine = rotation_tables(positions, HALF)
    cosine, sine = cosine[:, 0], sine[:, 0]
    return (
        jnp.concatenate([cosine] * 4, axis=1),
        jnp.concatenate([-sine, sine, -sine, sine], axis=1),
    )


def shards(
    block_input,
    segments,
    positions,
    norm1_gain,
    q_norm_gain,
    k_norm_gain,
    w_q,
    w_k,
    w_v,
    w_o,
    norm2_gain,
    w_gate,
    w_up,
    w_down,
    cotangent,
    *,
    n_dp,
    n_tensor,
):
    rows = w_q.shape[0]
    q_cols, kv_cols, ff_cols = w_q.shape[1], w_k.shape[1], w_gate.shape[1]
    small_gain = q_norm_gain.shape[0]
    head_dim = small_gain * n_dp
    seg_col, seg_row = segments[:, None], segments[None, :]
    gains = gain_rows(norm1_gain, norm2_gain, q_norm_gain, k_norm_gain, n_dp)
    pack_attn = jnp.concatenate(
        [w_q.astype(BF16), w_k.astype(BF16), w_v.astype(BF16), w_o.T.astype(BF16)], axis=1
    )
    pack_gates = lay(w_gate.astype(BF16), w_up.astype(BF16))
    pack_down = jnp.pad(w_down.T.astype(BF16), ((0, 0), (0, -ff_cols % LANES)))
    cosine, sine = rotation_lanes(positions)
    w0, w1, n1, qk, qm, kb, vb, lse, ctx, h, n2, gains = forward_call(
        n_dp, block_input, seg_col, seg_row, cosine, sine, gains, pack_attn, pack_gates
    )
    first, second, dn2, mlp, down = mlp_call(n_dp, n2, cotangent, w1, pack_down)
    mlp_total = lax.psum(mlp, "tensor")
    dh, dm, dwo, gates_one, small_two = middle_call(n_dp, first, dn2, h, cotangent, w0, ctx, gains)
    grad_input, gates_two, grad_o, grad_qkv, small = last_call(
        n_dp, second, dwo, dm, qm, kb, vb, lse, qk, n1, w0, block_input, dh,
        cosine, sine, seg_col, seg_row, gains, small_two,
    )
    output_rows = (h + mlp_total.astype(F32)).astype(BF16)
    me = lax.axis_index("dp")
    quarter = block_input.shape[1] // 4
    one, two = small[:4, :quarter].reshape(-1), small[4:, :quarter].reshape(-1)
    heads = small[:2, quarter:].reshape(2, 2, head_dim).sum(axis=1)

    def own(values, size):
        return lax.dynamic_slice_in_dim(values, me * size, size, 0)

    grad_gate, grad_up = unlay(jnp.concatenate([gates_one, gates_two], axis=1))
    return (
        output_rows,
        grad_input,
        own(one, rows),
        own(heads[0], small_gain),
        own(heads[1], small_gain),
        grad_qkv[:, :q_cols],
        grad_qkv[:, q_cols : q_cols + kv_cols],
        grad_qkv[:, q_cols + kv_cols :],
        grad_o.T,
        own(two, rows),
        grad_gate,
        grad_up,
        down[:, :ff_cols].T,
    )


def solution(mesh):
    placed = (
        P("dp", None),
        P("dp"),
        P("dp"),
        P("dp"),
        P("dp"),
        P("dp"),
        P("dp", "tensor"),
        P("dp", "tensor"),
        P("dp", "tensor"),
        P("tensor", "dp"),
        P("dp"),
        P("dp", "tensor"),
        P("dp", "tensor"),
        P("tensor", "dp"),
        P("dp", None),
    )
    return jax.shard_map(
        functools.partial(shards, n_dp=mesh.shape["dp"], n_tensor=mesh.shape["tensor"]),
        mesh=mesh,
        in_specs=placed,
        out_specs=(
            P("dp", None),
            P("dp", None),
            P("dp"),
            P("dp"),
            P("dp"),
            P("dp", "tensor"),
            P("dp", "tensor"),
            P("dp", "tensor"),
            P("tensor", "dp"),
            P("dp"),
            P("dp", "tensor"),
            P("dp", "tensor"),
            P("tensor", "dp"),
        ),
        check_vma=False,
    )
```

```python
import functools

import jax
import jax.numpy as jnp
import numpy as np
from jax import lax
from jax.experimental import pallas as pl
from jax.experimental.pallas import tpu as pltpu
from jax.sharding import PartitionSpec as P

EPSILON = 1e-05
ROPE_BASE = 1000000.0
MASKED = -1e30


MESH = pl.DeviceIdType.MESH
NEAR = 2
HALF = 64
LANES = 128
HIGHEST = lax.Precision.HIGHEST
BF16 = jnp.bfloat16
F32 = jnp.float32


def whole_block():
    return pl.BlockSpec(memory_space=pltpu.VMEM)


def in_place():
    return pl.BlockSpec(memory_space=pl.ANY)


def remote(src, dst, send, recv, dp, tensor):
    return pltpu.make_async_remote_copy(
        src_ref=src,
        dst_ref=dst,
        send_sem=send,
        recv_sem=recv,
        device_id=(dp, tensor),
        device_id_type=MESH,
    )


def begin(src, dst, sem):
    copy = pltpu.make_async_copy(src, dst, sem)
    copy.start()
    return copy


def dot_nn(left, right):
    return jnp.dot(left, right, preferred_element_type=F32)


def dot_nt(left, right):
    return lax.dot_general(left, right, (((1,), (1,)), ((), ())), preferred_element_type=F32)


def dot_tn(left, right):
    return lax.dot_general(left, right, (((0,), (0,)), ((), ())), preferred_element_type=F32)


class Place:
    def __init__(self, count):
        self.count = count
        self.depth = count // NEAR
        self.me = lax.axis_index("dp")
        self.tensor = lax.axis_index("tensor")
        self.far = self.me // NEAR
        self.near = lax.rem(self.me, NEAR)
        self.core = lax.rem(self.tensor, 2)
        self.mate = self.tensor + 1 - 2 * self.core
        self.across = lax.rem(self.tensor + 2, 4)
        self.beside = self.me + 1 - 2 * self.near

    def ahead(self, step):
        return lax.rem(self.far + step, self.depth)

    def behind(self, step):
        return lax.rem(self.far + self.depth - step, self.depth)

    def greet(self, everyone, tensor):
        barrier = pltpu.get_barrier_semaphore()
        peers = []
        if everyone:
            peers += [(lax.rem(self.me + d, self.count), self.tensor) for d in range(1, self.count)]
        else:
            peers += [
                (self.ahead(step) * NEAR + self.near, self.tensor) for step in range(1, self.depth)
            ]
            peers.append((self.beside, self.tensor))
        if tensor:
            peers += [(self.me, lax.rem(self.tensor + t, 4)) for t in range(1, 4)]
        for peer in peers:
            pl.semaphore_signal(barrier, 1, device_id=peer, device_id_type=MESH)
        pl.semaphore_wait(barrier, len(peers))


class Gather:
    def __init__(self, place, shard, full, late, sems):
        self.place, self.shard, self.full = place, shard, full
        self.rows = shard.shape[0]
        self.cuts = [(0, self.rows - late)] + ([(self.rows - late, late)] if late else [])
        self.zsend, self.zrecv, self.ysend, self.yrecv, self.own = sems
        self.sent = []

    @staticmethod
    def sems(count):
        depth = count // NEAR
        dma = pltpu.SemaphoreType.DMA
        return [dma((2, depth - 1, 3)), dma((2, depth - 1, 3)), dma((2 * depth - 1, 2)), dma((2 * depth - 1, 2)), dma]

    def spot(self, block, cut):
        start, size = self.cuts[cut]
        return self.full.at[pl.ds(pl.multiple_of(block * self.rows + start, 16), size), :]

    def mine(self, cut):
        start, size = self.cuts[cut]
        return self.shard.at[pl.ds(start, size), :]

    def block(self, way, step, other):
        far = self.place.far - step if way == 0 else self.place.far + step
        return far * NEAR + (1 - self.place.near if other else self.place.near)

    def valid(self, way, step):
        return self.place.far >= step if way == 0 else self.place.far + step < self.place.depth

    def emit(self, make):
        copy, when = make()
        if when is None:
            copy.start()
        else:
            pl.when(when)(copy.start)
        self.sent.append(make)

    def along(self, way, step, cut, other):
        place = self.place
        if step >= place.depth - 1:
            return

        def make():
            more = place.far < place.depth - 1 if way == 0 else place.far > 0
            spot = self.spot(self.block(way, step, other), cut)
            copy = remote(
                self.mine(cut) if step == 0 and not other else spot, spot,
                self.zsend.at[way, step, cut + other], self.zrecv.at[way, step, cut + other],
                place.me + (NEAR if way == 0 else -NEAR), place.tensor,
            )
            return copy, more if step == 0 else more & self.valid(way, step)

        self.emit(make)

    def crossing(self, way, step, cut, other):
        place = self.place
        spot = self.spot(self.block(way, step, other), cut)
        slot = step if way == 0 else step + place.depth - 1
        return remote(
            self.mine(cut) if step == 0 and not other else spot, spot,
            self.ysend.at[slot, cut], self.yrecv.at[slot, cut], place.beside, place.tensor,
        ), (self.valid(way, step) if step else None)

    def over(self, way, step, cut):
        self.emit(lambda: self.crossing(way, step, cut, 0))

    def came_over(self, way, step, cut):
        copy, when = self.crossing(way, step, cut, 1)
        if when is None:
            copy.wait_recv()
        else:
            pl.when(when)(copy.wait_recv)

    def start(self):
        place = self.place
        self.local = lambda: pltpu.make_async_copy(
            self.shard, self.full.at[pl.ds(pl.multiple_of(place.me * self.rows, 16), self.rows), :], self.own
        )
        self.local().start()
        for cut in reversed(range(len(self.cuts))):
            self.over(0, 0, cut)
        for cut in range(len(self.cuts)):
            for way in range(2):
                self.along(way, 0, cut, 0)

    def steps(self):
        place = self.place
        if len(self.cuts) > 1:
            self.came_over(0, 0, 1)
            for way in range(2):
                self.along(way, 0, 1, 1)
            yield
        for step in range(1, place.depth):
            for cut in range(len(self.cuts)):
                for other in range(cut + 1):
                    for way in range(2):
                        spot = self.spot(self.block(way, step, other), cut)
                        copy = remote(
                            spot, spot, self.zsend.at[way, step - 1, cut + other],
                            self.zrecv.at[way, step - 1, cut + other], place.me, place.tensor,
                        )
                        pl.when(self.valid(way, step))(copy.wait_recv)
                        self.along(way, step, cut, other)
                        if cut == 0:
                            self.over(way, step, cut)
                    yield

    def finish(self):
        self.came_over(0, 0, 0)
        for step in range(1, self.place.depth):
            for way in range(2):
                self.came_over(way, step, 0)
        self.local().wait()

    def settle(self):
        for make in self.sent:
            copy, when = make()
            if when is None:
                copy.wait_send()
            else:
                pl.when(when)(copy.wait_send)


def late_share(rows, share):
    return int(rows * share) // 16 * 16


class TensorSum:
    def __init__(self, place, part, total, tiles, scratch):
        self.place, self.part, self.total, self.tiles = place, part, total, tiles
        self.tile = part.shape[0] // tiles
        self.half = self.tile // 2
        self.near, self.chip, self.far, self.sems = scratch
        self.sent = []

    @staticmethod
    def scratch(rows, width, tiles, kind):
        half = (rows // 2, width)
        return [
            pltpu.VMEM(half, kind), pltpu.VMEM(half, BF16), pltpu.VMEM(half, BF16), pltpu.SemaphoreType.DMA((6, tiles))
        ]

    def half_rows(self, index, which):
        return pl.ds(pl.multiple_of(index * self.tile + which * self.half, 16), self.half)

    def slot(self, index):
        return pl.ds(index * self.half, self.half)

    def core_copy(self, index):
        place = self.place
        return remote(
            self.part.at[self.half_rows(index, 1 - place.core), :], self.near.at[self.slot(index), :],
            self.sems.at[0, index], self.sems.at[1, index], place.me, place.mate,
        )

    def across_copy(self, index):
        place = self.place
        return remote(
            self.chip.at[self.slot(index), :], self.far.at[self.slot(index), :],
            self.sems.at[2, index], self.sems.at[3, index], place.me, place.across,
        )

    def back_copy(self, index, which):
        place = self.place
        rows = self.half_rows(index, which)
        return remote(
            self.total.at[rows, :], self.total.at[rows, :],
            self.sems.at[4, index], self.sems.at[5, index], place.me, place.mate,
        )

    def send_core(self, index):
        self.core_copy(index).start()
        self.sent.append(lambda: self.core_copy(index))

    def send_across(self, index):
        place = self.place
        self.core_copy(index).wait_recv()
        mine = self.part[self.half_rows(index, place.core), :].astype(F32)
        self.chip[self.slot(index), :] = (mine + self.near[self.slot(index), :].astype(F32)).astype(BF16)
        self.across_copy(index).start()
        self.sent.append(lambda: self.across_copy(index))

    def send_back(self, index):
        place = self.place
        self.across_copy(index).wait_recv()
        both = self.chip[self.slot(index), :].astype(F32) + self.far[self.slot(index), :].astype(F32)
        self.total[self.half_rows(index, place.core), :] = both.astype(self.total.dtype)
        self.back_copy(index, place.core).start()

    def finish(self, index):
        self.back_copy(index, 1 - self.place.core).wait_recv()
        self.back_copy(index, self.place.core).wait_send()

    def steps(self):
        for index in range(2):
            self.send_across(index)
            yield
        for index in range(self.tiles):
            self.send_back(index)
            if index + 2 < self.tiles:
                self.send_across(index + 2)
            yield

    def settle(self):
        for make in self.sent:
            make().wait_send()


def lane_ids(width=LANES):
    return lax.broadcasted_iota(jnp.int32, (1, width), 1)


def head_mean(values):
    row = lax.broadcasted_iota(jnp.int32, (LANES, LANES), 0)
    col = lax.broadcasted_iota(jnp.int32, (LANES, LANES), 1)
    groups = jnp.where(row // HALF == col // HALF, 1.0 / HALF, 0.0).astype(F32)
    return jnp.dot(values, groups, precision=HIGHEST, preferred_element_type=F32)


def turn(values, cosine, sine):
    ahead = pltpu.roll(values, LANES - HALF // 2, 1)
    back = pltpu.roll(values, HALF // 2, 1)
    first = lax.rem(lane_ids(), HALF) < HALF // 2
    return values * cosine + jnp.where(first, ahead, back) * sine


def bias_block(seg_col, seg_row, bias, first, tile):
    last = first + tile
    rows = lax.broadcasted_iota(jnp.int32, (tile, last), 0) + first
    cols = lax.broadcasted_iota(jnp.int32, (tile, last), 1)
    allowed = (seg_col[pl.ds(first, tile), :] == seg_row[:, pl.ds(0, last)]) & (rows >= cols)
    bias[:, pl.ds(0, last)] = jnp.where(allowed, 0.0, MASKED)


def drain(*moves):
    for one in moves:
        for _ in one:
            pass


def ahead(moves, count=1):
    for _ in range(count):
        next(moves, None)


def polled(count, body, *polls):
    def step(index, carry):
        body(index)
        for at in range(count):
            due = [(moves, times[at]) for moves, times in polls if at in times]
            if due:

                @pl.when(index == at)
                def _(due=due):
                    for moves, times in due:
                        ahead(moves, times)

        return carry

    lax.fori_loop(0, count, step, 0)


def every(count, times=1, first=0):
    return {index: times for index in range(first, count)}


def blocks(total, size, body):
    def step(index, carry):
        body(pl.multiple_of(index * size, size))
        return carry

    lax.fori_loop(0, total // size, step, 0)


def forward_kernel(count, *refs):
    (
        x_hbm, gate_hbm, up_hbm, seg_col, seg_row, cos_ref, sin_ref, gain_ref, wq_ref, wk_ref, wv_ref, wot_ref,
        full_attn, full_gates, n1_out, qk_out, qm_out, kb_out, vb_out, lse_out, ctx_out, h_out, n2_out, gains_out,
        x_ref, w0, n1_ref, qk_ref, qm_ref, kb_ref, vb_ref, lse_ref, ctx_ref, h_ref, n2_ref,
        pack_attn, pack_gates, gate_ref, up_ref, bias, gain_slots, part, total, tmp_near, tmp_chip, tmp_far, sum_sems, gain_send, gain_recv, copy_sems,
        *gather_sems,
    ) = refs
    place = Place(count)
    seq, width = x_ref.shape
    q_cols = ctx_ref.shape[1]
    kv_cols = kb_ref.shape[1]
    pairs = q_cols // LANES
    group = (q_cols // HALF) // (kv_cols // HALF)
    tile = seq // 4
    load = begin(x_hbm, x_ref, copy_sems.at[0])
    weights = [begin(gate_hbm, gate_ref, copy_sems.at[11]), begin(up_hbm, up_ref, copy_sems.at[12])]
    spot = 0
    for ref in (wq_ref, wk_ref, wv_ref, wot_ref):
        pack_attn[:, pl.ds(spot, ref.shape[1])] = ref[...].astype(BF16)
        spot += ref.shape[1]
    gain_slots[place.me] = gain_ref[...].astype(BF16).astype(F32)
    place.greet(True, True)
    first = Gather(place, pack_attn, w0, late_share(pack_attn.shape[0], 1 / 6), gather_sems[:5])
    second = Gather(place, pack_gates, full_gates, late_share(pack_gates.shape[0], 1 / 6), gather_sems[5:])
    first.start()
    gain_copies = []
    for step in range(1, count):
        copy = remote(
            gain_slots.at[place.me], gain_slots.at[place.me], gain_send.at[step], gain_recv.at[step],
            lax.rem(place.me + step, count), place.tensor,
        )
        copy.start()
        gain_copies.append(copy)
    for weight in weights:
        weight.wait()
    even = gate_ref.shape[1] // LANES

    def lay(index, carry):
        cols = pl.ds(pl.multiple_of(index * LANES, LANES), LANES)
        for side, ref in enumerate((gate_ref, up_ref)):
            spot = pl.multiple_of((2 * index + side) * LANES, LANES)
            pack_gates[:, pl.ds(spot, LANES)] = ref[:, cols].astype(BF16)
        return carry

    lax.fori_loop(0, even, lay, 0)
    rest = pl.ds(even * LANES, HALF)
    pack_gates[:, pl.ds(2 * even * LANES, LANES)] = jnp.concatenate(
        [gate_ref[:, rest], up_ref[:, rest]], axis=1
    ).astype(BF16)
    for qb in range(4):
        bias_block(seg_col, seg_row, bias.at[qb], qb * tile, tile)
    for step in range(1, count):
        whose = gain_slots.at[lax.rem(place.me + count - step, count)]
        remote(whose, whose, gain_send.at[step], gain_recv.at[step], place.me, place.tensor).wait_recv()
    gains_out[...] = jnp.zeros_like(gains_out)
    own = width // count
    for row in range(2):
        gains_out[pl.ds(row, 1), :] = jnp.concatenate(
            [gain_slots[d, pl.ds(row, 1), pl.ds(0, own)] for d in range(count)], axis=1
        )
    for row in range(2, 4):
        gains_out[pl.ds(row, 1), pl.ds(0, LANES)] = jnp.concatenate(
            [gain_slots[d, pl.ds(row, 1), pl.ds(0, HALF // count)] for d in range(count)] * 2, axis=1
        )
    moves_first = first.steps()
    ahead(moves_first, 2)
    g1 = gains_out[pl.ds(0, 1), :]
    g2 = gains_out[pl.ds(1, 1), :]
    load.wait()

    def norm_one(index, carry):
        rows = pl.ds(pl.multiple_of(index * LANES, LANES), LANES)
        x = x_ref[rows, :].astype(F32)
        inverse = lax.rsqrt(jnp.mean(x * x, axis=1, keepdims=True) + EPSILON)
        n1_ref[rows, :] = (x * inverse * g1).astype(BF16)
        return carry

    lax.fori_loop(0, seq // LANES, norm_one, 0)
    saves = [begin(n1_ref, n1_out, copy_sems.at[1])]
    drain(moves_first)
    second.start()
    moves = second.steps()
    first.finish()
    saves.append(begin(w0, full_attn, copy_sems.at[2]))
    gq = gains_out[pl.ds(2, 1), pl.ds(0, LANES)]
    gk = gains_out[pl.ds(3, 1), pl.ds(0, LANES)]
    lanes = lane_ids()

    def project(index, carry):
        rows = pl.ds(pl.multiple_of(index * tile, tile), tile)
        qkv = dot_nn(n1_ref[rows, :], w0[:, pl.ds(0, q_cols + 2 * kv_cols)])
        qk_ref[rows, :] = qkv[:, : q_cols + kv_cols]
        vb_ref[rows, :] = qkv[:, q_cols + kv_cols :].astype(BF16)
        cosine, sine = cos_ref[rows, :], sin_ref[rows, :]
        for pair in range(pairs + 1):
            raw = qkv[:, pair * LANES : (pair + 1) * LANES]
            inverse = lax.rsqrt(head_mean(raw * raw) + EPSILON)
            turned = turn(raw * inverse * (gk if pair == pairs else gq), cosine, sine)
            if pair == pairs:
                kb_ref[rows, :] = turned.astype(BF16)
                continue
            swapped = pltpu.roll(turned, HALF, 1)
            for side in range(2):
                head = 2 * pair + side
                kv = head // group
                keep = (turned if side == kv else swapped).astype(BF16) * 0.125
                qm_ref[head, rows, :] = jnp.where(lanes // HALF == kv, keep, jnp.zeros_like(keep))
        return carry

    lax.fori_loop(0, 4, project, 0)
    for index, (src, dst) in enumerate(((qk_ref, qk_out), (qm_ref, qm_out), (kb_ref, kb_out), (vb_ref, vb_out))):
        saves.append(begin(src, dst, copy_sems.at[3 + index]))
    next(moves, None)

    for qb in range(4):
        last = (qb + 1) * tile
        rows = pl.ds(qb * tile, tile)

        def attend(pair, carry, last=last, rows=rows, qb=qb):
            halves, sums = [], []
            for side in range(2):
                head = 2 * pair + side
                kv = head // group
                logits = dot_nt(qm_ref[head, rows, :], kb_ref[pl.ds(0, last), :]) + bias[qb, :, pl.ds(0, last)]
                top = jnp.max(logits, axis=1, keepdims=True)
                expo = jnp.exp(logits - top)
                summed = jnp.sum(expo, axis=1, keepdims=True)
                probs = (expo * (1.0 / summed)).astype(BF16)
                got = dot_nn(probs, vb_ref[pl.ds(0, last), :])
                halves.append(jnp.where(kv == side, got, pltpu.roll(got, HALF, 1)))
                sums.append(top + jnp.log(summed))
            ctx_ref[rows, pl.ds(pl.multiple_of(pair * LANES, LANES), LANES)] = jnp.where(
                lanes < HALF, halves[0], halves[1]
            ).astype(BF16)
            carry = jnp.where(lanes == 2 * pair, sums[0], carry)
            return jnp.where(lanes == 2 * pair + 1, sums[1], carry)

        lse_ref[rows, :] = lax.fori_loop(0, pairs, attend, jnp.zeros((tile, LANES), F32))
        next(moves, None)
    saves.append(begin(lse_ref, lse_out, copy_sems.at[7]))
    saves.append(begin(ctx_ref, ctx_out, copy_sems.at[8]))

    summed = TensorSum(place, part, total, 4, (tmp_near, tmp_chip, tmp_far, sum_sems))
    for index in range(4):
        rows = pl.ds(index * tile, tile)
        part[rows, :] = dot_nt(ctx_ref[rows, :], w0[:, pl.ds(q_cols + 2 * kv_cols, q_cols)])
        summed.send_core(index)
    summed.send_across(0)
    summed.send_across(1)
    next(moves, None)
    for index in range(4):
        summed.send_back(index)
        if index < 2:
            summed.send_across(index + 2)
        next(moves, None)
        summed.finish(index)

        def norm_two(sub, carry, index=index):
            rows = pl.ds(pl.multiple_of(index * tile + sub * LANES, LANES), LANES)
            h = x_ref[rows, :].astype(F32) + total[rows, :]
            h_ref[rows, :] = h
            inverse = lax.rsqrt(jnp.mean(h * h, axis=1, keepdims=True) + EPSILON)
            n2_ref[rows, :] = (h * inverse * g2).astype(BF16)
            return carry

        lax.fori_loop(0, tile // LANES, norm_two, 0)
        next(moves, None)
    saves.append(begin(h_ref, h_out, copy_sems.at[9]))
    saves.append(begin(n2_ref, n2_out, copy_sems.at[10]))
    drain(moves)
    second.finish()
    for save in saves:
        save.wait()
    for copy in gain_copies:
        copy.wait_send()
    first.settle()
    second.settle()
    summed.settle()


def forward_call(count, x, gate, up, seg_col, seg_row, cosine, sine, gains, wq, wk, wv, wot):
    seq, width = x.shape
    rows = wq.shape[0]
    q_cols, kv_cols = wq.shape[1], LANES
    attn_cols = wq.shape[1] + wk.shape[1] + wv.shape[1] + wot.shape[1]
    kept = [
        ((seq, width), BF16),
        ((seq, q_cols + kv_cols), F32),
        ((q_cols // HALF, seq, LANES), BF16),
        ((seq, LANES), BF16),
        ((seq, LANES), BF16),
        ((seq, LANES), F32),
        ((seq, q_cols), BF16),
        ((seq, width), F32),
        ((seq, width), BF16),
    ]
    attn = ((count * rows, attn_cols), BF16)
    outs = [attn, ((count * rows, 2 * gate.shape[1]), BF16), *kept, ((8, width), F32)]
    dma = pltpu.SemaphoreType.DMA
    return pl.pallas_call(
        functools.partial(forward_kernel, count),
        out_shape=[jax.ShapeDtypeStruct(*out) for out in outs],
        in_specs=[in_place()] * 3 + [whole_block()] * 9,
        out_specs=[in_place()] * 11 + [whole_block()],
        scratch_shapes=[
            pltpu.VMEM((seq, width), BF16),
            pltpu.VMEM(*attn),
            *[pltpu.VMEM(*one) for one in kept],
            pltpu.VMEM((rows, attn_cols), BF16),
            pltpu.VMEM((rows, 2 * gate.shape[1]), BF16),
            pltpu.VMEM(gate.shape, F32),
            pltpu.VMEM(up.shape, F32),
            pltpu.VMEM((4, seq // 4, seq), F32),
            pltpu.VMEM((count,) + gains.shape, F32),
            pltpu.VMEM((seq, width), F32),
            pltpu.VMEM((seq, width), F32),
            *TensorSum.scratch(seq, width, 4, F32),
            dma((count,)),
            dma((count,)),
            dma((13,)),
            *Gather.sems(count),
            *Gather.sems(count),
        ],
        compiler_params=pltpu.CompilerParams(
            collective_id=1, has_side_effects=True, vmem_limit_bytes=61 << 20
        ),
    )(x, gate, up, seg_col, seg_row, cosine, sine, gains, wq, wk, wv, wot)


def store(ref, rows, value):
    ref[rows, :] = value


def store_apart(gate, up, rows, value):
    even = gate.shape[1] // LANES
    for index in range(even):
        cols = pl.ds(index * LANES, LANES)
        gate[rows, cols] = value[:, 2 * index * LANES : (2 * index + 1) * LANES]
        up[rows, cols] = value[:, (2 * index + 1) * LANES : (2 * index + 2) * LANES]
    if gate.shape[1] % LANES:
        rest = value[:, 2 * even * LANES :]
        cols = pl.ds(even * LANES, HALF)
        gate[rows, cols] = rest[:, :HALF]
        up[rows, cols] = pltpu.roll(rest, HALF, 1)[:, :HALF]


class Scatter:
    def __init__(self, place, partial, result, late, scratch):
        self.place, self.partial = place, partial
        self.put = result if callable(result) else functools.partial(store, result)
        self.rows = partial.shape[0] // place.count
        self.late = late
        early = self.rows - late
        half = (early // 2 + 15) // 16 * 16
        self.cuts = [(0, half), (half, early - half)] if early > half else [(0, early)]
        self.tail = (early, late)
        self.over_in, self.far_in, self.far_other, self.late_in = scratch[:4]
        self.zsend, self.zrecv, self.ysend, self.yrecv, self.lsend, self.lrecv = scratch[4:]
        self.sent = []
        depth = place.depth
        orders = [
            sorted(range(depth), key=lambda goal, far=far: (-abs(goal - far), -goal)) for far in range(depth)
        ]
        self.goals = []
        for index in range(depth):
            goal = jnp.int32(0)
            for far in range(depth):
                goal = goal + orders[far][index] * (place.far == far).astype(jnp.int32)
            self.goals.append(goal)
        self.pieces = [(index, cut) for index in range(depth) for cut in range(len(self.cuts))]

    @staticmethod
    def scratch(count, rows, width, late):
        depth = count // NEAR
        dma = pltpu.SemaphoreType.DMA
        return [
            pltpu.VMEM((depth, rows - late, width), BF16),
            pltpu.VMEM((depth + 2, rows, width), BF16),
            pltpu.VMEM((depth + 2, max(late, 16), width), BF16),
            pltpu.VMEM((max(late, 16), width), BF16),
            dma((depth - 1, 4)),
            dma((depth + 2, 4)),
            dma((depth, 2)),
            dma((depth, 2)),
            dma,
            dma,
        ]

    def spot(self, goal, other, start, size):
        near = 1 - self.place.near if other else self.place.near
        return pl.ds(pl.multiple_of((goal * NEAR + near) * self.rows + start, 16), size)

    def over(self, number):
        place = self.place
        index, cut = self.pieces[number]
        start, size = self.cuts[cut]
        return remote(
            self.partial.at[self.spot(self.goals[index], True, start, size), :],
            self.over_in.at[index, pl.ds(start, size), :],
            self.ysend.at[index, cut], self.yrecv.at[index, cut], place.beside, place.tensor,
        )

    def cross(self, number):
        if number < len(self.pieces):
            self.over(number).start()
            self.sent.append(lambda: self.over(number))

    def start(self):
        self.start_far()
        self.start_near()

    def start_near(self):
        for number in range(len(self.cuts)):
            self.cross(number)

    def start_far(self):
        if self.late:
            for index in range(self.place.depth - 1):
                for item in (2, 3):
                    pl.when(jnp.logical_not(self.fed(index)))(lambda index=index, item=item: self.hop(index, item).start())

    def add(self, spot, sources):
        size = sources[0].shape[0]
        part = 32 if size % 32 == 0 else 16

        def body(index, carry):
            start = pl.multiple_of(index * part, 16)
            rows = pl.ds(pl.multiple_of(spot.start + start, 16), part)
            total = self.partial[rows, :].astype(F32)
            for source in sources:
                total = total + source[pl.ds(start, part), :].astype(F32)
            self.partial[rows, :] = total.astype(BF16)
            return carry

        lax.fori_loop(0, size // part, body, 0)

    def item(self, item):
        return (0, *self.cuts[item]) if item < 2 else (item - 2, *self.tail)

    def into(self, slot, item):
        other, start, size = self.item(item)
        return self.far_other.at[slot] if other else self.far_in.at[slot, pl.ds(start, size), :]

    def wait_far(self, slot, item):
        place = self.place
        into = self.into(slot, item)
        remote(
            into, into, self.zsend.at[0, item], self.zrecv.at[slot, item], place.me, place.tensor
        ).wait_recv()
        return into

    def hop(self, index, item):
        place = self.place
        goal = self.goals[index]
        sign = 2 * (goal > place.far).astype(jnp.int32) - 1
        ends = ((goal - place.far) * sign == 1).astype(jnp.int32)
        slot = goal + ends * (place.depth + (1 - sign) // 2 - goal)
        return remote(
            self.partial.at[self.spot(goal, *self.item(item)), :], self.into(slot, item),
            self.zsend.at[index, item], self.zrecv.at[slot, item], place.me + sign * NEAR, place.tensor,
        )

    def arrived(self, index, cut):
        number = index * len(self.cuts) + cut
        self.over(number).wait_recv()
        self.cross(number + len(self.cuts))
        start, size = self.cuts[cut]
        return self.over_in.at[index, pl.ds(start, size), :]

    def fed(self, index):
        place = self.place
        up = self.goals[index] > place.far
        return (up & (place.far > 0)) | (jnp.logical_not(up) & (place.far < place.depth - 1))

    def pass_on(self, index, item, base):
        self.add(self.spot(self.goals[index], *self.item(item)), base)
        self.hop(index, item).start()

    def first(self, number):
        index, cut = self.pieces[number]
        came = self.arrived(index, cut)
        if index < self.place.depth - 1:
            pl.when(jnp.logical_not(self.fed(index)))(lambda: self.pass_on(index, cut, [came]))

    def then(self, index, item):
        base = [self.over_in.at[index, pl.ds(*self.cuts[item]), :]] if item < 2 else []
        pl.when(self.fed(index))(
            lambda: self.pass_on(index, item, base + [self.wait_far(self.goals[index], item)])
        )
        self.sent.append(lambda: self.hop(index, item))

    def close(self, item):
        place = self.place
        spot = self.spot(place.far, *self.item(item))
        for way, comes in enumerate((place.far > 0, place.far < place.depth - 1)):

            @pl.when(comes)
            def _(way=way):
                self.add(spot, [self.wait_far(place.depth + way, item)])

    def last(self):
        place = self.place
        return remote(
            self.partial.at[self.spot(place.far, True, *self.tail), :], self.late_in,
            self.lsend, self.lrecv, place.beside, place.tensor,
        )

    def far_steps(self):
        for index in range(self.place.depth - 1 if self.late else 0):
            for item in (2, 3):
                self.then(index, item)
            yield

    def steps(self, far=True):
        place = self.place
        cuts = len(self.cuts)
        passing = cuts * (place.depth - 1)
        for number in range(len(self.pieces) + cuts):
            if number < len(self.pieces):
                self.first(number)
            index = (number - 1) // cuts
            if far and self.late and number and (number - 1) % cuts == 0 and index < place.depth - 1:
                self.then(index, 2)
                self.then(index, 3)
            if cuts <= number < passing + cuts:
                self.then(*self.pieces[number - cuts])
            if number == len(self.pieces) - 1 and self.late:
                self.close(3)
                self.last().start()
                self.sent.append(self.last)
                self.close(2)
            if number >= passing + cuts:
                cut = number - passing - cuts
                start, size = self.cuts[cut]
                own = self.spot(place.far, 0, start, size)
                self.add(own, [self.over_in.at[place.depth - 1, pl.ds(start, size), :]])
                self.close(cut)
                self.put(pl.ds(start, size), self.partial[own, :].astype(F32))
            yield
        if self.late:
            start, size = self.tail
            self.last().wait_recv()
            self.put(
                pl.ds(start, size),
                self.partial[self.spot(place.far, 0, start, size), :].astype(F32) + self.late_in[...].astype(F32),
            )
            yield

    def settle(self):
        for make in self.sent:
            make().wait_send()


def mlp_kernel(count, shares, *refs):
    (
        n2_hbm, cot_hbm, gates_hbm, pack_down,
        first_out, second_out, dn2_out, part_out, down_ref,
        n2_ref, cot_ref, dn2_part, dn2_ref, w1, w2, ab, hid, partial, near, chip, far, sum_sems, copy_sems, *rest,
    ) = refs
    place = Place(count)
    seq, width = n2_ref.shape
    both = w1.shape[1]
    even = both // (2 * LANES)
    split = first_out.shape[1]
    tile = seq // 4
    lanes = lane_ids()
    loads = [
        begin(src, dst, copy_sems.at[index])
        for index, (src, dst) in enumerate(((n2_hbm, n2_ref), (gates_hbm, w1), (cot_hbm, cot_ref)))
    ]
    place.greet(False, True)
    gather = Gather(place, pack_down, w2, shares[0], rest[:5])
    scatter = Scatter(place, partial, down_ref, shares[1], rest[5:])
    summed = TensorSum(place, dn2_part, dn2_ref, 4, (near, chip, far, sum_sems))
    gather.start()
    moves, sums, tensor = gather.steps(), scatter.steps(False), summed.steps()
    loads[0].wait()
    loads[1].wait()

    def gate_up(index):
        cols = pl.ds(pl.multiple_of(index * 2 * LANES, 2 * LANES), 2 * LANES)
        got = dot_nn(n2_ref[...], w1[:, cols])
        gate, up = got[:, :LANES], got[:, LANES:]
        sig = jax.nn.sigmoid(gate)
        act = gate * sig
        hid[:, pl.ds(pl.multiple_of(index * LANES, LANES), LANES)] = (act * up).astype(BF16)
        slope = up * sig * (1.0 + gate * (1.0 - sig))
        ab[:, cols] = jnp.concatenate([slope, act], axis=1).astype(BF16)

    polled(even, gate_up, (moves, {8: 1, 12: 1}))
    tail = pl.ds(2 * even * LANES, LANES)
    got = dot_nn(n2_ref[...], w1[:, tail])
    up = pltpu.roll(got, HALF, 1)
    sig = jax.nn.sigmoid(got)
    act = got * sig
    hid[:, pl.ds(even * LANES, LANES)] = jnp.where(lanes < HALF, act * up, 0.0).astype(BF16)
    slope = up * sig * (1.0 + got * (1.0 - sig))
    ab[:, tail] = jnp.where(lanes < HALF, slope, pltpu.roll(act, HALF, 1)).astype(BF16)
    loads[2].wait()

    def down_grad(index):
        rows = pl.ds(pl.multiple_of(index * 384, 384), 384)
        partial[rows, :] = dot_tn(cot_ref[:, rows], hid[...]).astype(BF16)

    polled(width // 384, down_grad, (moves, {1: 1, 3: 1}))
    scatter.start_far()
    drain(moves)
    drain(scatter.far_steps())
    gather.finish()
    scatter.start_near()

    def inner_grad(index):
        got = dot_nn(cot_ref[...], w2[:, pl.ds(pl.multiple_of(index * 2 * LANES, 2 * LANES), 2 * LANES)])
        for side in range(2):
            piece = got[:, side * LANES : (side + 1) * LANES]
            cols = pl.ds(pl.multiple_of(index * 4 * LANES + side * 2 * LANES, 2 * LANES), 2 * LANES)
            ab[:, cols] = (ab[:, cols].astype(F32) * jnp.concatenate([piece, piece], axis=1)).astype(BF16)

    polled(even // 2, inner_grad, (sums, {5: 1}))
    got = dot_nn(cot_ref[...], w2[:, pl.ds((even - 1) * LANES, 2 * LANES)])
    piece = got[:, :LANES]
    cols = pl.ds(2 * (even - 1) * LANES, 2 * LANES)
    ab[:, cols] = (ab[:, cols].astype(F32) * jnp.concatenate([piece, piece], axis=1)).astype(BF16)
    piece = got[:, LANES:]
    piece = jnp.where(lanes < HALF, piece, pltpu.roll(piece, HALF, 1))
    ab[:, tail] = (ab[:, tail].astype(F32) * piece).astype(BF16)

    def normed_grad(index):
        rows = pl.ds(pl.multiple_of(index * tile, tile), tile)
        dn2_part[rows, :] = dot_nt(ab[rows, :], w1[...]).astype(BF16)
        for at in range(4):

            @pl.when(index == at)
            def _(at=at):
                summed.send_core(at)
                ahead(sums, 1)
                if at:
                    ahead(tensor, 1)

    lax.fori_loop(0, 4, lambda index, carry: (normed_grad(index), carry)[1], 0)

    def output_part(index):
        rows = pl.ds(pl.multiple_of(index * 256, 256), 256)
        cot_ref[:, rows] = dot_nt(hid[...], w2[rows, :]).astype(BF16)

    polled(width // 256, output_part, (sums, {2: 1, 5: 1}), (tensor, {5: 1}))
    saves = [begin(cot_ref, part_out, copy_sems.at[4])]

    def gates_grad(index):
        rows = pl.ds(pl.multiple_of(index * 384, 384), 384)
        for low, high in ((0, split), (split, both)):
            w1[rows, pl.ds(low, high - low)] = dot_tn(n2_ref[:, rows], ab[:, pl.ds(low, high - low)]).astype(BF16)

    polled(width // 384, gates_grad, (sums, every(4)), (tensor, {1: 1, 3: 1}))
    saves.append(begin(w1.at[:, pl.ds(0, split)], first_out, copy_sems.at[5]))
    saves.append(begin(w1.at[:, pl.ds(split, both - split)], second_out, copy_sems.at[6]))
    drain(tensor, sums)
    for index in range(4):
        summed.finish(index)
    saves.append(begin(dn2_ref, dn2_out, copy_sems.at[3]))
    for save in saves:
        save.wait()
    gather.settle()
    scatter.settle()
    summed.settle()


def mlp_call(count, n2, cot, full_gates, pack_down):
    seq, width = n2.shape
    rows, down = pack_down.shape
    shares = late_share(rows, 1 / 6), late_share(rows, 1 / 4)
    both = full_gates.shape[1]
    split = 14 * LANES
    shape = jax.ShapeDtypeStruct
    dma = pltpu.SemaphoreType.DMA
    return pl.pallas_call(
        functools.partial(mlp_kernel, count, shares),
        out_shape=[
            shape((width, split), BF16),
            shape((width, both - split), BF16),
            shape((seq, width), BF16),
            shape((seq, width), BF16),
            shape((rows, down), F32),
        ],
        in_specs=[in_place()] * 4,
        out_specs=[in_place()] * 4 + [whole_block()],
        scratch_shapes=[
            *[pltpu.VMEM((seq, width), BF16)] * 4,
            pltpu.VMEM((width, both), BF16),
            pltpu.VMEM((width, down), BF16),
            pltpu.VMEM((seq, both), BF16),
            pltpu.VMEM((seq, down), BF16),
            pltpu.VMEM((width, down), BF16),
            *TensorSum.scratch(seq, width, 4, BF16),
            dma((7,)),
            *Gather.sems(count),
            *Scatter.scratch(count, rows, down, shares[1]),
        ],
        compiler_params=pltpu.CompilerParams(
            collective_id=2, has_side_effects=True, vmem_limit_bytes=61 << 20
        ),
    )(n2, cot, full_gates, pack_down)


def middle_kernel(count, *refs):
    (
        part_in, dn2_hbm, h_hbm, cot_hbm, w0_hbm, ctx_hbm, gain_ref,
        dh_out, dm_out, dwo_out, gate_ref, up_ref, small_ref,
        partial, dn2_ref, h_ref, cot_ref, wo, ctx_ref, dh_ref, dm_ref, dwo_ref, dhb, copy_sems, *rest,
    ) = refs
    place = Place(count)
    seq, width = dn2_ref.shape
    q_cols = ctx_ref.shape[1]
    heads = q_cols // HALF
    group = heads // 2
    tile = seq // 4
    lanes = lane_ids()
    loads = [
        begin(src, dst, copy_sems.at[index])
        for index, (src, dst) in enumerate(
            (
                (part_in, partial), (dn2_hbm, dn2_ref), (h_hbm, h_ref), (cot_hbm, cot_ref),
                (w0_hbm.at[:, pl.ds(w0_hbm.shape[1] - q_cols, q_cols)], wo), (ctx_hbm, ctx_ref),
            )
        )
    ]
    place.greet(False, False)
    put = functools.partial(store_apart, gate_ref, up_ref)
    scatter = Scatter(place, partial, put, late_share(gate_ref.shape[0], 1 / 6), rest)
    loads[0].wait()
    scatter.start()
    sums = scatter.steps()
    g2 = gain_ref[pl.ds(1, 1), :]
    for load in loads[1:]:
        load.wait()
    small_ref[...] = jnp.zeros_like(small_ref)

    def residual_grad(index, carry):
        rows = pl.ds(pl.multiple_of(index * 64, 64), 64)
        grad = dn2_ref[rows, :].astype(F32)
        h = h_ref[rows, :]
        inverse = lax.rsqrt(jnp.mean(h * h, axis=1, keepdims=True) + EPSILON)
        scaled = grad * g2
        inner = jnp.mean(scaled * h, axis=1, keepdims=True)
        dh = cot_ref[rows, :].astype(F32) + inverse * scaled - h * (inverse * inverse * inverse * inner)
        dh_ref[rows, :] = dh
        dhb[rows, :] = dh.astype(BF16)
        return carry + jnp.sum((grad * h * inverse).reshape(8, 8, width), axis=0)

    def back(index):
        small_ref[...] += lax.fori_loop(
            index * (tile // 64), (index + 1) * (tile // 64), residual_grad, jnp.zeros((8, width), F32)
        )
        rows = pl.ds(pl.multiple_of(index * tile, tile), tile)
        dctx = dot_nn(dhb[rows, :], wo[...])
        for pair in range(heads // 2):
            value = dctx[:, pair * LANES : (pair + 1) * LANES]
            swapped = pltpu.roll(value, HALF, 1)
            for side in range(2):
                head = 2 * pair + side
                keep = value if side == head // group else swapped
                dm_ref[head, rows, :] = jnp.where(lanes // HALF == head // group, keep, 0.0).astype(BF16)

    polled(4, back, (sums, {1: 1, 2: 1, 3: 1}))
    saves = [begin(dh_ref, dh_out, copy_sems.at[6]), begin(dm_ref, dm_out, copy_sems.at[7])]

    def out_grad(index):
        rows = pl.ds(pl.multiple_of(index * 384, 384), 384)
        dwo_ref[rows, :] = dot_tn(dhb[:, rows], ctx_ref[...]).astype(BF16)

    polled(width // 384, out_grad, (sums, {1: 1, 3: 1}))
    saves.append(begin(dwo_ref, dwo_out, copy_sems.at[8]))
    drain(sums)
    for save in saves:
        save.wait()
    scatter.settle()


def middle_call(count, part, dn2, h, cot, w0, ctx, gains):
    seq, width = dn2.shape
    q_cols = ctx.shape[1]
    rows = width // count
    shape = jax.ShapeDtypeStruct
    dma = pltpu.SemaphoreType.DMA
    return pl.pallas_call(
        functools.partial(middle_kernel, count),
        out_shape=[
            shape((seq, width), F32),
            shape((q_cols // HALF, seq, LANES), BF16),
            shape((width, q_cols), BF16),
            shape((rows, part.shape[1] // 2), F32),
            shape((rows, part.shape[1] // 2), F32),
            shape((8, width), F32),
        ],
        in_specs=[in_place()] * 6 + [whole_block()],
        out_specs=[in_place()] * 3 + [whole_block()] * 3,
        scratch_shapes=[
            pltpu.VMEM(part.shape, BF16),
            pltpu.VMEM((seq, width), BF16),
            pltpu.VMEM((seq, width), F32),
            pltpu.VMEM((seq, width), BF16),
            pltpu.VMEM((width, q_cols), BF16),
            pltpu.VMEM((seq, q_cols), BF16),
            pltpu.VMEM((seq, width), F32),
            pltpu.VMEM((q_cols // HALF, seq, LANES), BF16),
            pltpu.VMEM((width, q_cols), BF16),
            pltpu.VMEM((seq, width), BF16),
            dma((9,)),
            *Scatter.scratch(count, rows, part.shape[1], late_share(rows, 1 / 6)),
        ],
        compiler_params=pltpu.CompilerParams(
            collective_id=3, has_side_effects=True, vmem_limit_bytes=61 << 20
        ),
    )(part, dn2, h, cot, w0, ctx, gains)


def last_kernel(count, *refs):
    (
        part_in, dwo_in, dm_hbm, qm_hbm, kb_hbm, vb_hbm, lse_hbm, qk_hbm, n1_hbm, w0_hbm, x_hbm, dh_hbm,
        cos_ref, sin_ref, seg_col, seg_row, gain_ref, two_ref,
        grad_out, gate_ref, up_ref, out_ref, qkv_ref, small_ref,
        partial, partial_o, dm_ref, qm_ref, kb_ref, vb_ref, lse_ref, qk_ref, n1_ref, wqkv, x_ref, dh_ref,
        partial_qkv, bias, dk, dv, head_sums, dlow, part, dn1_ref, small, slots, head_slots,
        near, chip, far, sum_sems, small_send, small_recv, copy_sems, *rest,
    ) = refs
    place = Place(count)
    seq, width = n1_ref.shape
    kv_cols = kb_ref.shape[1]
    q_cols = qk_ref.shape[1] - kv_cols
    pairs = q_cols // LANES
    group = (q_cols // HALF) // (kv_cols // HALF)
    tile = seq // 4
    own = width // count
    few = HALF // count
    lanes = lane_ids()
    sources = (
        (part_in, partial), (dwo_in, partial_o), (qm_hbm, qm_ref), (kb_hbm, kb_ref), (lse_hbm, lse_ref),
        (dm_hbm, dm_ref), (vb_hbm, vb_ref), (qk_hbm, qk_ref),
        (w0_hbm.at[:, pl.ds(0, wqkv.shape[1])], wqkv), (n1_hbm, n1_ref), (x_hbm, x_ref), (dh_hbm, dh_ref),
    )
    loads = [begin(src, dst, copy_sems.at[index]) for index, (src, dst) in enumerate(sources)]
    place.greet(True, True)
    third = len(rest) // 3
    late = late_share(gate_ref.shape[0], 1 / 6)
    scatter = Scatter(place, partial, functools.partial(store_apart, gate_ref, up_ref), late, rest[:third])
    scatter_o = Scatter(place, partial_o, out_ref, late, rest[third : 2 * third])
    scatter_qkv = Scatter(place, partial_qkv, qkv_ref, late, rest[2 * third :])
    final = TensorSum(place, part, dn1_ref, 4, (near, chip, far, sum_sems))
    for load in loads[:2]:
        load.wait()
    scatter.start()
    sums, sums_o = scatter.steps(), scatter_o.steps()
    dk[...] = jnp.zeros_like(dk)
    dv[...] = jnp.zeros_like(dv)
    gq = gain_ref[pl.ds(2, 1), pl.ds(0, LANES)]
    gk = gain_ref[pl.ds(3, 1), pl.ds(0, LANES)]
    for load in loads[2:9]:
        load.wait()

    def head_back(grad, raw, cosine, sine, gain):
        back = turn(grad, cosine, -sine)
        inverse = lax.rsqrt(head_mean(raw * raw) + EPSILON)
        scaled = back * gain
        inner = head_mean(scaled * raw)
        low = inverse * scaled - raw * (inverse * inverse * inverse * inner)
        return low.astype(BF16), jnp.sum((back * raw * inverse).reshape(-1, 8, LANES), axis=0)

    head_sums[...] = jnp.zeros_like(head_sums)
    turns = {3: every(3), 2: every(3), 1: {0: 1, 2: 1}, 0: {2: 1}}
    for qb in reversed(range(4)):
        last = (qb + 1) * tile
        rows = pl.ds(qb * tile, tile)
        bias_block(seg_col, seg_row, bias, qb * tile, tile)

        def attend_back(pair, last=last, rows=rows):
            keys = pl.ds(0, last)
            sides = []
            for side in range(2):
                head = 2 * pair + side
                kv = head // group
                query, grad = qm_ref[head, rows, :], dm_ref[head, rows, :]
                logsum = jnp.sum(jnp.where(lanes == head, lse_ref[rows, :], 0.0), axis=1, keepdims=True)
                logits = dot_nt(query, kb_ref[keys, :]) + bias[:, keys]
                probs = jnp.exp(logits - logsum)
                dprob = dot_nt(grad, vb_ref[keys, :])
                inner = jnp.sum(probs * dprob, axis=1, keepdims=True)
                ds = (probs * (dprob - inner)).astype(BF16)
                got = dot_nn(ds, kb_ref[keys, :]) * 0.125
                sides.append(jnp.where(kv == side, got, pltpu.roll(got, HALF, 1)))
                dk[keys, :] += dot_tn(ds, query)
                dv[keys, :] += dot_tn(probs.astype(BF16), grad)
            cols = pl.ds(pl.multiple_of(pair * LANES, LANES), LANES)
            low, terms = head_back(
                jnp.where(lanes < HALF, sides[0], sides[1]), qk_ref[rows, cols], cos_ref[rows, :], sin_ref[rows, :], gq
            )
            dlow[rows, cols] = low
            head_sums[pl.ds(0, 8), :] += terms

        polled(pairs, attend_back, (sums, turns[qb]))
        low, terms = head_back(
            dk[rows, :], qk_ref[rows, pl.ds(q_cols, LANES)], cos_ref[rows, :], sin_ref[rows, :], gk
        )
        dlow[rows, pl.ds(q_cols, LANES)] = low
        dlow[rows, pl.ds(q_cols + LANES, LANES)] = dv[rows, :].astype(BF16)
        head_sums[pl.ds(8, 8), :] += terms
        part[rows, :] = dot_nt(dlow[rows, :], wqkv[...]).astype(BF16)
        final.send_core(qb)
        if qb < 3:
            final.send_back(qb + 1)
        final.send_across(qb)
        if qb == 2:
            scatter_o.start()
        if qb < 2:
            ahead(sums_o, 2)
    mine = head_slots.at[place.tensor]
    mine[...] = head_sums[...]
    head_copies = []
    for step in range(1, 4):
        copy = remote(
            mine, mine, small_send.at[step - 1], small_recv.at[step - 1], place.me, lax.rem(place.tensor + step, 4)
        )
        copy.start()
        head_copies.append(copy)
    for load in loads[9:]:
        load.wait()

    def qkv_grad(start):
        partial_qkv[pl.ds(start, 384), :] = dot_tn(n1_ref[:, pl.ds(start, 384)], dlow[...]).astype(BF16)

    blocks(width, 384, qkv_grad)
    scatter_qkv.start()
    sums_qkv = scatter_qkv.steps()
    for step, copy in enumerate(head_copies):
        whose = head_slots.at[lax.rem(place.tensor + 3 - step, 4)]
        remote(whose, whose, small_send.at[step], small_recv.at[step], place.me, place.tensor).wait_recv()
    heads = head_slots[0] + head_slots[1] + head_slots[2] + head_slots[3]
    ahead(sums_o, 2)
    g1 = gain_ref[pl.ds(0, 1), :]
    gain_one = jnp.zeros((8, width), F32)
    saves = []
    for index in reversed(range(4)):
        if index == 0:
            final.send_back(0)
        ahead(sums, 1)
        ahead(sums_o, 1)
        ahead(sums_qkv, 1)
        final.finish(index)

        def input_grad(sub, carry, index=index):
            rows = pl.ds(pl.multiple_of(index * tile + sub * 64, 64), 64)
            grad = dn1_ref[rows, :].astype(F32)
            x = x_ref[rows, :].astype(F32)
            inverse = lax.rsqrt(jnp.mean(x * x, axis=1, keepdims=True) + EPSILON)
            scaled = grad * g1
            inner = jnp.mean(scaled * x, axis=1, keepdims=True)
            dh_ref[rows, :] = dh_ref[rows, :] + inverse * scaled - x * (inverse * inverse * inverse * inner)
            return carry + jnp.sum((grad * x * inverse).reshape(8, 8, width), axis=0)

        gain_one = lax.fori_loop(0, tile // 64, input_grad, gain_one)
        rows = pl.ds(index * tile, tile)
        saves.append(begin(dh_ref.at[rows, :], grad_out.at[rows, :], copy_sems.at[index]))
    one = jnp.sum(gain_one, axis=0, keepdims=True)
    two = jnp.sum(two_ref[...], axis=0, keepdims=True)
    small[...] = jnp.zeros_like(small)
    q_sum = jnp.sum(heads[:8], axis=0, keepdims=True)
    k_sum = jnp.sum(heads[8:], axis=0, keepdims=True)
    q_sum = q_sum + pltpu.roll(q_sum, HALF, 1)
    k_sum = k_sum + pltpu.roll(k_sum, HALF, 1)

    def small_copy(d):
        return remote(
            small.at[d], slots.at[place.me], small_send.at[3 + d], small_recv.at[3 + place.me], d, place.tensor
        )

    for d in range(count):
        for row, (values, size) in enumerate(((one, own), (two, own), (q_sum, few), (k_sum, few))):
            small[d, pl.ds(row, 1), pl.ds(0, size)] = values[:, d * size : (d + 1) * size]
        pl.when(place.me != d)(lambda d=d: small_copy(d).start())
    slots[place.me] = small[place.me]
    drain(sums, sums_o, sums_qkv)
    for d in range(count):

        @pl.when(place.me != d)
        def _(d=d):
            remote(
                slots.at[d], slots.at[d], small_send.at[3 + d], small_recv.at[3 + d], d, place.tensor
            ).wait_recv()

    total = slots[0]
    for d in range(1, count):
        total = total + slots[d]
    small_ref[...] = total
    for d in range(count):
        pl.when(place.me != d)(lambda d=d: small_copy(d).wait_send())
    for save in saves:
        save.wait()
    for copy in head_copies:
        copy.wait_send()
    for each in (scatter, scatter_o, scatter_qkv, final):
        each.settle()


def last_call(count, part, dwo, dm, qm, kb, vb, lse, qk, n1, w0, x, dh, cosine, sine, seg_col, seg_row, gains, two):
    seq, width = n1.shape
    rows = width // count
    q_cols = dwo.shape[1]
    low = qk.shape[1] + LANES
    shape = jax.ShapeDtypeStruct
    dma = pltpu.SemaphoreType.DMA
    loaded = [part, dwo, dm, qm, kb, vb, lse, qk, n1, jax.ShapeDtypeStruct((width, low), BF16), x, dh]
    small = (8, 2 * LANES)
    return pl.pallas_call(
        functools.partial(last_kernel, count),
        out_shape=[
            shape((seq, width), F32),
            shape((rows, part.shape[1] // 2), F32),
            shape((rows, part.shape[1] // 2), F32),
            shape((rows, q_cols), F32),
            shape((rows, low), F32),
            shape(small, F32),
        ],
        in_specs=[in_place()] * 12 + [whole_block()] * 6,
        out_specs=[in_place()] + [whole_block()] * 5,
        scratch_shapes=[
            *[pltpu.VMEM(one.shape, one.dtype) for one in loaded],
            pltpu.VMEM((width, low), BF16),
            pltpu.VMEM((seq // 4, seq), F32),
            pltpu.VMEM((seq, LANES), F32),
            pltpu.VMEM((seq, LANES), F32),
            pltpu.VMEM((16, LANES), F32),
            pltpu.VMEM((seq, low), BF16),
            pltpu.VMEM((seq, width), BF16),
            pltpu.VMEM((seq, width), BF16),
            pltpu.VMEM((count,) + small, F32),
            pltpu.VMEM((count,) + small, F32),
            pltpu.VMEM((4, 16, LANES), F32),
            *TensorSum.scratch(seq, width, 4, BF16),
            dma((count + 3,)),
            dma((count + 3,)),
            dma((12,)),
            *Scatter.scratch(count, rows, part.shape[1], late_share(rows, 1 / 6)),
            *Scatter.scratch(count, rows, q_cols, late_share(rows, 1 / 6)),
            *Scatter.scratch(count, rows, low, late_share(rows, 1 / 6)),
        ],
        compiler_params=pltpu.CompilerParams(
            collective_id=4, has_side_effects=True, vmem_limit_bytes=61 << 20
        ),
    )(part, dwo, dm, qm, kb, vb, lse, qk, n1, w0, x, dh, cosine, sine, seg_col, seg_row, gains, two)


def rotation_lanes(positions):
    lane = np.arange(LANES)
    frequency = ROPE_BASE ** (-(lane % (HALF // 2)) * 2.0 / HALF)
    sign = np.where(lane % HALF < HALF // 2, -1.0, 1.0)
    angles = positions.astype(F32)[:, None] * frequency.astype(np.float32)[None, :]
    return jnp.cos(angles), jnp.sin(angles) * sign.astype(np.float32)[None, :]


def shards(
    block_input,
    segments,
    positions,
    norm1_gain,
    q_norm_gain,
    k_norm_gain,
    w_q,
    w_k,
    w_v,
    w_o,
    norm2_gain,
    w_gate,
    w_up,
    w_down,
    cotangent,
    *,
    n_dp,
    n_tensor,
):
    rows = w_q.shape[0]
    q_cols, kv_cols, ff_cols = w_q.shape[1], w_k.shape[1], w_gate.shape[1]
    small_gain = q_norm_gain.shape[0]
    seg_col, seg_row = segments[:, None], segments[None, :]
    gains = jnp.concatenate(
        [jnp.pad(gain, (0, 2 * LANES - gain.shape[0])) for gain in (norm1_gain, norm2_gain, q_norm_gain, k_norm_gain)]
        + [jnp.zeros((8 * LANES,), F32)]
    ).reshape(8, 2 * LANES)
    pack_down = jnp.pad(w_down.T.astype(BF16), ((0, 0), (0, -ff_cols % LANES)))
    cosine, sine = rotation_lanes(positions)
    w0, w1, n1, qk, qm, kb, vb, lse, ctx, h, n2, gains = forward_call(
        n_dp, block_input, w_gate, w_up, seg_col, seg_row, cosine, sine, gains, w_q, w_k, w_v, w_o.T.astype(BF16)
    )
    first, second, dn2, mlp, down = mlp_call(n_dp, n2, cotangent, w1, pack_down)
    mlp_total = lax.psum(mlp, "tensor")
    dh, dm, dwo, gate_one, up_one, small_two = middle_call(n_dp, first, dn2, h, cotangent, w0, ctx, gains)
    grad_input, gate_two, up_two, grad_o, grad_qkv, small = last_call(
        n_dp, second, dwo, dm, qm, kb, vb, lse, qk, n1, w0, block_input, dh,
        cosine, sine, seg_col, seg_row, gains, small_two,
    )
    output_rows = (h + mlp_total.astype(F32)).astype(BF16)
    return (
        output_rows,
        grad_input,
        small[0, :rows],
        small[2, :small_gain],
        small[3, :small_gain],
        grad_qkv[:, :q_cols],
        grad_qkv[:, q_cols : q_cols + kv_cols],
        grad_qkv[:, q_cols + kv_cols :],
        grad_o.T,
        small[1, :rows],
        jnp.concatenate([gate_one, gate_two], axis=1),
        jnp.concatenate([up_one, up_two], axis=1),
        down[:, :ff_cols].T,
    )


def solution(mesh):
    placed = (
        P("dp", None),
        P("dp"),
        P("dp"),
        P("dp"),
        P("dp"),
        P("dp"),
        P("dp", "tensor"),
        P("dp", "tensor"),
        P("dp", "tensor"),
        P("tensor", "dp"),
        P("dp"),
        P("dp", "tensor"),
        P("dp", "tensor"),
        P("tensor", "dp"),
        P("dp", None),
    )
    return jax.shard_map(
        functools.partial(shards, n_dp=mesh.shape["dp"], n_tensor=mesh.shape["tensor"]),
        mesh=mesh,
        in_specs=placed,
        out_specs=(
            P("dp", None),
            P("dp", None),
            P("dp"),
            P("dp"),
            P("dp"),
            P("dp", "tensor"),
            P("dp", "tensor"),
            P("dp", "tensor"),
            P("tensor", "dp"),
            P("dp"),
            P("dp", "tensor"),
            P("dp", "tensor"),
            P("tensor", "dp"),
        ),
        check_vma=False,
    )
```

```python
import functools

import jax
import jax.numpy as jnp
import numpy as np
from jax import lax
from jax.experimental import pallas as pl
from jax.experimental.pallas import tpu as pltpu
from jax.sharding import PartitionSpec as P

EPSILON = 1e-05
ROPE_BASE = 1000000.0
MASKED = -1e30


MESH = pl.DeviceIdType.MESH
NEAR = 2
HALF = 64
LANES = 128
HIGHEST = lax.Precision.HIGHEST
BF16 = jnp.bfloat16
F32 = jnp.float32


def whole_block():
    return pl.BlockSpec(memory_space=pltpu.VMEM)


def in_place():
    return pl.BlockSpec(memory_space=pl.ANY)


def remote(src, dst, send, recv, dp, tensor):
    return pltpu.make_async_remote_copy(
        src_ref=src,
        dst_ref=dst,
        send_sem=send,
        recv_sem=recv,
        device_id=(dp, tensor),
        device_id_type=MESH,
    )


def begin(src, dst, sem):
    copy = pltpu.make_async_copy(src, dst, sem)
    copy.start()
    return copy


def dot_nn(left, right):
    return jnp.dot(left, right, preferred_element_type=F32)


def dot_nt(left, right):
    return lax.dot_general(left, right, (((1,), (1,)), ((), ())), preferred_element_type=F32)


def dot_tn(left, right):
    return lax.dot_general(left, right, (((0,), (0,)), ((), ())), preferred_element_type=F32)


class Place:
    def __init__(self, count):
        self.count = count
        self.depth = count // NEAR
        self.me = lax.axis_index("dp")
        self.tensor = lax.axis_index("tensor")
        self.far = self.me // NEAR
        self.near = lax.rem(self.me, NEAR)
        self.core = lax.rem(self.tensor, 2)
        self.mate = self.tensor + 1 - 2 * self.core
        self.across = lax.rem(self.tensor + 2, 4)
        self.beside = self.me + 1 - 2 * self.near

    def ahead(self, step):
        return lax.rem(self.far + step, self.depth)

    def behind(self, step):
        return lax.rem(self.far + self.depth - step, self.depth)

    def greet(self, everyone, tensor):
        barrier = pltpu.get_barrier_semaphore()
        peers = []
        if everyone:
            peers += [(lax.rem(self.me + d, self.count), self.tensor) for d in range(1, self.count)]
        else:
            peers += [
                (self.ahead(step) * NEAR + self.near, self.tensor) for step in range(1, self.depth)
            ]
            peers.append((self.beside, self.tensor))
        if tensor:
            peers += [(self.me, lax.rem(self.tensor + t, 4)) for t in range(1, 4)]
        for peer in peers:
            pl.semaphore_signal(barrier, 1, device_id=peer, device_id_type=MESH)
        pl.semaphore_wait(barrier, len(peers))


class Gather:
    def __init__(self, place, shard, full, late, sems):
        self.place, self.shard, self.full = place, shard, full
        self.rows = shard.shape[0]
        self.cuts = [(0, self.rows - late)] + ([(self.rows - late, late)] if late else [])
        self.zsend, self.zrecv, self.ysend, self.yrecv, self.own = sems
        self.sent = []

    @staticmethod
    def sems(count):
        depth = count // NEAR
        dma = pltpu.SemaphoreType.DMA
        return [dma((2, depth - 1, 3)), dma((2, depth - 1, 3)), dma((2 * depth - 1, 2)), dma((2 * depth - 1, 2)), dma]

    def spot(self, block, cut):
        start, size = self.cuts[cut]
        return self.full.at[pl.ds(pl.multiple_of(block * self.rows + start, 16), size), :]

    def mine(self, cut):
        start, size = self.cuts[cut]
        return self.shard.at[pl.ds(start, size), :]

    def block(self, way, step, other):
        far = self.place.far - step if way == 0 else self.place.far + step
        return far * NEAR + (1 - self.place.near if other else self.place.near)

    def valid(self, way, step):
        return self.place.far >= step if way == 0 else self.place.far + step < self.place.depth

    def emit(self, make):
        copy, when = make()
        if when is None:
            copy.start()
        else:
            pl.when(when)(copy.start)
        self.sent.append(make)

    def along(self, way, step, cut, other):
        place = self.place
        if step >= place.depth - 1:
            return

        def make():
            more = place.far < place.depth - 1 if way == 0 else place.far > 0
            spot = self.spot(self.block(way, step, other), cut)
            copy = remote(
                self.mine(cut) if step == 0 and not other else spot, spot,
                self.zsend.at[way, step, cut + other], self.zrecv.at[way, step, cut + other],
                place.me + (NEAR if way == 0 else -NEAR), place.tensor,
            )
            return copy, more if step == 0 else more & self.valid(way, step)

        self.emit(make)

    def crossing(self, way, step, cut, other):
        place = self.place
        spot = self.spot(self.block(way, step, other), cut)
        slot = step if way == 0 else step + place.depth - 1
        return remote(
            self.mine(cut) if step == 0 and not other else spot, spot,
            self.ysend.at[slot, cut], self.yrecv.at[slot, cut], place.beside, place.tensor,
        ), (self.valid(way, step) if step else None)

    def over(self, way, step, cut):
        self.emit(lambda: self.crossing(way, step, cut, 0))

    def came_over(self, way, step, cut):
        copy, when = self.crossing(way, step, cut, 1)
        if when is None:
            copy.wait_recv()
        else:
            pl.when(when)(copy.wait_recv)

    def start(self):
        place = self.place
        self.local = lambda: pltpu.make_async_copy(
            self.shard, self.full.at[pl.ds(pl.multiple_of(place.me * self.rows, 16), self.rows), :], self.own
        )
        self.local().start()
        for cut in reversed(range(len(self.cuts))):
            self.over(0, 0, cut)
        for cut in range(len(self.cuts)):
            for way in range(2):
                self.along(way, 0, cut, 0)

    def steps(self):
        place = self.place
        if len(self.cuts) > 1:
            self.came_over(0, 0, 1)
            for way in range(2):
                self.along(way, 0, 1, 1)
            yield
        for step in range(1, place.depth):
            for cut in range(len(self.cuts)):
                for other in range(cut + 1):
                    for way in range(2):
                        spot = self.spot(self.block(way, step, other), cut)
                        copy = remote(
                            spot, spot, self.zsend.at[way, step - 1, cut + other],
                            self.zrecv.at[way, step - 1, cut + other], place.me, place.tensor,
                        )
                        pl.when(self.valid(way, step))(copy.wait_recv)
                        self.along(way, step, cut, other)
                        if cut == 0:
                            self.over(way, step, cut)
                    yield

    def finish(self):
        self.came_over(0, 0, 0)
        for step in range(1, self.place.depth):
            for way in range(2):
                self.came_over(way, step, 0)
        self.local().wait()

    def settle(self):
        for make in self.sent:
            copy, when = make()
            if when is None:
                copy.wait_send()
            else:
                pl.when(when)(copy.wait_send)


def late_share(rows, share):
    return int(rows * share) // 16 * 16


class TensorSum:
    def __init__(self, place, part, total, tiles, scratch):
        self.place, self.part, self.total, self.tiles = place, part, total, tiles
        self.tile = part.shape[0] // tiles
        self.half = self.tile // 2
        self.near, self.chip, self.far, self.sems = scratch
        self.sent = []

    @staticmethod
    def scratch(rows, width, tiles, kind):
        half = (rows // 2, width)
        return [
            pltpu.VMEM(half, kind), pltpu.VMEM(half, BF16), pltpu.VMEM(half, BF16), pltpu.SemaphoreType.DMA((6, tiles))
        ]

    def half_rows(self, index, which):
        return pl.ds(pl.multiple_of(index * self.tile + which * self.half, 16), self.half)

    def slot(self, index):
        return pl.ds(index * self.half, self.half)

    def core_copy(self, index):
        place = self.place
        return remote(
            self.part.at[self.half_rows(index, 1 - place.core), :], self.near.at[self.slot(index), :],
            self.sems.at[0, index], self.sems.at[1, index], place.me, place.mate,
        )

    def across_copy(self, index):
        place = self.place
        return remote(
            self.chip.at[self.slot(index), :], self.far.at[self.slot(index), :],
            self.sems.at[2, index], self.sems.at[3, index], place.me, place.across,
        )

    def back_copy(self, index, which):
        place = self.place
        rows = self.half_rows(index, which)
        return remote(
            self.total.at[rows, :], self.total.at[rows, :],
            self.sems.at[4, index], self.sems.at[5, index], place.me, place.mate,
        )

    def send_core(self, index):
        self.core_copy(index).start()
        self.sent.append(lambda: self.core_copy(index))

    def send_across(self, index):
        place = self.place
        self.core_copy(index).wait_recv()
        mine = self.part[self.half_rows(index, place.core), :].astype(F32)
        self.chip[self.slot(index), :] = (mine + self.near[self.slot(index), :].astype(F32)).astype(BF16)
        self.across_copy(index).start()
        self.sent.append(lambda: self.across_copy(index))

    def send_back(self, index):
        place = self.place
        self.across_copy(index).wait_recv()
        both = self.chip[self.slot(index), :].astype(F32) + self.far[self.slot(index), :].astype(F32)
        self.total[self.half_rows(index, place.core), :] = both.astype(self.total.dtype)
        self.back_copy(index, place.core).start()

    def finish(self, index):
        self.back_copy(index, 1 - self.place.core).wait_recv()
        self.back_copy(index, self.place.core).wait_send()

    def steps(self):
        for index in range(2):
            self.send_across(index)
            yield
        for index in range(self.tiles):
            self.send_back(index)
            if index + 2 < self.tiles:
                self.send_across(index + 2)
            yield

    def settle(self):
        for make in self.sent:
            make().wait_send()


def lane_ids(width=LANES):
    return lax.broadcasted_iota(jnp.int32, (1, width), 1)


def head_mean(values):
    row = lax.broadcasted_iota(jnp.int32, (LANES, LANES), 0)
    col = lax.broadcasted_iota(jnp.int32, (LANES, LANES), 1)
    groups = jnp.where(row // HALF == col // HALF, 1.0 / HALF, 0.0).astype(F32)
    return jnp.dot(values, groups, precision=HIGHEST, preferred_element_type=F32)


def turn(values, cosine, sine):
    ahead = pltpu.roll(values, LANES - HALF // 2, 1)
    back = pltpu.roll(values, HALF // 2, 1)
    first = lax.rem(lane_ids(), HALF) < HALF // 2
    return values * cosine + jnp.where(first, ahead, back) * sine


def column_of(row_ref, column):
    for index in range(row_ref.shape[1] // LANES):
        spot = pl.ds(index * LANES, LANES)
        row = row_ref[:, spot].astype(F32)
        column[spot, :] = jnp.broadcast_to(row, (LANES, LANES)).T


def bias_block(seg_col, seg_row, bias, first, tile):
    last = first + tile
    rows = lax.broadcasted_iota(jnp.int32, (tile, last), 0) + first
    cols = lax.broadcasted_iota(jnp.int32, (tile, last), 1)
    same = seg_col[pl.ds(first, tile), pl.ds(0, 1)] == seg_row[:, pl.ds(0, last)].astype(F32)
    allowed = same & (rows >= cols)
    bias[:, pl.ds(0, last)] = jnp.where(allowed, 0.0, MASKED)


def drain(*moves):
    for one in moves:
        for _ in one:
            pass


def ahead(moves, count=1):
    for _ in range(count):
        next(moves, None)


def polled(count, body, *polls):
    def step(index, carry):
        body(index)
        for at in range(count):
            due = [(moves, times[at]) for moves, times in polls if at in times]
            if due:

                @pl.when(index == at)
                def _(due=due):
                    for moves, times in due:
                        ahead(moves, times)

        return carry

    lax.fori_loop(0, count, step, 0)


def every(count, times=1, first=0):
    return {index: times for index in range(first, count)}


def blocks(total, size, body):
    def step(index, carry):
        body(pl.multiple_of(index * size, size))
        return carry

    lax.fori_loop(0, total // size, step, 0)


def forward_kernel(count, *refs):
    (
        x_hbm, gate_hbm, up_hbm, seg_row, pos_row, turn_ref, g1_ref, g2_ref, gq_ref, gk_ref,
        wq_ref, wk_ref, wv_ref, wot_ref,
        full_attn, full_gates, n1_out, qk_out, qm_out, kb_out, vb_out, lse_out, ctx_out, h_out, n2_out, cos_out, sin_out, hq_out,
        gains_out,
        x_ref, w0, n1_ref, qk_ref, qm_ref, kb_ref, vb_ref, lse_ref, ctx_ref, h_ref, n2_ref, cos_ref, sin_ref, hq_ref,
        column, pack_attn, pack_gates, gate_ref, up_ref, bias, gain_slots, part, total, tmp_near, tmp_chip, tmp_far, sum_sems, gain_send, gain_recv, copy_sems,
        *gather_sems,
    ) = refs
    place = Place(count)
    seq, width = x_ref.shape
    q_cols = ctx_ref.shape[1]
    kv_cols = kb_ref.shape[1]
    pairs = q_cols // LANES
    group = (q_cols // HALF) // (kv_cols // HALF)
    tile = seq // 4
    load = begin(x_hbm, x_ref, copy_sems.at[0])
    weights = [begin(gate_hbm, gate_ref, copy_sems.at[11]), begin(up_hbm, up_ref, copy_sems.at[12])]
    spot = 0
    for ref in (wq_ref, wk_ref, wv_ref, wot_ref):
        pack_attn[:, pl.ds(spot, ref.shape[1])] = ref[...].astype(BF16)
        spot += ref.shape[1]
    gain_slots[place.me] = jnp.zeros(gain_slots.shape[1:], F32)
    for row, ref in enumerate((g1_ref, g2_ref, gq_ref, gk_ref)):
        gain_slots[place.me, pl.ds(row, 1), pl.ds(0, ref.shape[1])] = ref[...].astype(BF16).astype(F32)
    place.greet(True, True)
    first = Gather(place, pack_attn, w0, late_share(pack_attn.shape[0], 1 / 6), gather_sems[:5])
    second = Gather(place, pack_gates, full_gates, late_share(pack_gates.shape[0], 1 / 6), gather_sems[5:])
    first.start()
    gain_copies = []
    for step in range(1, count):
        copy = remote(
            gain_slots.at[place.me], gain_slots.at[place.me], gain_send.at[step], gain_recv.at[step],
            lax.rem(place.me + step, count), place.tensor,
        )
        copy.start()
        gain_copies.append(copy)
    for weight in weights:
        weight.wait()
    even = gate_ref.shape[1] // LANES

    def lay(index, carry):
        cols = pl.ds(pl.multiple_of(index * LANES, LANES), LANES)
        for side, ref in enumerate((gate_ref, up_ref)):
            spot = pl.multiple_of((2 * index + side) * LANES, LANES)
            pack_gates[:, pl.ds(spot, LANES)] = ref[:, cols].astype(BF16)
        return carry

    lax.fori_loop(0, even, lay, 0)
    rest = pl.ds(even * LANES, HALF)
    pack_gates[:, pl.ds(2 * even * LANES, LANES)] = jnp.concatenate(
        [gate_ref[:, rest], up_ref[:, rest]], axis=1
    ).astype(BF16)
    column_of(pos_row, column)

    def angles(index, carry):
        rows = pl.ds(pl.multiple_of(index * LANES, LANES), LANES)
        angle = column[rows, pl.ds(0, 1)] * turn_ref[pl.ds(0, 1), :]
        cos_ref[rows, :] = jnp.cos(angle)
        sin_ref[rows, :] = jnp.sin(angle) * turn_ref[pl.ds(1, 1), :]
        return carry

    lax.fori_loop(0, seq // LANES, angles, 0)
    column_of(seg_row, column)
    for qb in range(4):
        bias_block(column, seg_row, bias.at[qb], qb * tile, tile)
    for step in range(1, count):
        whose = gain_slots.at[lax.rem(place.me + count - step, count)]
        remote(whose, whose, gain_send.at[step], gain_recv.at[step], place.me, place.tensor).wait_recv()
    gains_out[...] = jnp.zeros_like(gains_out)
    own = width // count
    for row in range(2):
        gains_out[pl.ds(row, 1), :] = jnp.concatenate(
            [gain_slots[d, pl.ds(row, 1), pl.ds(0, own)] for d in range(count)], axis=1
        )
    for row in range(2, 4):
        gains_out[pl.ds(row, 1), pl.ds(0, LANES)] = jnp.concatenate(
            [gain_slots[d, pl.ds(row, 1), pl.ds(0, HALF // count)] for d in range(count)] * 2, axis=1
        )
    moves_first = first.steps()
    ahead(moves_first, 2)
    g1 = gains_out[pl.ds(0, 1), :]
    g2 = gains_out[pl.ds(1, 1), :]
    load.wait()

    def norm_one(index, carry):
        rows = pl.ds(pl.multiple_of(index * LANES, LANES), LANES)
        x = x_ref[rows, :].astype(F32)
        inverse = lax.rsqrt(jnp.mean(x * x, axis=1, keepdims=True) + EPSILON)
        n1_ref[rows, :] = (x * inverse * g1).astype(BF16)
        return carry

    lax.fori_loop(0, seq // LANES, norm_one, 0)
    saves = [
        begin(n1_ref, n1_out, copy_sems.at[1]),
        begin(cos_ref, cos_out, copy_sems.at[13]),
        begin(sin_ref, sin_out, copy_sems.at[14]),
    ]
    drain(moves_first)
    second.start()
    moves = second.steps()
    first.finish()
    saves.append(begin(w0, full_attn, copy_sems.at[2]))
    gq = gains_out[pl.ds(2, 1), pl.ds(0, LANES)]
    gk = gains_out[pl.ds(3, 1), pl.ds(0, LANES)]
    lanes = lane_ids()

    def project(index, carry):
        rows = pl.ds(pl.multiple_of(index * tile, tile), tile)
        qkv = dot_nn(n1_ref[rows, :], w0[:, pl.ds(0, q_cols + 2 * kv_cols)])
        qk_ref[rows, :] = qkv[:, : q_cols + kv_cols]
        vb_ref[rows, :] = qkv[:, q_cols + kv_cols :].astype(BF16)
        cosine, sine = cos_ref[rows, :], sin_ref[rows, :]
        for pair in range(pairs + 1):
            raw = qkv[:, pair * LANES : (pair + 1) * LANES]
            inverse = lax.rsqrt(head_mean(raw * raw) + EPSILON)
            turned = turn(raw * inverse * (gk if pair == pairs else gq), cosine, sine)
            if pair == pairs:
                kb_ref[rows, :] = turned.astype(BF16)
                continue
            swapped = pltpu.roll(turned, HALF, 1)
            for side in range(2):
                head = 2 * pair + side
                kv = head // group
                keep = (turned if side == kv else swapped).astype(BF16) * 0.125
                qm_ref[head, rows, :] = jnp.where(lanes // HALF == kv, keep, jnp.zeros_like(keep))
        return carry

    lax.fori_loop(0, 4, project, 0)
    for index, (src, dst) in enumerate(((qk_ref, qk_out), (qm_ref, qm_out), (kb_ref, kb_out), (vb_ref, vb_out))):
        saves.append(begin(src, dst, copy_sems.at[3 + index]))
    next(moves, None)

    for qb in range(4):
        last = (qb + 1) * tile
        rows = pl.ds(qb * tile, tile)

        def attend(pair, carry, last=last, rows=rows, qb=qb):
            halves, sums = [], []
            for side in range(2):
                head = 2 * pair + side
                kv = head // group
                logits = dot_nt(qm_ref[head, rows, :], kb_ref[pl.ds(0, last), :]) + bias[qb, :, pl.ds(0, last)]
                top = jnp.max(logits, axis=1, keepdims=True)
                expo = jnp.exp(logits - top)
                summed = jnp.sum(expo, axis=1, keepdims=True)
                probs = (expo * (1.0 / summed)).astype(BF16)
                got = dot_nn(probs, vb_ref[pl.ds(0, last), :])
                halves.append(jnp.where(kv == side, got, pltpu.roll(got, HALF, 1)))
                sums.append(top + jnp.log(summed))
            ctx_ref[rows, pl.ds(pl.multiple_of(pair * LANES, LANES), LANES)] = jnp.where(
                lanes < HALF, halves[0], halves[1]
            ).astype(BF16)
            carry = jnp.where(lanes == 2 * pair, sums[0], carry)
            return jnp.where(lanes == 2 * pair + 1, sums[1], carry)

        lse_ref[rows, :] = lax.fori_loop(0, pairs, attend, jnp.zeros((tile, LANES), F32))
        next(moves, None)
    saves.append(begin(lse_ref, lse_out, copy_sems.at[7]))
    saves.append(begin(ctx_ref, ctx_out, copy_sems.at[8]))

    summed = TensorSum(place, part, total, 4, (tmp_near, tmp_chip, tmp_far, sum_sems))
    for index in range(4):
        rows = pl.ds(index * tile, tile)
        part[rows, :] = dot_nt(ctx_ref[rows, :], w0[:, pl.ds(q_cols + 2 * kv_cols, q_cols)])
        summed.send_core(index)
    summed.send_across(0)
    summed.send_across(1)
    next(moves, None)
    for index in range(4):
        summed.send_back(index)
        if index < 2:
            summed.send_across(index + 2)
        next(moves, None)
        summed.finish(index)

        def norm_two(sub, carry, index=index):
            rows = pl.ds(pl.multiple_of(index * tile + sub * LANES, LANES), LANES)
            h = x_ref[rows, :].astype(F32) + total[rows, :]
            h_ref[rows, :] = h
            hq_ref[rows, :] = (h * 0.25).astype(BF16)
            inverse = lax.rsqrt(jnp.mean(h * h, axis=1, keepdims=True) + EPSILON)
            n2_ref[rows, :] = (h * inverse * g2).astype(BF16)
            return carry

        lax.fori_loop(0, tile // LANES, norm_two, 0)
        next(moves, None)
    saves.append(begin(h_ref, h_out, copy_sems.at[9]))
    saves.append(begin(n2_ref, n2_out, copy_sems.at[10]))
    saves.append(begin(hq_ref, hq_out, copy_sems.at[15]))
    drain(moves)
    second.finish()
    for save in saves:
        save.wait()
    for copy in gain_copies:
        copy.wait_send()
    first.settle()
    second.settle()
    summed.settle()


def forward_call(count, x, gate, up, seg_row, pos_row, turns, g1, g2, gq, gk, wq, wk, wv, wot):
    seq, width = x.shape
    rows = wq.shape[0]
    q_cols, kv_cols = wq.shape[1], LANES
    attn_cols = wq.shape[1] + wk.shape[1] + wv.shape[1] + wot.shape[1]
    kept = [
        ((seq, width), BF16),
        ((seq, q_cols + kv_cols), F32),
        ((q_cols // HALF, seq, LANES), BF16),
        ((seq, LANES), BF16),
        ((seq, LANES), BF16),
        ((seq, LANES), F32),
        ((seq, q_cols), BF16),
        ((seq, width), F32),
        ((seq, width), BF16),
        ((seq, LANES), F32),
        ((seq, LANES), F32),
        ((seq, width), BF16),
    ]
    attn = ((count * rows, attn_cols), BF16)
    outs = [attn, ((count * rows, 2 * gate.shape[1]), BF16), *kept, ((8, width), F32)]
    dma = pltpu.SemaphoreType.DMA
    return pl.pallas_call(
        functools.partial(forward_kernel, count),
        out_shape=[jax.ShapeDtypeStruct(*out) for out in outs],
        in_specs=[in_place()] * 3 + [whole_block()] * 11,
        out_specs=[in_place()] * 14 + [whole_block()],
        scratch_shapes=[
            pltpu.VMEM((seq, width), BF16),
            pltpu.VMEM(*attn),
            *[pltpu.VMEM(*one) for one in kept],
            pltpu.VMEM((seq, LANES), F32),
            pltpu.VMEM((rows, attn_cols), BF16),
            pltpu.VMEM((rows, 2 * gate.shape[1]), BF16),
            pltpu.VMEM(gate.shape, F32),
            pltpu.VMEM(up.shape, F32),
            pltpu.VMEM((4, seq // 4, seq), F32),
            pltpu.VMEM((count, 8, 2 * LANES), F32),
            pltpu.VMEM((seq, width), F32),
            pltpu.VMEM((seq, width), F32),
            *TensorSum.scratch(seq, width, 4, F32),
            dma((count,)),
            dma((count,)),
            dma((16,)),
            *Gather.sems(count),
            *Gather.sems(count),
        ],
        compiler_params=pltpu.CompilerParams(
            collective_id=1, has_side_effects=True, vmem_limit_bytes=61 << 20
        ),
    )(x, gate, up, seg_row, pos_row, turns, g1, g2, gq, gk, wq, wk, wv, wot)


def store(ref, rows, value):
    ref[rows, :] = value


def store_apart(gate, up, rows, value):
    even = gate.shape[1] // LANES
    for index in range(even):
        cols = pl.ds(index * LANES, LANES)
        gate[rows, cols] = value[:, 2 * index * LANES : (2 * index + 1) * LANES]
        up[rows, cols] = value[:, (2 * index + 1) * LANES : (2 * index + 2) * LANES]
    if gate.shape[1] % LANES:
        rest = value[:, 2 * even * LANES :]
        cols = pl.ds(even * LANES, HALF)
        gate[rows, cols] = rest[:, :HALF]
        up[rows, cols] = pltpu.roll(rest, HALF, 1)[:, :HALF]


class Scatter:
    def __init__(self, place, partial, result, late, scratch, flight=2, source=None):
        self.place, self.partial = place, partial
        self.flight = flight
        self.source = partial if source is None else source
        self.put = result if callable(result) else functools.partial(store, result)
        self.rows = partial.shape[0] // place.count
        self.late = late
        early = self.rows - late
        half = (early // 2 + 15) // 16 * 16
        self.cuts = [(0, half), (half, early - half)] if early > half else [(0, early)]
        self.tail = (early, late)
        self.over_in, self.far_in, self.far_other, self.late_in = scratch[:4]
        self.zsend, self.zrecv, self.ysend, self.yrecv, self.lsend, self.lrecv = scratch[4:]
        self.sent = []
        depth = place.depth
        orders = [
            sorted(range(depth), key=lambda goal, far=far: (-abs(goal - far), -goal)) for far in range(depth)
        ]
        self.goals = []
        for index in range(depth):
            goal = jnp.int32(0)
            for far in range(depth):
                goal = goal + orders[far][index] * (place.far == far).astype(jnp.int32)
            self.goals.append(goal)
        self.pieces = [(index, cut) for index in range(depth) for cut in range(len(self.cuts))]

    @staticmethod
    def scratch(count, rows, width, late):
        depth = count // NEAR
        dma = pltpu.SemaphoreType.DMA
        return [
            pltpu.VMEM((depth, rows - late, width), BF16),
            pltpu.VMEM((depth + 2, rows, width), BF16),
            pltpu.VMEM((depth + 2, max(late, 16), width), BF16),
            pltpu.VMEM((max(late, 16), width), BF16),
            dma((depth - 1, 4)),
            dma((depth + 2, 4)),
            dma((depth, 2)),
            dma((depth, 2)),
            dma,
            dma,
        ]

    def spot(self, goal, other, start, size):
        near = 1 - self.place.near if other else self.place.near
        return pl.ds(pl.multiple_of((goal * NEAR + near) * self.rows + start, 16), size)

    def over(self, number):
        place = self.place
        index, cut = self.pieces[number]
        start, size = self.cuts[cut]
        return remote(
            self.source.at[self.spot(self.goals[index], True, start, size), :],
            self.over_in.at[index, pl.ds(start, size), :],
            self.ysend.at[index, cut], self.yrecv.at[index, cut], place.beside, place.tensor,
        )

    def cross(self, number):
        if number < len(self.pieces):
            self.over(number).start()
            self.sent.append(lambda: self.over(number))

    def start(self):
        self.start_far()
        self.start_near()

    def start_near(self):
        for number in range(self.flight):
            self.cross(number)

    def start_far(self):
        if self.late:
            for index in range(self.place.depth - 1):
                for item in (2, 3):
                    pl.when(jnp.logical_not(self.fed(index)))(lambda index=index, item=item: self.hop(index, item).start())

    def add(self, spot, sources):
        size = sources[0].shape[0]
        part = 32 if size % 32 == 0 else 16

        def body(index, carry):
            start = pl.multiple_of(index * part, 16)
            rows = pl.ds(pl.multiple_of(spot.start + start, 16), part)
            total = self.partial[rows, :].astype(F32)
            for source in sources:
                total = total + source[pl.ds(start, part), :].astype(F32)
            self.partial[rows, :] = total.astype(BF16)
            return carry

        lax.fori_loop(0, size // part, body, 0)

    def item(self, item):
        return (0, *self.cuts[item]) if item < 2 else (item - 2, *self.tail)

    def into(self, slot, item):
        other, start, size = self.item(item)
        return self.far_other.at[slot] if other else self.far_in.at[slot, pl.ds(start, size), :]

    def wait_far(self, slot, item):
        place = self.place
        into = self.into(slot, item)
        remote(
            into, into, self.zsend.at[0, item], self.zrecv.at[slot, item], place.me, place.tensor
        ).wait_recv()
        return into

    def hop(self, index, item):
        place = self.place
        goal = self.goals[index]
        sign = 2 * (goal > place.far).astype(jnp.int32) - 1
        ends = ((goal - place.far) * sign == 1).astype(jnp.int32)
        slot = goal + ends * (place.depth + (1 - sign) // 2 - goal)
        return remote(
            self.partial.at[self.spot(goal, *self.item(item)), :], self.into(slot, item),
            self.zsend.at[index, item], self.zrecv.at[slot, item], place.me + sign * NEAR, place.tensor,
        )

    def arrived(self, index, cut):
        number = index * len(self.cuts) + cut
        self.over(number).wait_recv()
        self.cross(number + self.flight)
        start, size = self.cuts[cut]
        return self.over_in.at[index, pl.ds(start, size), :]

    def fed(self, index):
        place = self.place
        up = self.goals[index] > place.far
        return (up & (place.far > 0)) | (jnp.logical_not(up) & (place.far < place.depth - 1))

    def pass_on(self, index, item, base):
        self.add(self.spot(self.goals[index], *self.item(item)), base)
        self.hop(index, item).start()

    def first(self, number):
        index, cut = self.pieces[number]
        came = self.arrived(index, cut)
        if index < self.place.depth - 1:
            pl.when(jnp.logical_not(self.fed(index)))(lambda: self.pass_on(index, cut, [came]))

    def then(self, index, item):
        base = [self.over_in.at[index, pl.ds(*self.cuts[item]), :]] if item < 2 else []
        pl.when(self.fed(index))(
            lambda: self.pass_on(index, item, base + [self.wait_far(self.goals[index], item)])
        )
        self.sent.append(lambda: self.hop(index, item))

    def close(self, item):
        place = self.place
        spot = self.spot(place.far, *self.item(item))
        for way, comes in enumerate((place.far > 0, place.far < place.depth - 1)):

            @pl.when(comes)
            def _(way=way):
                self.add(spot, [self.wait_far(place.depth + way, item)])

    def last(self):
        place = self.place
        return remote(
            self.partial.at[self.spot(place.far, True, *self.tail), :], self.late_in,
            self.lsend, self.lrecv, place.beside, place.tensor,
        )

    def far_steps(self):
        for index in range(self.place.depth - 1 if self.late else 0):
            for item in (2, 3):
                self.then(index, item)
            yield

    def steps(self, far=True):
        place = self.place
        cuts = len(self.cuts)
        passing = cuts * (place.depth - 1)
        for number in range(len(self.pieces) + cuts):
            if number < len(self.pieces):
                self.first(number)
            index = (number - 1) // cuts
            if far and self.late and number and (number - 1) % cuts == 0 and index < place.depth - 1:
                self.then(index, 2)
                self.then(index, 3)
            if cuts <= number < passing + cuts:
                self.then(*self.pieces[number - cuts])
            if number == len(self.pieces) - 1 and self.late:
                self.close(3)
                self.last().start()
                self.sent.append(self.last)
                self.close(2)
            if number >= passing + cuts:
                cut = number - passing - cuts
                start, size = self.cuts[cut]
                own = self.spot(place.far, 0, start, size)
                self.add(own, [self.over_in.at[place.depth - 1, pl.ds(start, size), :]])
                self.close(cut)
                self.put(pl.ds(start, size), self.partial[own, :].astype(F32))
            yield
        if self.late:
            start, size = self.tail
            self.last().wait_recv()
            self.put(
                pl.ds(start, size),
                self.partial[self.spot(place.far, 0, start, size), :].astype(F32) + self.late_in[...].astype(F32),
            )
            yield

    def settle(self):
        for make in self.sent:
            make().wait_send()


def mlp_kernel(count, shares, *refs):
    (
        n2_hbm, cot_hbm, gates_hbm, hq_hbm, pack_down,
        first_out, second_out, dn2_out, part_out, down_ref,
        n2_ref, cot_ref, dn2_part, dn2_ref, w1, w2, ab, hid, partial, near, chip, far, sum_sems, copy_sems, *rest,
    ) = refs
    place = Place(count)
    seq, width = n2_ref.shape
    both = w1.shape[1]
    even = both // (2 * LANES)
    split = first_out.shape[1]
    tile = seq // 4
    lanes = lane_ids()
    loads = [
        begin(src, dst, copy_sems.at[index])
        for index, (src, dst) in enumerate(((n2_hbm, n2_ref), (gates_hbm, w1), (cot_hbm, cot_ref)))
    ]
    place.greet(False, True)
    gather = Gather(place, pack_down, w2, shares[0], rest[:5])
    scatter = Scatter(place, partial, down_ref, shares[1], rest[5:])
    summed = TensorSum(place, dn2_part, dn2_ref, 4, (near, chip, far, sum_sems))
    gather.start()
    moves, sums, tensor = gather.steps(), scatter.steps(False), summed.steps()
    loads[0].wait()
    loads[1].wait()

    def gate_up(index):
        cols = pl.ds(pl.multiple_of(index * 2 * LANES, 2 * LANES), 2 * LANES)
        got = dot_nn(n2_ref[...], w1[:, cols])
        gate, up = got[:, :LANES], got[:, LANES:]
        sig = jax.nn.sigmoid(gate)
        act = gate * sig
        hid[:, pl.ds(pl.multiple_of(index * LANES, LANES), LANES)] = (act * up).astype(BF16)
        slope = up * sig * (1.0 + gate * (1.0 - sig))
        ab[:, cols] = jnp.concatenate([slope, act], axis=1).astype(BF16)

    polled(even, gate_up, (moves, {8: 1, 12: 1}))
    tail = pl.ds(2 * even * LANES, LANES)
    got = dot_nn(n2_ref[...], w1[:, tail])
    up = pltpu.roll(got, HALF, 1)
    sig = jax.nn.sigmoid(got)
    act = got * sig
    hid[:, pl.ds(even * LANES, LANES)] = jnp.where(lanes < HALF, act * up, 0.0).astype(BF16)
    slope = up * sig * (1.0 + got * (1.0 - sig))
    ab[:, tail] = jnp.where(lanes < HALF, slope, pltpu.roll(act, HALF, 1)).astype(BF16)
    loads[2].wait()

    def down_grad(index):
        rows = pl.ds(pl.multiple_of(index * 384, 384), 384)
        partial[rows, :] = dot_tn(cot_ref[:, rows], hid[...]).astype(BF16)

    polled(width // 384, down_grad, (moves, {1: 1, 3: 1}))
    scatter.start_far()
    drain(moves)
    drain(scatter.far_steps())
    gather.finish()
    scatter.start_near()

    def inner_grad(index):
        got = dot_nn(cot_ref[...], w2[:, pl.ds(pl.multiple_of(index * 2 * LANES, 2 * LANES), 2 * LANES)])
        for side in range(2):
            piece = got[:, side * LANES : (side + 1) * LANES]
            cols = pl.ds(pl.multiple_of(index * 4 * LANES + side * 2 * LANES, 2 * LANES), 2 * LANES)
            ab[:, cols] = (ab[:, cols].astype(F32) * jnp.concatenate([piece, piece], axis=1)).astype(BF16)

    polled(even // 2, inner_grad, (sums, {5: 1}))
    got = dot_nn(cot_ref[...], w2[:, pl.ds((even - 1) * LANES, 2 * LANES)])
    piece = got[:, :LANES]
    cols = pl.ds(2 * (even - 1) * LANES, 2 * LANES)
    ab[:, cols] = (ab[:, cols].astype(F32) * jnp.concatenate([piece, piece], axis=1)).astype(BF16)
    piece = got[:, LANES:]
    piece = jnp.where(lanes < HALF, piece, pltpu.roll(piece, HALF, 1))
    ab[:, tail] = (ab[:, tail].astype(F32) * piece).astype(BF16)

    base = begin(hq_hbm, cot_ref, copy_sems.at[2])

    def normed_grad(index):
        rows = pl.ds(pl.multiple_of(index * tile, tile), tile)
        dn2_part[rows, :] = dot_nt(ab[rows, :], w1[...]).astype(BF16)
        for at in range(4):

            @pl.when(index == at)
            def _(at=at):
                summed.send_core(at)
                ahead(sums, 1)
                if at:
                    ahead(tensor, 1)

    lax.fori_loop(0, 4, lambda index, carry: (normed_grad(index), carry)[1], 0)

    def output_part(index):
        rows = pl.ds(pl.multiple_of(index * 256, 256), 256)
        cot_ref[:, rows] = (dot_nt(hid[...], w2[rows, :]) + cot_ref[:, rows].astype(F32)).astype(BF16)

    base.wait()
    polled(width // 256, output_part, (sums, {2: 1, 5: 1}), (tensor, {5: 1}))
    saves = [begin(cot_ref, part_out, copy_sems.at[4])]

    def gates_grad(index):
        rows = pl.ds(pl.multiple_of(index * 384, 384), 384)
        for low, high in ((0, split), (split, both)):
            w1[rows, pl.ds(low, high - low)] = dot_tn(n2_ref[:, rows], ab[:, pl.ds(low, high - low)]).astype(BF16)

    polled(width // 384, gates_grad, (sums, every(4)), (tensor, {1: 1, 3: 1}))
    saves.append(begin(w1.at[:, pl.ds(0, split)], first_out, copy_sems.at[5]))
    saves.append(begin(w1.at[:, pl.ds(split, both - split)], second_out, copy_sems.at[6]))
    drain(tensor, sums)
    for index in range(4):
        summed.finish(index)
    saves.append(begin(dn2_ref, dn2_out, copy_sems.at[3]))
    for save in saves:
        save.wait()
    gather.settle()
    scatter.settle()
    summed.settle()


def mlp_call(count, n2, cot, full_gates, hq, pack_down):
    seq, width = n2.shape
    rows, down = pack_down.shape
    shares = late_share(rows, 1 / 6), late_share(rows, 1 / 4)
    both = full_gates.shape[1]
    split = 14 * LANES
    shape = jax.ShapeDtypeStruct
    dma = pltpu.SemaphoreType.DMA
    return pl.pallas_call(
        functools.partial(mlp_kernel, count, shares),
        out_shape=[
            shape((width, split), BF16),
            shape((width, both - split), BF16),
            shape((seq, width), BF16),
            shape((seq, width), BF16),
            shape((rows, down), F32),
        ],
        in_specs=[in_place()] * 5,
        out_specs=[in_place()] * 4 + [whole_block()],
        scratch_shapes=[
            *[pltpu.VMEM((seq, width), BF16)] * 4,
            pltpu.VMEM((width, both), BF16),
            pltpu.VMEM((width, down), BF16),
            pltpu.VMEM((seq, both), BF16),
            pltpu.VMEM((seq, down), BF16),
            pltpu.VMEM((width, down), BF16),
            *TensorSum.scratch(seq, width, 4, BF16),
            dma((7,)),
            *Gather.sems(count),
            *Scatter.scratch(count, rows, down, shares[1]),
        ],
        compiler_params=pltpu.CompilerParams(
            collective_id=2, has_side_effects=True, vmem_limit_bytes=61 << 20
        ),
    )(n2, cot, full_gates, hq, pack_down)


def middle_kernel(count, *refs):
    (
        part_in, dn2_hbm, h_hbm, cot_hbm, w0_hbm, ctx_hbm, gain_ref,
        dh_out, dm_out, dwo_out, gate_ref, up_ref, small_ref,
        partial, dn2_ref, h_ref, cot_ref, wo, ctx_ref, dh_ref, dm_ref, dwo_ref, dhb, copy_sems, *rest,
    ) = refs
    place = Place(count)
    seq, width = dn2_ref.shape
    q_cols = ctx_ref.shape[1]
    heads = q_cols // HALF
    group = heads // 2
    tile = seq // 4
    lanes = lane_ids()
    load = begin(part_in, partial, copy_sems.at[0])
    place.greet(False, False)
    put = functools.partial(store_apart, gate_ref, up_ref)
    scatter = Scatter(place, partial, put, late_share(gate_ref.shape[0], 1 / 6), rest, 3, part_in)
    scatter.start_near()
    load.wait()
    scatter.start_far()
    loads = [
        begin(src, dst, copy_sems.at[index + 1])
        for index, (src, dst) in enumerate(
            (
                (dn2_hbm, dn2_ref), (h_hbm, h_ref), (cot_hbm, cot_ref),
                (w0_hbm.at[:, pl.ds(w0_hbm.shape[1] - q_cols, q_cols)], wo), (ctx_hbm, ctx_ref),
            )
        )
    ]
    sums = scatter.steps()
    g2 = gain_ref[pl.ds(1, 1), :]
    for load in loads:
        load.wait()
    small_ref[...] = jnp.zeros_like(small_ref)

    def residual_grad(index, carry):
        rows = pl.ds(pl.multiple_of(index * 64, 64), 64)
        grad = dn2_ref[rows, :].astype(F32)
        h = h_ref[rows, :]
        inverse = lax.rsqrt(jnp.mean(h * h, axis=1, keepdims=True) + EPSILON)
        scaled = grad * g2
        inner = jnp.mean(scaled * h, axis=1, keepdims=True)
        dh = cot_ref[rows, :].astype(F32) + inverse * scaled - h * (inverse * inverse * inverse * inner)
        dh_ref[rows, :] = dh
        dhb[rows, :] = dh.astype(BF16)
        return carry + jnp.sum((grad * h * inverse).reshape(8, 8, width), axis=0)

    def back(index):
        small_ref[...] += lax.fori_loop(
            index * (tile // 64), (index + 1) * (tile // 64), residual_grad, jnp.zeros((8, width), F32)
        )
        rows = pl.ds(pl.multiple_of(index * tile, tile), tile)
        dctx = dot_nn(dhb[rows, :], wo[...])
        for pair in range(heads // 2):
            value = dctx[:, pair * LANES : (pair + 1) * LANES]
            swapped = pltpu.roll(value, HALF, 1)
            for side in range(2):
                head = 2 * pair + side
                keep = value if side == head // group else swapped
                dm_ref[head, rows, :] = jnp.where(lanes // HALF == head // group, keep, 0.0).astype(BF16)

    polled(4, back, (sums, {1: 1, 2: 1, 3: 1}))
    saves = [
        begin(dh_ref, dh_out, copy_sems.at[7]),
        begin(dm_ref, dm_out, copy_sems.at[8]),
    ]

    def out_grad(index):
        rows = pl.ds(pl.multiple_of(index * 384, 384), 384)
        dwo_ref[rows, :] = dot_tn(dhb[:, rows], ctx_ref[...]).astype(BF16)

    polled(width // 384, out_grad, (sums, {1: 1, 3: 1}))
    saves.append(begin(dwo_ref, dwo_out, copy_sems.at[10]))
    drain(sums)
    for save in saves:
        save.wait()
    scatter.settle()


def middle_call(count, part, dn2, h, cot, w0, ctx, gains):
    seq, width = dn2.shape
    q_cols = ctx.shape[1]
    rows = width // count
    shape = jax.ShapeDtypeStruct
    dma = pltpu.SemaphoreType.DMA
    return pl.pallas_call(
        functools.partial(middle_kernel, count),
        out_shape=[
            shape((seq, width), F32),
            shape((q_cols // HALF, seq, LANES), BF16),
            shape((width, q_cols), BF16),
            shape((rows, part.shape[1] // 2), F32),
            shape((rows, part.shape[1] // 2), F32),
            shape((8, width), F32),
        ],
        in_specs=[in_place()] * 6 + [whole_block()],
        out_specs=[in_place()] * 3 + [whole_block()] * 3,
        scratch_shapes=[
            pltpu.VMEM(part.shape, BF16),
            pltpu.VMEM((seq, width), BF16),
            pltpu.VMEM((seq, width), F32),
            pltpu.VMEM((seq, width), BF16),
            pltpu.VMEM((width, q_cols), BF16),
            pltpu.VMEM((seq, q_cols), BF16),
            pltpu.VMEM((seq, width), F32),
            pltpu.VMEM((q_cols // HALF, seq, LANES), BF16),
            pltpu.VMEM((width, q_cols), BF16),
            pltpu.VMEM((seq, width), BF16),
            dma((11,)),
            *Scatter.scratch(count, rows, part.shape[1], late_share(rows, 1 / 6)),
        ],
        compiler_params=pltpu.CompilerParams(
            collective_id=3, has_side_effects=True, vmem_limit_bytes=61 << 20
        ),
    )(part, dn2, h, cot, w0, ctx, gains)


def last_kernel(count, *refs):
    (
        part_in, dwo_in, dm_hbm, qm_hbm, kb_hbm, vb_hbm, lse_hbm, qk_hbm, n1_hbm, w0_hbm, x_hbm, dh_hbm,
        cos_hbm, sin_hbm, seg_row, gain_ref, two_ref,
        grad_out, gate_ref, up_ref, out_ref, qkv_ref, small_ref,
        partial, partial_o, dm_ref, qm_ref, kb_ref, vb_ref, lse_ref, qk_ref, n1_ref, wqkv, x_ref, dh_ref, cos_ref, sin_ref,
        column, partial_qkv, bias, dk, dv, head_sums, dlow, part, dn1_ref, small, slots, head_slots,
        near, chip, far, sum_sems, small_send, small_recv, copy_sems, *rest,
    ) = refs
    place = Place(count)
    seq, width = n1_ref.shape
    kv_cols = kb_ref.shape[1]
    q_cols = qk_ref.shape[1] - kv_cols
    pairs = q_cols // LANES
    group = (q_cols // HALF) // (kv_cols // HALF)
    tile = seq // 4
    own = width // count
    few = HALF // count
    lanes = lane_ids()
    sources = (
        (part_in, partial), (dwo_in, partial_o), (qm_hbm, qm_ref), (kb_hbm, kb_ref), (lse_hbm, lse_ref),
        (dm_hbm, dm_ref), (vb_hbm, vb_ref), (qk_hbm, qk_ref), (cos_hbm, cos_ref), (sin_hbm, sin_ref),
        (w0_hbm.at[:, pl.ds(0, wqkv.shape[1])], wqkv), (n1_hbm, n1_ref), (x_hbm, x_ref), (dh_hbm, dh_ref),
    )
    loads = [begin(src, dst, copy_sems.at[index]) for index, (src, dst) in enumerate(sources[:2])]
    place.greet(True, True)
    third = len(rest) // 3
    late = late_share(gate_ref.shape[0], 1 / 6)
    scatter = Scatter(place, partial, functools.partial(store_apart, gate_ref, up_ref), late, rest[:third], 3, part_in)
    scatter_o = Scatter(place, partial_o, out_ref, late, rest[third : 2 * third], 8)
    scatter_qkv = Scatter(place, partial_qkv, qkv_ref, late, rest[2 * third :], 8)
    final = TensorSum(place, part, dn1_ref, 4, (near, chip, far, sum_sems))
    scatter.start_near()
    for load in loads:
        load.wait()
    scatter.start_far()
    loads = [begin(src, dst, copy_sems.at[index + 2]) for index, (src, dst) in enumerate(sources[2:])]
    column_of(seg_row, column)
    sums, sums_o = scatter.steps(), scatter_o.steps()
    dk[...] = jnp.zeros_like(dk)
    dv[...] = jnp.zeros_like(dv)
    gq = gain_ref[pl.ds(2, 1), pl.ds(0, LANES)]
    gk = gain_ref[pl.ds(3, 1), pl.ds(0, LANES)]
    for load in loads[:9]:
        load.wait()

    def head_back(grad, raw, cosine, sine, gain):
        back = turn(grad, cosine, -sine)
        inverse = lax.rsqrt(head_mean(raw * raw) + EPSILON)
        scaled = back * gain
        inner = head_mean(scaled * raw)
        low = inverse * scaled - raw * (inverse * inverse * inverse * inner)
        return low.astype(BF16), jnp.sum((back * raw * inverse).reshape(-1, 8, LANES), axis=0)

    head_sums[...] = jnp.zeros_like(head_sums)
    turns = {3: every(3), 2: every(3), 1: {0: 1, 2: 1}, 0: {2: 1}}
    for qb in reversed(range(4)):
        last = (qb + 1) * tile
        rows = pl.ds(qb * tile, tile)
        bias_block(column, seg_row, bias, qb * tile, tile)

        def attend_back(pair, last=last, rows=rows):
            keys = pl.ds(0, last)
            sides = []
            for side in range(2):
                head = 2 * pair + side
                kv = head // group
                query, grad = qm_ref[head, rows, :], dm_ref[head, rows, :]
                logsum = jnp.sum(jnp.where(lanes == head, lse_ref[rows, :], 0.0), axis=1, keepdims=True)
                logits = dot_nt(query, kb_ref[keys, :]) + bias[:, keys]
                probs = jnp.exp(logits - logsum)
                dprob = dot_nt(grad, vb_ref[keys, :])
                inner = jnp.sum(probs * dprob, axis=1, keepdims=True)
                ds = (probs * (dprob - inner)).astype(BF16)
                got = dot_nn(ds, kb_ref[keys, :]) * 0.125
                sides.append(jnp.where(kv == side, got, pltpu.roll(got, HALF, 1)))
                dk[keys, :] += dot_tn(ds, query)
                dv[keys, :] += dot_tn(probs.astype(BF16), grad)
            cols = pl.ds(pl.multiple_of(pair * LANES, LANES), LANES)
            low, terms = head_back(
                jnp.where(lanes < HALF, sides[0], sides[1]), qk_ref[rows, cols], cos_ref[rows, :], sin_ref[rows, :], gq
            )
            dlow[rows, cols] = low
            head_sums[pl.ds(0, 8), :] += terms

        polled(pairs, attend_back, (sums, turns[qb]))
        low, terms = head_back(
            dk[rows, :], qk_ref[rows, pl.ds(q_cols, LANES)], cos_ref[rows, :], sin_ref[rows, :], gk
        )
        dlow[rows, pl.ds(q_cols, LANES)] = low
        dlow[rows, pl.ds(q_cols + LANES, LANES)] = dv[rows, :].astype(BF16)
        head_sums[pl.ds(8, 8), :] += terms
        part[rows, :] = dot_nt(dlow[rows, :], wqkv[...]).astype(BF16)
        final.send_core(qb)
        if qb < 3:
            final.send_back(qb + 1)
        final.send_across(qb)
        if qb == 2:
            scatter_o.start()
        if qb < 2:
            ahead(sums_o, 2)
    mine = head_slots.at[place.tensor]
    mine[...] = head_sums[...]
    head_copies = []
    for step in range(1, 4):
        copy = remote(
            mine, mine, small_send.at[step - 1], small_recv.at[step - 1], place.me, lax.rem(place.tensor + step, 4)
        )
        copy.start()
        head_copies.append(copy)
    for load in loads[9:]:
        load.wait()

    def qkv_grad(start):
        partial_qkv[pl.ds(start, 384), :] = dot_tn(n1_ref[:, pl.ds(start, 384)], dlow[...]).astype(BF16)

    blocks(width, 384, qkv_grad)
    scatter_qkv.start()
    sums_qkv = scatter_qkv.steps()
    for step, copy in enumerate(head_copies):
        whose = head_slots.at[lax.rem(place.tensor + 3 - step, 4)]
        remote(whose, whose, small_send.at[step], small_recv.at[step], place.me, place.tensor).wait_recv()
    heads = head_slots[0] + head_slots[1] + head_slots[2] + head_slots[3]
    ahead(sums_o, 2)
    g1 = gain_ref[pl.ds(0, 1), :]
    gain_one = jnp.zeros((8, width), F32)
    saves = []
    for index in reversed(range(4)):
        if index == 0:
            final.send_back(0)
        ahead(sums, 1)
        ahead(sums_o, 1)
        ahead(sums_qkv, 1)
        final.finish(index)

        def input_grad(sub, carry, index=index):
            rows = pl.ds(pl.multiple_of(index * tile + sub * 64, 64), 64)
            grad = dn1_ref[rows, :].astype(F32)
            x = x_ref[rows, :].astype(F32)
            inverse = lax.rsqrt(jnp.mean(x * x, axis=1, keepdims=True) + EPSILON)
            scaled = grad * g1
            inner = jnp.mean(scaled * x, axis=1, keepdims=True)
            dh_ref[rows, :] = dh_ref[rows, :] + inverse * scaled - x * (inverse * inverse * inverse * inner)
            return carry + jnp.sum((grad * x * inverse).reshape(8, 8, width), axis=0)

        gain_one = lax.fori_loop(0, tile // 64, input_grad, gain_one)
        rows = pl.ds(index * tile, tile)
        saves.append(begin(dh_ref.at[rows, :], grad_out.at[rows, :], copy_sems.at[index]))
    one = jnp.sum(gain_one, axis=0, keepdims=True)
    two = jnp.sum(two_ref[...], axis=0, keepdims=True)
    small[...] = jnp.zeros_like(small)
    q_sum = jnp.sum(heads[:8], axis=0, keepdims=True)
    k_sum = jnp.sum(heads[8:], axis=0, keepdims=True)
    q_sum = q_sum + pltpu.roll(q_sum, HALF, 1)
    k_sum = k_sum + pltpu.roll(k_sum, HALF, 1)

    def small_copy(d):
        return remote(
            small.at[d], slots.at[place.me], small_send.at[3 + d], small_recv.at[3 + place.me], d, place.tensor
        )

    for d in range(count):
        for row, (values, size) in enumerate(((one, own), (two, own), (q_sum, few), (k_sum, few))):
            small[d, pl.ds(row, 1), pl.ds(0, size)] = values[:, d * size : (d + 1) * size]
        pl.when(place.me != d)(lambda d=d: small_copy(d).start())
    slots[place.me] = small[place.me]
    drain(sums, sums_o, sums_qkv)
    for d in range(count):

        @pl.when(place.me != d)
        def _(d=d):
            remote(
                slots.at[d], slots.at[d], small_send.at[3 + d], small_recv.at[3 + d], d, place.tensor
            ).wait_recv()

    total = slots[0]
    for d in range(1, count):
        total = total + slots[d]
    small_ref[...] = total
    for d in range(count):
        pl.when(place.me != d)(lambda d=d: small_copy(d).wait_send())
    for save in saves:
        save.wait()
    for copy in head_copies:
        copy.wait_send()
    for each in (scatter, scatter_o, scatter_qkv, final):
        each.settle()


def last_call(count, part, dwo, dm, qm, kb, vb, lse, qk, n1, w0, x, dh, cosine, sine, seg_row, gains, two):
    seq, width = n1.shape
    rows = width // count
    q_cols = dwo.shape[1]
    low = qk.shape[1] + LANES
    shape = jax.ShapeDtypeStruct
    dma = pltpu.SemaphoreType.DMA
    loaded = [part, dwo, dm, qm, kb, vb, lse, qk, n1, jax.ShapeDtypeStruct((width, low), BF16), x, dh, cosine, sine]
    small = (8, 2 * LANES)
    return pl.pallas_call(
        functools.partial(last_kernel, count),
        out_shape=[
            shape((seq, width), F32),
            shape((rows, part.shape[1] // 2), F32),
            shape((rows, part.shape[1] // 2), F32),
            shape((rows, q_cols), F32),
            shape((rows, low), F32),
            shape(small, F32),
        ],
        in_specs=[in_place()] * 14 + [whole_block()] * 3,
        out_specs=[in_place()] + [whole_block()] * 5,
        scratch_shapes=[
            *[pltpu.VMEM(one.shape, one.dtype) for one in loaded],
            pltpu.VMEM((seq, LANES), F32),
            pltpu.VMEM((width, low), BF16),
            pltpu.VMEM((seq // 4, seq), F32),
            pltpu.VMEM((seq, LANES), F32),
            pltpu.VMEM((seq, LANES), F32),
            pltpu.VMEM((16, LANES), F32),
            pltpu.VMEM((seq, low), BF16),
            pltpu.VMEM((seq, width), BF16),
            pltpu.VMEM((seq, width), BF16),
            pltpu.VMEM((count,) + small, F32),
            pltpu.VMEM((count,) + small, F32),
            pltpu.VMEM((4, 16, LANES), F32),
            *TensorSum.scratch(seq, width, 4, BF16),
            dma((count + 3,)),
            dma((count + 3,)),
            dma((14,)),
            *Scatter.scratch(count, rows, part.shape[1], late_share(rows, 1 / 6)),
            *Scatter.scratch(count, rows, q_cols, late_share(rows, 1 / 6)),
            *Scatter.scratch(count, rows, low, late_share(rows, 1 / 6)),
        ],
        compiler_params=pltpu.CompilerParams(
            collective_id=4, has_side_effects=True, vmem_limit_bytes=61 << 20
        ),
    )(part, dwo, dm, qm, kb, vb, lse, qk, n1, w0, x, dh, cosine, sine, seg_row, gains, two)


def rotary_rows():
    lane = np.arange(LANES)
    frequency = ROPE_BASE ** (-(lane % (HALF // 2)) * 2.0 / HALF)
    sign = np.where(lane % HALF < HALF // 2, -1.0, 1.0)
    return jnp.asarray(np.concatenate([frequency[None], sign[None], np.zeros((6, LANES))]).astype(np.float32))


def shards(
    block_input,
    segments,
    positions,
    norm1_gain,
    q_norm_gain,
    k_norm_gain,
    w_q,
    w_k,
    w_v,
    w_o,
    norm2_gain,
    w_gate,
    w_up,
    w_down,
    cotangent,
    *,
    n_dp,
    n_tensor,
):
    rows = w_q.shape[0]
    q_cols, kv_cols, ff_cols = w_q.shape[1], w_k.shape[1], w_gate.shape[1]
    small_gain = q_norm_gain.shape[0]
    seg_row, pos_row = segments[None, :], positions[None, :]
    pack_down = jnp.pad(w_down.T.astype(BF16), ((0, 0), (0, -ff_cols % LANES)))
    w0, w1, n1, qk, qm, kb, vb, lse, ctx, h, n2, cosine, sine, hq, gains = forward_call(
        n_dp, block_input, w_gate, w_up, seg_row, pos_row, rotary_rows(),
        norm1_gain[None, :], norm2_gain[None, :], q_norm_gain[None, :], k_norm_gain[None, :],
        w_q, w_k, w_v, w_o.T.astype(BF16),
    )
    first, second, dn2, mlp, down = mlp_call(n_dp, n2, cotangent, w1, hq, pack_down)
    output_rows = lax.psum(mlp, "tensor")
    dh, dm, dwo, gate_one, up_one, small_two = middle_call(
        n_dp, first, dn2, h, cotangent, w0, ctx, gains
    )
    grad_input, gate_two, up_two, grad_o, grad_qkv, small = last_call(
        n_dp, second, dwo, dm, qm, kb, vb, lse, qk, n1, w0, block_input, dh,
        cosine, sine, seg_row, gains, small_two,
    )
    return (
        output_rows,
        grad_input,
        small[0, :rows],
        small[2, :small_gain],
        small[3, :small_gain],
        grad_qkv[:, :q_cols],
        grad_qkv[:, q_cols : q_cols + kv_cols],
        grad_qkv[:, q_cols + kv_cols :],
        grad_o.T,
        small[1, :rows],
        jnp.concatenate([gate_one, gate_two], axis=1),
        jnp.concatenate([up_one, up_two], axis=1),
        down[:, :ff_cols].T,
    )


def solution(mesh):
    placed = (
        P("dp", None),
        P("dp"),
        P("dp"),
        P("dp"),
        P("dp"),
        P("dp"),
        P("dp", "tensor"),
        P("dp", "tensor"),
        P("dp", "tensor"),
        P("tensor", "dp"),
        P("dp"),
        P("dp", "tensor"),
        P("dp", "tensor"),
        P("tensor", "dp"),
        P("dp", None),
    )
    return jax.shard_map(
        functools.partial(shards, n_dp=mesh.shape["dp"], n_tensor=mesh.shape["tensor"]),
        mesh=mesh,
        in_specs=placed,
        out_specs=(
            P("dp", None),
            P("dp", None),
            P("dp"),
            P("dp"),
            P("dp"),
            P("dp", "tensor"),
            P("dp", "tensor"),
            P("dp", "tensor"),
            P("tensor", "dp"),
            P("dp"),
            P("dp", "tensor"),
            P("dp", "tensor"),
            P("tensor", "dp"),
        ),
        check_vma=False,
    )
```

```python
import functools

import jax
import jax.numpy as jnp
import numpy as np
from jax import lax
from jax.experimental import pallas as pl
from jax.experimental.pallas import tpu as pltpu
from jax.sharding import PartitionSpec as P

EPSILON = 1e-05
ROPE_BASE = 1000000.0
MASKED = -1e30


MESH = pl.DeviceIdType.MESH
NEAR = 2
HALF = 64
LANES = 128
HIGHEST = lax.Precision.HIGHEST
BF16 = jnp.bfloat16
F32 = jnp.float32


def whole_block():
    return pl.BlockSpec(memory_space=pltpu.VMEM)


def in_place():
    return pl.BlockSpec(memory_space=pl.ANY)


def remote(src, dst, send, recv, dp, tensor):
    return pltpu.make_async_remote_copy(
        src_ref=src,
        dst_ref=dst,
        send_sem=send,
        recv_sem=recv,
        device_id=(dp, tensor),
        device_id_type=MESH,
    )


def begin(src, dst, sem):
    copy = pltpu.make_async_copy(src, dst, sem)
    copy.start()
    return copy


def dot_nn(left, right):
    return jnp.dot(left, right, preferred_element_type=F32)


def dot_nt(left, right):
    return lax.dot_general(left, right, (((1,), (1,)), ((), ())), preferred_element_type=F32)


def dot_tn(left, right):
    return lax.dot_general(left, right, (((0,), (0,)), ((), ())), preferred_element_type=F32)


class Place:
    def __init__(self, count):
        self.count = count
        self.depth = count // NEAR
        self.me = lax.axis_index("dp")
        self.tensor = lax.axis_index("tensor")
        self.far = self.me // NEAR
        self.near = lax.rem(self.me, NEAR)
        self.core = lax.rem(self.tensor, 2)
        self.mate = self.tensor + 1 - 2 * self.core
        self.across = lax.rem(self.tensor + 2, 4)
        self.beside = self.me + 1 - 2 * self.near

    def ahead(self, step):
        return lax.rem(self.far + step, self.depth)

    def behind(self, step):
        return lax.rem(self.far + self.depth - step, self.depth)

    def greet(self, everyone, tensor):
        barrier = pltpu.get_barrier_semaphore()
        peers = []
        if everyone:
            peers += [(lax.rem(self.me + d, self.count), self.tensor) for d in range(1, self.count)]
        else:
            peers += [
                (self.ahead(step) * NEAR + self.near, self.tensor) for step in range(1, self.depth)
            ]
            peers.append((self.beside, self.tensor))
        if tensor:
            peers += [(self.me, lax.rem(self.tensor + t, 4)) for t in range(1, 4)]
        for peer in peers:
            pl.semaphore_signal(barrier, 1, device_id=peer, device_id_type=MESH)
        pl.semaphore_wait(barrier, len(peers))


class Gather:
    def __init__(self, place, shard, full, late, sems):
        self.place, self.shard, self.full = place, shard, full
        self.rows = shard.shape[0]
        self.cuts = [(0, self.rows - late)] + ([(self.rows - late, late)] if late else [])
        self.zsend, self.zrecv, self.ysend, self.yrecv, self.own = sems
        self.sent = []

    @staticmethod
    def sems(count):
        depth = count // NEAR
        dma = pltpu.SemaphoreType.DMA
        return [dma((2, depth - 1, 3)), dma((2, depth - 1, 3)), dma((2 * depth - 1, 2)), dma((2 * depth - 1, 2)), dma]

    def spot(self, block, cut):
        start, size = self.cuts[cut]
        return self.full.at[pl.ds(pl.multiple_of(block * self.rows + start, 16), size), :]

    def mine(self, cut):
        start, size = self.cuts[cut]
        return self.shard.at[pl.ds(start, size), :]

    def block(self, way, step, other):
        far = self.place.far - step if way == 0 else self.place.far + step
        return far * NEAR + (1 - self.place.near if other else self.place.near)

    def valid(self, way, step):
        return self.place.far >= step if way == 0 else self.place.far + step < self.place.depth

    def emit(self, make):
        copy, when = make()
        if when is None:
            copy.start()
        else:
            pl.when(when)(copy.start)
        self.sent.append(make)

    def along(self, way, step, cut, other, turn=None):
        place = self.place
        if step >= place.depth - 1:
            return

        def make():
            more = place.far < place.depth - 1 if way == 0 else place.far > 0
            spot = self.spot(self.block(way, step, other), cut)
            copy = remote(
                self.mine(cut) if step == 0 and not other else spot, spot,
                self.zsend.at[way, step, cut + other], self.zrecv.at[way, step, cut + other],
                place.me + (NEAR if way == 0 else -NEAR), place.tensor,
            )
            when = more if step == 0 else more & self.valid(way, step)
            return copy, when if turn is None else when & turn()

        self.emit(make)

    def crossing(self, way, step, cut, other):
        place = self.place
        spot = self.spot(self.block(way, step, other), cut)
        slot = step if way == 0 else step + place.depth - 1
        return remote(
            self.mine(cut) if step == 0 and not other else spot, spot,
            self.ysend.at[slot, cut], self.yrecv.at[slot, cut], place.beside, place.tensor,
        ), (self.valid(way, step) if step else None)

    def over(self, way, step, cut):
        self.emit(lambda: self.crossing(way, step, cut, 0))

    def came_over(self, way, step, cut):
        copy, when = self.crossing(way, step, cut, 1)
        if when is None:
            copy.wait_recv()
        else:
            pl.when(when)(copy.wait_recv)

    def start(self):
        place = self.place
        self.local = lambda: pltpu.make_async_copy(
            self.shard, self.full.at[pl.ds(pl.multiple_of(place.me * self.rows, 16), self.rows), :], self.own
        )
        self.local().start()
        for cut in reversed(range(len(self.cuts))):
            self.over(0, 0, cut)
        for way in range(2):
            self.along(way, 0, 0, 0)
            if len(self.cuts) > 1:
                self.along(way, 0, 1, 0, lambda way=way: jnp.logical_not(self.valid(way, 1)))

    def ends(self, way, step):
        return self.valid(way, step) & jnp.logical_not(self.valid(way, step + 1))

    def arrive(self, way, step, cut, other):
        place = self.place
        spot = self.spot(self.block(way, step, other), cut)
        copy = remote(
            spot, spot, self.zsend.at[way, step - 1, cut + other], self.zrecv.at[way, step - 1, cut + other],
            place.me, place.tensor,
        )
        pl.when(self.valid(way, step))(copy.wait_recv)
        self.along(way, step, cut, other)

    def steps(self):
        late = len(self.cuts) > 1
        if late:
            self.came_over(0, 0, 1)
            for way in range(2):
                self.along(way, 0, 1, 1, lambda way=way: jnp.logical_not(self.valid(way, 1)))
            yield
        for step in range(1, self.place.depth):
            for way in range(2):
                self.arrive(way, step, 0, 0)
                self.over(way, step, 0)
                if late:
                    for other in range(2):
                        self.along(way, 0, 1, other, lambda way=way, step=step: self.ends(way, step))
                yield
        if late:
            for step in range(1, self.place.depth):
                for other in range(2):
                    for way in range(2):
                        self.arrive(way, step, 1, other)
                    yield

    def finish(self):
        self.came_over(0, 0, 0)
        for step in range(1, self.place.depth):
            for way in range(2):
                self.came_over(way, step, 0)
        self.local().wait()

    def settle(self):
        for make in self.sent:
            copy, when = make()
            if when is None:
                copy.wait_send()
            else:
                pl.when(when)(copy.wait_send)


def late_share(rows, share):
    return int(rows * share) // 16 * 16


class TensorSum:
    def __init__(self, place, part, total, tiles, scratch):
        self.place, self.part, self.total, self.tiles = place, part, total, tiles
        self.tile = part.shape[0] // tiles
        self.half = self.tile // 2
        self.near, self.chip, self.far, self.sems = scratch
        self.sent = []

    @staticmethod
    def scratch(rows, width, tiles, kind):
        half = (rows // 2, width)
        return [
            pltpu.VMEM(half, kind), pltpu.VMEM(half, BF16), pltpu.VMEM(half, BF16), pltpu.SemaphoreType.DMA((6, tiles))
        ]

    def half_rows(self, index, which):
        return pl.ds(pl.multiple_of(index * self.tile + which * self.half, 16), self.half)

    def slot(self, index):
        return pl.ds(index * self.half, self.half)

    def core_copy(self, index):
        place = self.place
        return remote(
            self.part.at[self.half_rows(index, 1 - place.core), :], self.near.at[self.slot(index), :],
            self.sems.at[0, index], self.sems.at[1, index], place.me, place.mate,
        )

    def across_copy(self, index):
        place = self.place
        return remote(
            self.chip.at[self.slot(index), :], self.far.at[self.slot(index), :],
            self.sems.at[2, index], self.sems.at[3, index], place.me, place.across,
        )

    def back_copy(self, index, which):
        place = self.place
        rows = self.half_rows(index, which)
        return remote(
            self.total.at[rows, :], self.total.at[rows, :],
            self.sems.at[4, index], self.sems.at[5, index], place.me, place.mate,
        )

    def send_core(self, index):
        self.core_copy(index).start()
        self.sent.append(lambda: self.core_copy(index))

    def send_across(self, index):
        place = self.place
        self.core_copy(index).wait_recv()
        mine = self.part[self.half_rows(index, place.core), :].astype(F32)
        self.chip[self.slot(index), :] = (mine + self.near[self.slot(index), :].astype(F32)).astype(BF16)
        self.across_copy(index).start()
        self.sent.append(lambda: self.across_copy(index))

    def send_back(self, index):
        place = self.place
        self.across_copy(index).wait_recv()
        both = self.chip[self.slot(index), :].astype(F32) + self.far[self.slot(index), :].astype(F32)
        self.total[self.half_rows(index, place.core), :] = both.astype(self.total.dtype)
        self.back_copy(index, place.core).start()

    def finish(self, index):
        self.back_copy(index, 1 - self.place.core).wait_recv()
        self.back_copy(index, self.place.core).wait_send()

    def steps(self):
        for index in range(2):
            self.send_across(index)
            yield
        for index in range(self.tiles):
            self.send_back(index)
            if index + 2 < self.tiles:
                self.send_across(index + 2)
            yield

    def settle(self):
        for make in self.sent:
            make().wait_send()


def lane_ids(width=LANES):
    return lax.broadcasted_iota(jnp.int32, (1, width), 1)


def head_mean(values):
    row = lax.broadcasted_iota(jnp.int32, (LANES, LANES), 0)
    col = lax.broadcasted_iota(jnp.int32, (LANES, LANES), 1)
    groups = jnp.where(row // HALF == col // HALF, 1.0 / HALF, 0.0).astype(F32)
    return jnp.dot(values, groups, precision=HIGHEST, preferred_element_type=F32)


def turn(values, cosine, sine):
    ahead = pltpu.roll(values, LANES - HALF // 2, 1)
    back = pltpu.roll(values, HALF // 2, 1)
    first = lax.rem(lane_ids(), HALF) < HALF // 2
    return values * cosine + jnp.where(first, ahead, back) * sine


def column_of(row_ref, column):
    for index in range(row_ref.shape[1] // LANES):
        spot = pl.ds(index * LANES, LANES)
        row = row_ref[:, spot].astype(F32)
        column[spot, :] = jnp.broadcast_to(row, (LANES, LANES)).T


def bias_block(seg_col, seg_row, bias, first, tile):
    last = first + tile
    rows = lax.broadcasted_iota(jnp.int32, (tile, last), 0) + first
    cols = lax.broadcasted_iota(jnp.int32, (tile, last), 1)
    same = seg_col[pl.ds(first, tile), pl.ds(0, 1)] == seg_row[:, pl.ds(0, last)].astype(F32)
    allowed = same & (rows >= cols)
    bias[:, pl.ds(0, last)] = jnp.where(allowed, 0.0, MASKED)


def drain(*moves):
    for one in moves:
        for _ in one:
            pass


def ahead(moves, count=1):
    for _ in range(count):
        next(moves, None)


def polled(count, body, *polls):
    def step(index, carry):
        body(index)
        for at in range(count):
            due = [(moves, times[at]) for moves, times in polls if at in times]
            if due:

                @pl.when(index == at)
                def _(due=due):
                    for moves, times in due:
                        ahead(moves, times)

        return carry

    lax.fori_loop(0, count, step, 0)


def every(count, times=1, first=0):
    return {index: times for index in range(first, count)}


def blocks(total, size, body):
    def step(index, carry):
        body(pl.multiple_of(index * size, size))
        return carry

    lax.fori_loop(0, total // size, step, 0)


def forward_kernel(count, *refs):
    (
        x_hbm, gate_hbm, up_hbm, seg_row, pos_row, turn_ref, g1_ref, g2_ref, gq_ref, gk_ref,
        wq_ref, wk_ref, wv_ref, wot_ref,
        full_attn, full_gates, n1_out, qk_out, qm_out, kb_out, vb_out, lse_out, ctx_out, h_out, n2_out, cos_out, sin_out, hq_out,
        gains_out,
        x_ref, w0, n1_ref, qk_ref, qm_ref, kb_ref, vb_ref, lse_ref, ctx_ref, h_ref, n2_ref, cos_ref, sin_ref, hq_ref,
        column, pack_attn, pack_gates, gate_ref, up_ref, bias, gain_slots, part, total, tmp_near, tmp_chip, tmp_far, sum_sems, gain_send, gain_recv, copy_sems,
        *gather_sems,
    ) = refs
    place = Place(count)
    seq, width = x_ref.shape
    q_cols = ctx_ref.shape[1]
    kv_cols = kb_ref.shape[1]
    pairs = q_cols // LANES
    group = (q_cols // HALF) // (kv_cols // HALF)
    tile = seq // 4
    load = begin(x_hbm, x_ref, copy_sems.at[0])
    weights = [begin(gate_hbm, gate_ref, copy_sems.at[11]), begin(up_hbm, up_ref, copy_sems.at[12])]
    spot = 0
    for ref in (wq_ref, wk_ref, wv_ref, wot_ref):
        pack_attn[:, pl.ds(spot, ref.shape[1])] = ref[...].astype(BF16)
        spot += ref.shape[1]
    gain_slots[place.me] = jnp.zeros(gain_slots.shape[1:], F32)
    for row, ref in enumerate((g1_ref, g2_ref, gq_ref, gk_ref)):
        gain_slots[place.me, pl.ds(row, 1), pl.ds(0, ref.shape[1])] = ref[...].astype(BF16).astype(F32)
    place.greet(True, True)
    first = Gather(place, pack_attn, w0, late_share(pack_attn.shape[0], 1 / 6), gather_sems[:5])
    second = Gather(place, pack_gates, full_gates, late_share(pack_gates.shape[0], 1 / 6), gather_sems[5:])
    first.start()
    gain_copies = []
    for step in range(1, count):
        copy = remote(
            gain_slots.at[place.me], gain_slots.at[place.me], gain_send.at[step], gain_recv.at[step],
            lax.rem(place.me + step, count), place.tensor,
        )
        copy.start()
        gain_copies.append(copy)
    for weight in weights:
        weight.wait()
    even = gate_ref.shape[1] // LANES

    def lay(index, carry):
        cols = pl.ds(pl.multiple_of(index * LANES, LANES), LANES)
        for side, ref in enumerate((gate_ref, up_ref)):
            spot = pl.multiple_of((2 * index + side) * LANES, LANES)
            pack_gates[:, pl.ds(spot, LANES)] = ref[:, cols].astype(BF16)
        return carry

    lax.fori_loop(0, even, lay, 0)
    rest = pl.ds(even * LANES, HALF)
    pack_gates[:, pl.ds(2 * even * LANES, LANES)] = jnp.concatenate(
        [gate_ref[:, rest], up_ref[:, rest]], axis=1
    ).astype(BF16)
    column_of(pos_row, column)

    def angles(index, carry):
        rows = pl.ds(pl.multiple_of(index * LANES, LANES), LANES)
        angle = column[rows, pl.ds(0, 1)] * turn_ref[pl.ds(0, 1), :]
        cos_ref[rows, :] = jnp.cos(angle)
        sin_ref[rows, :] = jnp.sin(angle) * turn_ref[pl.ds(1, 1), :]
        return carry

    lax.fori_loop(0, seq // LANES, angles, 0)
    column_of(seg_row, column)
    for qb in range(4):
        bias_block(column, seg_row, bias.at[qb], qb * tile, tile)
    for step in range(1, count):
        whose = gain_slots.at[lax.rem(place.me + count - step, count)]
        remote(whose, whose, gain_send.at[step], gain_recv.at[step], place.me, place.tensor).wait_recv()
    gains_out[...] = jnp.zeros_like(gains_out)
    own = width // count
    for row in range(2):
        gains_out[pl.ds(row, 1), :] = jnp.concatenate(
            [gain_slots[d, pl.ds(row, 1), pl.ds(0, own)] for d in range(count)], axis=1
        )
    for row in range(2, 4):
        gains_out[pl.ds(row, 1), pl.ds(0, LANES)] = jnp.concatenate(
            [gain_slots[d, pl.ds(row, 1), pl.ds(0, HALF // count)] for d in range(count)] * 2, axis=1
        )
    moves_first = first.steps()
    ahead(moves_first, 2)
    g1 = gains_out[pl.ds(0, 1), :]
    g2 = gains_out[pl.ds(1, 1), :]
    load.wait()

    def norm_one(index, carry):
        rows = pl.ds(pl.multiple_of(index * LANES, LANES), LANES)
        x = x_ref[rows, :].astype(F32)
        inverse = lax.rsqrt(jnp.mean(x * x, axis=1, keepdims=True) + EPSILON)
        n1_ref[rows, :] = (x * inverse * g1).astype(BF16)
        return carry

    lax.fori_loop(0, seq // LANES, norm_one, 0)
    saves = [
        begin(n1_ref, n1_out, copy_sems.at[1]),
        begin(cos_ref, cos_out, copy_sems.at[13]),
        begin(sin_ref, sin_out, copy_sems.at[14]),
    ]
    drain(moves_first)
    second.start()
    moves = second.steps()
    first.finish()
    saves.append(begin(w0, full_attn, copy_sems.at[2]))
    gq = gains_out[pl.ds(2, 1), pl.ds(0, LANES)]
    gk = gains_out[pl.ds(3, 1), pl.ds(0, LANES)]
    lanes = lane_ids()

    def project(index, carry):
        rows = pl.ds(pl.multiple_of(index * tile, tile), tile)
        qkv = dot_nn(n1_ref[rows, :], w0[:, pl.ds(0, q_cols + 2 * kv_cols)])
        qk_ref[rows, :] = qkv[:, : q_cols + kv_cols]
        vb_ref[rows, :] = qkv[:, q_cols + kv_cols :].astype(BF16)
        cosine, sine = cos_ref[rows, :], sin_ref[rows, :]
        for pair in range(pairs + 1):
            raw = qkv[:, pair * LANES : (pair + 1) * LANES]
            inverse = lax.rsqrt(head_mean(raw * raw) + EPSILON)
            turned = turn(raw * inverse * (gk if pair == pairs else gq), cosine, sine)
            if pair == pairs:
                kb_ref[rows, :] = turned.astype(BF16)
                continue
            swapped = pltpu.roll(turned, HALF, 1)
            for side in range(2):
                head = 2 * pair + side
                kv = head // group
                keep = (turned if side == kv else swapped).astype(BF16) * 0.125
                qm_ref[head, rows, :] = jnp.where(lanes // HALF == kv, keep, jnp.zeros_like(keep))
        return carry

    lax.fori_loop(0, 4, project, 0)
    for index, (src, dst) in enumerate(((qk_ref, qk_out), (qm_ref, qm_out), (kb_ref, kb_out), (vb_ref, vb_out))):
        saves.append(begin(src, dst, copy_sems.at[3 + index]))
    next(moves, None)

    for qb in range(4):
        last = (qb + 1) * tile
        rows = pl.ds(qb * tile, tile)

        def attend(pair, carry, last=last, rows=rows, qb=qb):
            halves, sums = [], []
            for side in range(2):
                head = 2 * pair + side
                kv = head // group
                logits = dot_nt(qm_ref[head, rows, :], kb_ref[pl.ds(0, last), :]) + bias[qb, :, pl.ds(0, last)]
                top = jnp.max(logits, axis=1, keepdims=True)
                expo = jnp.exp(logits - top)
                summed = jnp.sum(expo, axis=1, keepdims=True)
                probs = (expo * (1.0 / summed)).astype(BF16)
                got = dot_nn(probs, vb_ref[pl.ds(0, last), :])
                halves.append(jnp.where(kv == side, got, pltpu.roll(got, HALF, 1)))
                sums.append(top + jnp.log(summed))
            ctx_ref[rows, pl.ds(pl.multiple_of(pair * LANES, LANES), LANES)] = jnp.where(
                lanes < HALF, halves[0], halves[1]
            ).astype(BF16)
            carry = jnp.where(lanes == 2 * pair, sums[0], carry)
            return jnp.where(lanes == 2 * pair + 1, sums[1], carry)

        lse_ref[rows, :] = lax.fori_loop(0, pairs, attend, jnp.zeros((tile, LANES), F32))
        if qb > 1:
            next(moves, None)
    saves.append(begin(lse_ref, lse_out, copy_sems.at[7]))
    saves.append(begin(ctx_ref, ctx_out, copy_sems.at[8]))

    summed = TensorSum(place, part, total, 4, (tmp_near, tmp_chip, tmp_far, sum_sems))
    for index in range(4):
        rows = pl.ds(index * tile, tile)
        part[rows, :] = dot_nt(ctx_ref[rows, :], w0[:, pl.ds(q_cols + 2 * kv_cols, q_cols)])
        summed.send_core(index)
    summed.send_across(0)
    summed.send_across(1)
    next(moves, None)
    for index in range(4):
        summed.send_back(index)
        if index < 2:
            summed.send_across(index + 2)
        next(moves, None)
        summed.finish(index)

        def norm_two(sub, carry, index=index):
            rows = pl.ds(pl.multiple_of(index * tile + sub * LANES, LANES), LANES)
            h = x_ref[rows, :].astype(F32) + total[rows, :]
            h_ref[rows, :] = h
            hq_ref[rows, :] = (h * 0.25).astype(BF16)
            inverse = lax.rsqrt(jnp.mean(h * h, axis=1, keepdims=True) + EPSILON)
            n2_ref[rows, :] = (h * inverse * g2).astype(BF16)
            return carry

        lax.fori_loop(0, tile // LANES, norm_two, 0)
        next(moves, None)
    saves.append(begin(h_ref, h_out, copy_sems.at[9]))
    saves.append(begin(n2_ref, n2_out, copy_sems.at[10]))
    saves.append(begin(hq_ref, hq_out, copy_sems.at[15]))
    drain(moves)
    second.finish()
    for save in saves:
        save.wait()
    for copy in gain_copies:
        copy.wait_send()
    first.settle()
    second.settle()
    summed.settle()


def forward_call(count, x, gate, up, seg_row, pos_row, turns, g1, g2, gq, gk, wq, wk, wv, wot):
    seq, width = x.shape
    rows = wq.shape[0]
    q_cols, kv_cols = wq.shape[1], LANES
    attn_cols = wq.shape[1] + wk.shape[1] + wv.shape[1] + wot.shape[1]
    kept = [
        ((seq, width), BF16),
        ((seq, q_cols + kv_cols), F32),
        ((q_cols // HALF, seq, LANES), BF16),
        ((seq, LANES), BF16),
        ((seq, LANES), BF16),
        ((seq, LANES), F32),
        ((seq, q_cols), BF16),
        ((seq, width), F32),
        ((seq, width), BF16),
        ((seq, LANES), F32),
        ((seq, LANES), F32),
        ((seq, width), BF16),
    ]
    attn = ((count * rows, attn_cols), BF16)
    outs = [attn, ((count * rows, 2 * gate.shape[1]), BF16), *kept, ((8, width), F32)]
    dma = pltpu.SemaphoreType.DMA
    return pl.pallas_call(
        functools.partial(forward_kernel, count),
        out_shape=[jax.ShapeDtypeStruct(*out) for out in outs],
        in_specs=[in_place()] * 3 + [whole_block()] * 11,
        out_specs=[in_place()] * 14 + [whole_block()],
        scratch_shapes=[
            pltpu.VMEM((seq, width), BF16),
            pltpu.VMEM(*attn),
            *[pltpu.VMEM(*one) for one in kept],
            pltpu.VMEM((seq, LANES), F32),
            pltpu.VMEM((rows, attn_cols), BF16),
            pltpu.VMEM((rows, 2 * gate.shape[1]), BF16),
            pltpu.VMEM(gate.shape, F32),
            pltpu.VMEM(up.shape, F32),
            pltpu.VMEM((4, seq // 4, seq), F32),
            pltpu.VMEM((count, 8, 2 * LANES), F32),
            pltpu.VMEM((seq, width), F32),
            pltpu.VMEM((seq, width), F32),
            *TensorSum.scratch(seq, width, 4, F32),
            dma((count,)),
            dma((count,)),
            dma((16,)),
            *Gather.sems(count),
            *Gather.sems(count),
        ],
        compiler_params=pltpu.CompilerParams(
            collective_id=1, has_side_effects=True, vmem_limit_bytes=61 << 20
        ),
    )(x, gate, up, seg_row, pos_row, turns, g1, g2, gq, gk, wq, wk, wv, wot)


def store(ref, rows, value):
    ref[rows, :] = value


def store_apart(gate, up, rows, value):
    even = gate.shape[1] // LANES
    for index in range(even):
        cols = pl.ds(index * LANES, LANES)
        gate[rows, cols] = value[:, 2 * index * LANES : (2 * index + 1) * LANES]
        up[rows, cols] = value[:, (2 * index + 1) * LANES : (2 * index + 2) * LANES]
    if gate.shape[1] % LANES:
        rest = value[:, 2 * even * LANES :]
        cols = pl.ds(even * LANES, HALF)
        gate[rows, cols] = rest[:, :HALF]
        up[rows, cols] = pltpu.roll(rest, HALF, 1)[:, :HALF]


class Scatter:
    def __init__(self, place, partial, result, late, scratch, flight=2, source=None):
        self.place, self.partial = place, partial
        self.flight = flight
        self.source = partial if source is None else source
        self.put = result if callable(result) else functools.partial(store, result)
        self.rows = partial.shape[0] // place.count
        self.late = late
        early = self.rows - late
        half = (early // 2 + 15) // 16 * 16
        self.cuts = [(0, half), (half, early - half)] if early > half else [(0, early)]
        self.tail = (early, late)
        self.over_in, self.far_in, self.far_other, self.late_in = scratch[:4]
        self.zsend, self.zrecv, self.ysend, self.yrecv, self.lsend, self.lrecv = scratch[4:]
        self.sent = []
        depth = place.depth
        orders = [
            sorted(range(depth), key=lambda goal, far=far: (-abs(goal - far), -goal)) for far in range(depth)
        ]
        self.goals = []
        for index in range(depth):
            goal = jnp.int32(0)
            for far in range(depth):
                goal = goal + orders[far][index] * (place.far == far).astype(jnp.int32)
            self.goals.append(goal)
        self.pieces = [(index, cut) for index in range(depth) for cut in range(len(self.cuts))]

    @staticmethod
    def scratch(count, rows, width, late):
        depth = count // NEAR
        dma = pltpu.SemaphoreType.DMA
        return [
            pltpu.VMEM((depth, rows - late, width), BF16),
            pltpu.VMEM((depth + 2, rows, width), BF16),
            pltpu.VMEM((depth + 2, max(late, 16), width), BF16),
            pltpu.VMEM((max(late, 16), width), BF16),
            dma((depth - 1, 4)),
            dma((depth + 2, 4)),
            dma((depth, 2)),
            dma((depth, 2)),
            dma,
            dma,
        ]

    def spot(self, goal, other, start, size):
        near = 1 - self.place.near if other else self.place.near
        return pl.ds(pl.multiple_of((goal * NEAR + near) * self.rows + start, 16), size)

    def over(self, number):
        place = self.place
        index, cut = self.pieces[number]
        start, size = self.cuts[cut]
        return remote(
            self.source.at[self.spot(self.goals[index], True, start, size), :],
            self.over_in.at[index, pl.ds(start, size), :],
            self.ysend.at[index, cut], self.yrecv.at[index, cut], place.beside, place.tensor,
        )

    def cross(self, number):
        if number < len(self.pieces):
            self.over(number).start()
            self.sent.append(lambda: self.over(number))

    def start(self):
        self.start_far()
        self.start_near()

    def start_near(self):
        for number in range(self.flight):
            self.cross(number)

    def start_far(self):
        if self.late:
            for index in range(self.place.depth - 1):
                for item in (2, 3):
                    pl.when(jnp.logical_not(self.fed(index)))(lambda index=index, item=item: self.hop(index, item).start())

    def add(self, spot, sources):
        size = sources[0].shape[0]
        part = 32 if size % 32 == 0 else 16

        def body(index, carry):
            start = pl.multiple_of(index * part, 16)
            rows = pl.ds(pl.multiple_of(spot.start + start, 16), part)
            total = self.partial[rows, :].astype(F32)
            for source in sources:
                total = total + source[pl.ds(start, part), :].astype(F32)
            self.partial[rows, :] = total.astype(BF16)
            return carry

        lax.fori_loop(0, size // part, body, 0)

    def item(self, item):
        return (0, *self.cuts[item]) if item < 2 else (item - 2, *self.tail)

    def into(self, slot, item):
        other, start, size = self.item(item)
        return self.far_other.at[slot] if other else self.far_in.at[slot, pl.ds(start, size), :]

    def wait_far(self, slot, item):
        place = self.place
        into = self.into(slot, item)
        remote(
            into, into, self.zsend.at[0, item], self.zrecv.at[slot, item], place.me, place.tensor
        ).wait_recv()
        return into

    def hop(self, index, item):
        place = self.place
        goal = self.goals[index]
        sign = 2 * (goal > place.far).astype(jnp.int32) - 1
        ends = ((goal - place.far) * sign == 1).astype(jnp.int32)
        slot = goal + ends * (place.depth + (1 - sign) // 2 - goal)
        return remote(
            self.partial.at[self.spot(goal, *self.item(item)), :], self.into(slot, item),
            self.zsend.at[index, item], self.zrecv.at[slot, item], place.me + sign * NEAR, place.tensor,
        )

    def arrived(self, index, cut):
        number = index * len(self.cuts) + cut
        self.over(number).wait_recv()
        self.cross(number + self.flight)
        start, size = self.cuts[cut]
        return self.over_in.at[index, pl.ds(start, size), :]

    def fed(self, index):
        place = self.place
        up = self.goals[index] > place.far
        return (up & (place.far > 0)) | (jnp.logical_not(up) & (place.far < place.depth - 1))

    def pass_on(self, index, item, base):
        self.add(self.spot(self.goals[index], *self.item(item)), base)
        self.hop(index, item).start()

    def first(self, number):
        index, cut = self.pieces[number]
        came = self.arrived(index, cut)
        if index < self.place.depth - 1:
            pl.when(jnp.logical_not(self.fed(index)))(lambda: self.pass_on(index, cut, [came]))

    def then(self, index, item):
        base = [self.over_in.at[index, pl.ds(*self.cuts[item]), :]] if item < 2 else []
        pl.when(self.fed(index))(
            lambda: self.pass_on(index, item, base + [self.wait_far(self.goals[index], item)])
        )
        self.sent.append(lambda: self.hop(index, item))

    def close(self, item):
        place = self.place
        spot = self.spot(place.far, *self.item(item))
        for way, comes in enumerate((place.far > 0, place.far < place.depth - 1)):

            @pl.when(comes)
            def _(way=way):
                self.add(spot, [self.wait_far(place.depth + way, item)])

    def last(self):
        place = self.place
        return remote(
            self.partial.at[self.spot(place.far, True, *self.tail), :], self.late_in,
            self.lsend, self.lrecv, place.beside, place.tensor,
        )

    def far_steps(self):
        for index in range(self.place.depth - 1 if self.late else 0):
            for item in (2, 3):
                self.then(index, item)
            yield

    def steps(self, far=True):
        place = self.place
        cuts = len(self.cuts)
        passing = cuts * (place.depth - 1)
        for number in range(len(self.pieces) + cuts):
            if number < len(self.pieces):
                self.first(number)
            index = (number - 1) // cuts
            if far and self.late and number and (number - 1) % cuts == 0 and index < place.depth - 1:
                self.then(index, 2)
                self.then(index, 3)
            if cuts <= number < passing + cuts:
                self.then(*self.pieces[number - cuts])
            if number == len(self.pieces) - 1 and self.late:
                self.close(3)
                self.last().start()
                self.sent.append(self.last)
                self.close(2)
            if number >= passing + cuts:
                cut = number - passing - cuts
                start, size = self.cuts[cut]
                own = self.spot(place.far, 0, start, size)
                self.add(own, [self.over_in.at[place.depth - 1, pl.ds(start, size), :]])
                self.close(cut)
                self.put(pl.ds(start, size), self.partial[own, :].astype(F32))
            yield
        if self.late:
            start, size = self.tail
            self.last().wait_recv()
            self.put(
                pl.ds(start, size),
                self.partial[self.spot(place.far, 0, start, size), :].astype(F32) + self.late_in[...].astype(F32),
            )
            yield

    def settle(self):
        for make in self.sent:
            make().wait_send()


def mlp_kernel(count, shares, *refs):
    (
        n2_hbm, cot_hbm, gates_hbm, hq_hbm, pack_down,
        first_out, second_out, dn2_out, part_out, down_ref,
        n2_ref, cot_ref, dn2_part, dn2_ref, w1, w2, ab, hid, partial, near, chip, far, sum_sems, copy_sems, *rest,
    ) = refs
    place = Place(count)
    seq, width = n2_ref.shape
    both = w1.shape[1]
    even = both // (2 * LANES)
    split = first_out.shape[1]
    tile = seq // 4
    lanes = lane_ids()
    loads = [
        begin(src, dst, copy_sems.at[index])
        for index, (src, dst) in enumerate(((n2_hbm, n2_ref), (gates_hbm, w1), (cot_hbm, cot_ref)))
    ]
    place.greet(False, True)
    gather = Gather(place, pack_down, w2, shares[0], rest[:5])
    scatter = Scatter(place, partial, down_ref, shares[1], rest[5:])
    summed = TensorSum(place, dn2_part, dn2_ref, 4, (near, chip, far, sum_sems))
    gather.start()
    moves, sums, tensor = gather.steps(), scatter.steps(False), summed.steps()
    loads[0].wait()
    loads[1].wait()

    def gate_up(index):
        cols = pl.ds(pl.multiple_of(index * 2 * LANES, 2 * LANES), 2 * LANES)
        got = dot_nn(n2_ref[...], w1[:, cols])
        gate, up = got[:, :LANES], got[:, LANES:]
        sig = jax.nn.sigmoid(gate)
        act = gate * sig
        hid[:, pl.ds(pl.multiple_of(index * LANES, LANES), LANES)] = (act * up).astype(BF16)
        slope = up * sig * (1.0 + gate * (1.0 - sig))
        ab[:, cols] = jnp.concatenate([slope, act], axis=1).astype(BF16)

    polled(even, gate_up, (moves, {8: 1, 12: 1}))
    tail = pl.ds(2 * even * LANES, LANES)
    got = dot_nn(n2_ref[...], w1[:, tail])
    up = pltpu.roll(got, HALF, 1)
    sig = jax.nn.sigmoid(got)
    act = got * sig
    hid[:, pl.ds(even * LANES, LANES)] = jnp.where(lanes < HALF, act * up, 0.0).astype(BF16)
    slope = up * sig * (1.0 + got * (1.0 - sig))
    ab[:, tail] = jnp.where(lanes < HALF, slope, pltpu.roll(act, HALF, 1)).astype(BF16)
    loads[2].wait()

    def down_grad(index):
        rows = pl.ds(pl.multiple_of(index * 384, 384), 384)
        partial[rows, :] = dot_tn(cot_ref[:, rows], hid[...]).astype(BF16)

    polled(width // 384, down_grad, (moves, {1: 1, 3: 1}))
    scatter.start_far()
    drain(moves)
    drain(scatter.far_steps())
    gather.finish()
    scatter.start_near()

    def inner_grad(index):
        got = dot_nn(cot_ref[...], w2[:, pl.ds(pl.multiple_of(index * 2 * LANES, 2 * LANES), 2 * LANES)])
        for side in range(2):
            piece = got[:, side * LANES : (side + 1) * LANES]
            cols = pl.ds(pl.multiple_of(index * 4 * LANES + side * 2 * LANES, 2 * LANES), 2 * LANES)
            ab[:, cols] = (ab[:, cols].astype(F32) * jnp.concatenate([piece, piece], axis=1)).astype(BF16)

    polled(even // 2, inner_grad, (sums, {5: 1}))
    got = dot_nn(cot_ref[...], w2[:, pl.ds((even - 1) * LANES, 2 * LANES)])
    piece = got[:, :LANES]
    cols = pl.ds(2 * (even - 1) * LANES, 2 * LANES)
    ab[:, cols] = (ab[:, cols].astype(F32) * jnp.concatenate([piece, piece], axis=1)).astype(BF16)
    piece = got[:, LANES:]
    piece = jnp.where(lanes < HALF, piece, pltpu.roll(piece, HALF, 1))
    ab[:, tail] = (ab[:, tail].astype(F32) * piece).astype(BF16)

    base = begin(hq_hbm, cot_ref, copy_sems.at[2])

    def normed_grad(index):
        rows = pl.ds(pl.multiple_of(index * tile, tile), tile)
        dn2_part[rows, :] = dot_nt(ab[rows, :], w1[...]).astype(BF16)
        for at in range(4):

            @pl.when(index == at)
            def _(at=at):
                summed.send_core(at)
                ahead(sums, 1)
                if at:
                    ahead(tensor, 1)

    lax.fori_loop(0, 4, lambda index, carry: (normed_grad(index), carry)[1], 0)

    def output_part(index):
        rows = pl.ds(pl.multiple_of(index * 256, 256), 256)
        cot_ref[:, rows] = (dot_nt(hid[...], w2[rows, :]) + cot_ref[:, rows].astype(F32)).astype(BF16)

    base.wait()
    polled(width // 256, output_part, (sums, {2: 1, 5: 1}), (tensor, {5: 1}))
    saves = [begin(cot_ref, part_out, copy_sems.at[4])]

    def gates_grad(index):
        rows = pl.ds(pl.multiple_of(index * 384, 384), 384)
        for low, high in ((0, split), (split, both)):
            w1[rows, pl.ds(low, high - low)] = dot_tn(n2_ref[:, rows], ab[:, pl.ds(low, high - low)]).astype(BF16)

    polled(width // 384, gates_grad, (sums, every(4)), (tensor, {1: 1, 3: 1}))
    saves.append(begin(w1.at[:, pl.ds(0, split)], first_out, copy_sems.at[5]))
    saves.append(begin(w1.at[:, pl.ds(split, both - split)], second_out, copy_sems.at[6]))
    drain(tensor, sums)
    for index in range(4):
        summed.finish(index)
    saves.append(begin(dn2_ref, dn2_out, copy_sems.at[3]))
    for save in saves:
        save.wait()
    gather.settle()
    scatter.settle()
    summed.settle()


def mlp_call(count, n2, cot, full_gates, hq, pack_down):
    seq, width = n2.shape
    rows, down = pack_down.shape
    shares = late_share(rows, 1 / 6), late_share(rows, 1 / 4)
    both = full_gates.shape[1]
    split = 14 * LANES
    shape = jax.ShapeDtypeStruct
    dma = pltpu.SemaphoreType.DMA
    return pl.pallas_call(
        functools.partial(mlp_kernel, count, shares),
        out_shape=[
            shape((width, split), BF16),
            shape((width, both - split), BF16),
            shape((seq, width), BF16),
            shape((seq, width), BF16),
            shape((rows, down), F32),
        ],
        in_specs=[in_place()] * 5,
        out_specs=[in_place()] * 4 + [whole_block()],
        scratch_shapes=[
            *[pltpu.VMEM((seq, width), BF16)] * 4,
            pltpu.VMEM((width, both), BF16),
            pltpu.VMEM((width, down), BF16),
            pltpu.VMEM((seq, both), BF16),
            pltpu.VMEM((seq, down), BF16),
            pltpu.VMEM((width, down), BF16),
            *TensorSum.scratch(seq, width, 4, BF16),
            dma((7,)),
            *Gather.sems(count),
            *Scatter.scratch(count, rows, down, shares[1]),
        ],
        compiler_params=pltpu.CompilerParams(
            collective_id=2, has_side_effects=True, vmem_limit_bytes=61 << 20
        ),
    )(n2, cot, full_gates, hq, pack_down)


def middle_kernel(count, *refs):
    (
        part_in, dn2_hbm, h_hbm, cot_hbm, w0_hbm, ctx_hbm, gain_ref,
        dh_out, dm_out, dwo_out, gate_ref, up_ref, small_ref,
        partial, dn2_ref, h_ref, cot_ref, wo, ctx_ref, dh_ref, dm_ref, dwo_ref, dhb, copy_sems, *rest,
    ) = refs
    place = Place(count)
    seq, width = dn2_ref.shape
    q_cols = ctx_ref.shape[1]
    heads = q_cols // HALF
    group = heads // 2
    tile = seq // 4
    lanes = lane_ids()
    load = begin(part_in, partial, copy_sems.at[0])
    place.greet(False, False)
    put = functools.partial(store_apart, gate_ref, up_ref)
    scatter = Scatter(place, partial, put, late_share(gate_ref.shape[0], 1 / 6), rest, 3, part_in)
    scatter.start_near()
    load.wait()
    scatter.start_far()
    loads = [
        begin(src, dst, copy_sems.at[index + 1])
        for index, (src, dst) in enumerate(
            (
                (dn2_hbm, dn2_ref), (h_hbm, h_ref), (cot_hbm, cot_ref),
                (w0_hbm.at[:, pl.ds(w0_hbm.shape[1] - q_cols, q_cols)], wo), (ctx_hbm, ctx_ref),
            )
        )
    ]
    sums = scatter.steps()
    g2 = gain_ref[pl.ds(1, 1), :]
    for load in loads:
        load.wait()
    small_ref[...] = jnp.zeros_like(small_ref)

    def residual_grad(index, carry):
        rows = pl.ds(pl.multiple_of(index * 64, 64), 64)
        grad = dn2_ref[rows, :].astype(F32)
        h = h_ref[rows, :]
        inverse = lax.rsqrt(jnp.mean(h * h, axis=1, keepdims=True) + EPSILON)
        scaled = grad * g2
        inner = jnp.mean(scaled * h, axis=1, keepdims=True)
        dh = cot_ref[rows, :].astype(F32) + inverse * scaled - h * (inverse * inverse * inverse * inner)
        dh_ref[rows, :] = dh
        dhb[rows, :] = dh.astype(BF16)
        return carry + jnp.sum((grad * h * inverse).reshape(8, 8, width), axis=0)

    def back(index):
        small_ref[...] += lax.fori_loop(
            index * (tile // 64), (index + 1) * (tile // 64), residual_grad, jnp.zeros((8, width), F32)
        )
        rows = pl.ds(pl.multiple_of(index * tile, tile), tile)
        dctx = dot_nn(dhb[rows, :], wo[...])
        for pair in range(heads // 2):
            value = dctx[:, pair * LANES : (pair + 1) * LANES]
            swapped = pltpu.roll(value, HALF, 1)
            for side in range(2):
                head = 2 * pair + side
                keep = value if side == head // group else swapped
                dm_ref[head, rows, :] = jnp.where(lanes // HALF == head // group, keep, 0.0).astype(BF16)

    polled(4, back, (sums, {1: 1, 2: 1, 3: 1}))
    saves = [
        begin(dh_ref, dh_out, copy_sems.at[7]),
        begin(dm_ref, dm_out, copy_sems.at[8]),
    ]

    def out_grad(index):
        rows = pl.ds(pl.multiple_of(index * 384, 384), 384)
        dwo_ref[rows, :] = dot_tn(dhb[:, rows], ctx_ref[...]).astype(BF16)

    polled(width // 384, out_grad, (sums, {1: 1, 3: 1}))
    saves.append(begin(dwo_ref, dwo_out, copy_sems.at[10]))
    drain(sums)
    for save in saves:
        save.wait()
    scatter.settle()


def middle_call(count, part, dn2, h, cot, w0, ctx, gains):
    seq, width = dn2.shape
    q_cols = ctx.shape[1]
    rows = width // count
    shape = jax.ShapeDtypeStruct
    dma = pltpu.SemaphoreType.DMA
    return pl.pallas_call(
        functools.partial(middle_kernel, count),
        out_shape=[
            shape((seq, width), F32),
            shape((q_cols // HALF, seq, LANES), BF16),
            shape((width, q_cols), BF16),
            shape((rows, part.shape[1] // 2), F32),
            shape((rows, part.shape[1] // 2), F32),
            shape((8, width), F32),
        ],
        in_specs=[in_place()] * 6 + [whole_block()],
        out_specs=[in_place()] * 3 + [whole_block()] * 3,
        scratch_shapes=[
            pltpu.VMEM(part.shape, BF16),
            pltpu.VMEM((seq, width), BF16),
            pltpu.VMEM((seq, width), F32),
            pltpu.VMEM((seq, width), BF16),
            pltpu.VMEM((width, q_cols), BF16),
            pltpu.VMEM((seq, q_cols), BF16),
            pltpu.VMEM((seq, width), F32),
            pltpu.VMEM((q_cols // HALF, seq, LANES), BF16),
            pltpu.VMEM((width, q_cols), BF16),
            pltpu.VMEM((seq, width), BF16),
            dma((11,)),
            *Scatter.scratch(count, rows, part.shape[1], late_share(rows, 1 / 6)),
        ],
        compiler_params=pltpu.CompilerParams(
            collective_id=3, has_side_effects=True, vmem_limit_bytes=61 << 20
        ),
    )(part, dn2, h, cot, w0, ctx, gains)


def last_kernel(count, *refs):
    (
        part_in, dwo_in, dm_hbm, qm_hbm, kb_hbm, vb_hbm, lse_hbm, qk_hbm, n1_hbm, w0_hbm, x_hbm, dh_hbm,
        cos_hbm, sin_hbm, seg_row, gain_ref, two_ref,
        grad_out, gate_ref, up_ref, out_ref, qkv_ref, small_ref,
        partial, partial_o, dm_ref, qm_ref, kb_ref, vb_ref, lse_ref, qk_ref, n1_ref, wqkv, x_ref, dh_ref, cos_ref, sin_ref,
        column, partial_qkv, bias, dk, dv, head_sums, dlow, part, dn1_ref, small, slots, head_slots,
        near, chip, far, sum_sems, small_send, small_recv, copy_sems, *rest,
    ) = refs
    place = Place(count)
    seq, width = n1_ref.shape
    kv_cols = kb_ref.shape[1]
    q_cols = qk_ref.shape[1] - kv_cols
    pairs = q_cols // LANES
    group = (q_cols // HALF) // (kv_cols // HALF)
    tile = seq // 4
    own = width // count
    few = HALF // count
    lanes = lane_ids()
    sources = (
        (part_in, partial), (dwo_in, partial_o), (qm_hbm, qm_ref), (kb_hbm, kb_ref), (lse_hbm, lse_ref),
        (dm_hbm, dm_ref), (vb_hbm, vb_ref), (qk_hbm, qk_ref), (cos_hbm, cos_ref), (sin_hbm, sin_ref),
        (w0_hbm.at[:, pl.ds(0, wqkv.shape[1])], wqkv), (n1_hbm, n1_ref), (x_hbm, x_ref), (dh_hbm, dh_ref),
    )
    loads = [begin(src, dst, copy_sems.at[index]) for index, (src, dst) in enumerate(sources[:2])]
    place.greet(True, True)
    third = len(rest) // 3
    late = late_share(gate_ref.shape[0], 1 / 6)
    scatter = Scatter(place, partial, functools.partial(store_apart, gate_ref, up_ref), late, rest[:third], 3, part_in)
    scatter_o = Scatter(place, partial_o, out_ref, late, rest[third : 2 * third], 8)
    scatter_qkv = Scatter(place, partial_qkv, qkv_ref, late, rest[2 * third :], 8)
    final = TensorSum(place, part, dn1_ref, 4, (near, chip, far, sum_sems))
    scatter.start_near()
    for load in loads:
        load.wait()
    scatter.start_far()
    loads = [begin(src, dst, copy_sems.at[index + 2]) for index, (src, dst) in enumerate(sources[2:])]
    column_of(seg_row, column)
    sums, sums_o = scatter.steps(), scatter_o.steps()
    dk[...] = jnp.zeros_like(dk)
    dv[...] = jnp.zeros_like(dv)
    gq = gain_ref[pl.ds(2, 1), pl.ds(0, LANES)]
    gk = gain_ref[pl.ds(3, 1), pl.ds(0, LANES)]
    for load in loads[:9]:
        load.wait()

    def head_back(grad, raw, cosine, sine, gain):
        back = turn(grad, cosine, -sine)
        inverse = lax.rsqrt(head_mean(raw * raw) + EPSILON)
        scaled = back * gain
        inner = head_mean(scaled * raw)
        low = inverse * scaled - raw * (inverse * inverse * inverse * inner)
        return low.astype(BF16), jnp.sum((back * raw * inverse).reshape(-1, 8, LANES), axis=0)

    head_sums[...] = jnp.zeros_like(head_sums)
    turns = {3: every(3), 2: every(3), 1: {0: 1, 2: 1}, 0: {2: 1}}
    for qb in reversed(range(4)):
        last = (qb + 1) * tile
        rows = pl.ds(qb * tile, tile)
        bias_block(column, seg_row, bias, qb * tile, tile)

        def attend_back(pair, last=last, rows=rows):
            keys = pl.ds(0, last)
            sides = []
            for side in range(2):
                head = 2 * pair + side
                kv = head // group
                query, grad = qm_ref[head, rows, :], dm_ref[head, rows, :]
                logsum = jnp.sum(jnp.where(lanes == head, lse_ref[rows, :], 0.0), axis=1, keepdims=True)
                logits = dot_nt(query, kb_ref[keys, :]) + bias[:, keys]
                probs = jnp.exp(logits - logsum)
                dprob = dot_nt(grad, vb_ref[keys, :])
                inner = jnp.sum(probs * dprob, axis=1, keepdims=True)
                ds = (probs * (dprob - inner)).astype(BF16)
                got = dot_nn(ds, kb_ref[keys, :]) * 0.125
                sides.append(jnp.where(kv == side, got, pltpu.roll(got, HALF, 1)))
                dk[keys, :] += dot_tn(ds, query)
                dv[keys, :] += dot_tn(probs.astype(BF16), grad)
            cols = pl.ds(pl.multiple_of(pair * LANES, LANES), LANES)
            low, terms = head_back(
                jnp.where(lanes < HALF, sides[0], sides[1]), qk_ref[rows, cols], cos_ref[rows, :], sin_ref[rows, :], gq
            )
            dlow[rows, cols] = low
            head_sums[pl.ds(0, 8), :] += terms

        polled(pairs, attend_back, (sums, turns[qb]))
        low, terms = head_back(
            dk[rows, :], qk_ref[rows, pl.ds(q_cols, LANES)], cos_ref[rows, :], sin_ref[rows, :], gk
        )
        dlow[rows, pl.ds(q_cols, LANES)] = low
        dlow[rows, pl.ds(q_cols + LANES, LANES)] = dv[rows, :].astype(BF16)
        head_sums[pl.ds(8, 8), :] += terms
        part[rows, :] = dot_nt(dlow[rows, :], wqkv[...]).astype(BF16)
        final.send_core(qb)
        if qb < 3:
            final.send_back(qb + 1)
        final.send_across(qb)
        if qb == 2:
            scatter_o.start()
        if qb < 2:
            ahead(sums_o, 2)
    mine = head_slots.at[place.tensor]
    mine[...] = head_sums[...]
    head_copies = []
    for step in range(1, 4):
        copy = remote(
            mine, mine, small_send.at[step - 1], small_recv.at[step - 1], place.me, lax.rem(place.tensor + step, 4)
        )
        copy.start()
        head_copies.append(copy)
    for load in loads[9:]:
        load.wait()

    def qkv_grad(start):
        partial_qkv[pl.ds(start, 384), :] = dot_tn(n1_ref[:, pl.ds(start, 384)], dlow[...]).astype(BF16)

    blocks(width, 384, qkv_grad)
    scatter_qkv.start()
    sums_qkv = scatter_qkv.steps()
    for step, copy in enumerate(head_copies):
        whose = head_slots.at[lax.rem(place.tensor + 3 - step, 4)]
        remote(whose, whose, small_send.at[step], small_recv.at[step], place.me, place.tensor).wait_recv()
    heads = head_slots[0] + head_slots[1] + head_slots[2] + head_slots[3]
    ahead(sums_o, 2)
    g1 = gain_ref[pl.ds(0, 1), :]
    gain_one = jnp.zeros((8, width), F32)
    saves = []
    for index in reversed(range(4)):
        if index == 0:
            final.send_back(0)
        ahead(sums, 1)
        ahead(sums_o, 1)
        ahead(sums_qkv, 1)
        final.finish(index)

        def input_grad(sub, carry, index=index):
            rows = pl.ds(pl.multiple_of(index * tile + sub * 64, 64), 64)
            grad = dn1_ref[rows, :].astype(F32)
            x = x_ref[rows, :].astype(F32)
            inverse = lax.rsqrt(jnp.mean(x * x, axis=1, keepdims=True) + EPSILON)
            scaled = grad * g1
            inner = jnp.mean(scaled * x, axis=1, keepdims=True)
            dh_ref[rows, :] = dh_ref[rows, :] + inverse * scaled - x * (inverse * inverse * inverse * inner)
            return carry + jnp.sum((grad * x * inverse).reshape(8, 8, width), axis=0)

        gain_one = lax.fori_loop(0, tile // 64, input_grad, gain_one)
        rows = pl.ds(index * tile, tile)
        saves.append(begin(dh_ref.at[rows, :], grad_out.at[rows, :], copy_sems.at[index]))
    one = jnp.sum(gain_one, axis=0, keepdims=True)
    two = jnp.sum(two_ref[...], axis=0, keepdims=True)
    small[...] = jnp.zeros_like(small)
    q_sum = jnp.sum(heads[:8], axis=0, keepdims=True)
    k_sum = jnp.sum(heads[8:], axis=0, keepdims=True)
    q_sum = q_sum + pltpu.roll(q_sum, HALF, 1)
    k_sum = k_sum + pltpu.roll(k_sum, HALF, 1)

    def small_copy(d):
        return remote(
            small.at[d], slots.at[place.me], small_send.at[3 + d], small_recv.at[3 + place.me], d, place.tensor
        )

    for d in range(count):
        for row, (values, size) in enumerate(((one, own), (two, own), (q_sum, few), (k_sum, few))):
            small[d, pl.ds(row, 1), pl.ds(0, size)] = values[:, d * size : (d + 1) * size]
        pl.when(place.me != d)(lambda d=d: small_copy(d).start())
    slots[place.me] = small[place.me]
    drain(sums, sums_o, sums_qkv)
    for d in range(count):

        @pl.when(place.me != d)
        def _(d=d):
            remote(
                slots.at[d], slots.at[d], small_send.at[3 + d], small_recv.at[3 + d], d, place.tensor
            ).wait_recv()

    total = slots[0]
    for d in range(1, count):
        total = total + slots[d]
    small_ref[...] = total
    for d in range(count):
        pl.when(place.me != d)(lambda d=d: small_copy(d).wait_send())
    for save in saves:
        save.wait()
    for copy in head_copies:
        copy.wait_send()
    for each in (scatter, scatter_o, scatter_qkv, final):
        each.settle()


def last_call(count, part, dwo, dm, qm, kb, vb, lse, qk, n1, w0, x, dh, cosine, sine, seg_row, gains, two):
    seq, width = n1.shape
    rows = width // count
    q_cols = dwo.shape[1]
    low = qk.shape[1] + LANES
    shape = jax.ShapeDtypeStruct
    dma = pltpu.SemaphoreType.DMA
    loaded = [part, dwo, dm, qm, kb, vb, lse, qk, n1, jax.ShapeDtypeStruct((width, low), BF16), x, dh, cosine, sine]
    small = (8, 2 * LANES)
    return pl.pallas_call(
        functools.partial(last_kernel, count),
        out_shape=[
            shape((seq, width), F32),
            shape((rows, part.shape[1] // 2), F32),
            shape((rows, part.shape[1] // 2), F32),
            shape((rows, q_cols), F32),
            shape((rows, low), F32),
            shape(small, F32),
        ],
        in_specs=[in_place()] * 14 + [whole_block()] * 3,
        out_specs=[in_place()] + [whole_block()] * 5,
        scratch_shapes=[
            *[pltpu.VMEM(one.shape, one.dtype) for one in loaded],
            pltpu.VMEM((seq, LANES), F32),
            pltpu.VMEM((width, low), BF16),
            pltpu.VMEM((seq // 4, seq), F32),
            pltpu.VMEM((seq, LANES), F32),
            pltpu.VMEM((seq, LANES), F32),
            pltpu.VMEM((16, LANES), F32),
            pltpu.VMEM((seq, low), BF16),
            pltpu.VMEM((seq, width), BF16),
            pltpu.VMEM((seq, width), BF16),
            pltpu.VMEM((count,) + small, F32),
            pltpu.VMEM((count,) + small, F32),
            pltpu.VMEM((4, 16, LANES), F32),
            *TensorSum.scratch(seq, width, 4, BF16),
            dma((count + 3,)),
            dma((count + 3,)),
            dma((14,)),
            *Scatter.scratch(count, rows, part.shape[1], late_share(rows, 1 / 6)),
            *Scatter.scratch(count, rows, q_cols, late_share(rows, 1 / 6)),
            *Scatter.scratch(count, rows, low, late_share(rows, 1 / 6)),
        ],
        compiler_params=pltpu.CompilerParams(
            collective_id=4, has_side_effects=True, vmem_limit_bytes=61 << 20
        ),
    )(part, dwo, dm, qm, kb, vb, lse, qk, n1, w0, x, dh, cosine, sine, seg_row, gains, two)


def rotary_rows():
    lane = np.arange(LANES)
    frequency = ROPE_BASE ** (-(lane % (HALF // 2)) * 2.0 / HALF)
    sign = np.where(lane % HALF < HALF // 2, -1.0, 1.0)
    return jnp.asarray(np.concatenate([frequency[None], sign[None], np.zeros((6, LANES))]).astype(np.float32))


def shards(
    block_input,
    segments,
    positions,
    norm1_gain,
    q_norm_gain,
    k_norm_gain,
    w_q,
    w_k,
    w_v,
    w_o,
    norm2_gain,
    w_gate,
    w_up,
    w_down,
    cotangent,
    *,
    n_dp,
    n_tensor,
):
    rows = w_q.shape[0]
    q_cols, kv_cols, ff_cols = w_q.shape[1], w_k.shape[1], w_gate.shape[1]
    small_gain = q_norm_gain.shape[0]
    seg_row, pos_row = segments[None, :], positions[None, :]
    pack_down = jnp.pad(w_down.T.astype(BF16), ((0, 0), (0, -ff_cols % LANES)))
    w0, w1, n1, qk, qm, kb, vb, lse, ctx, h, n2, cosine, sine, hq, gains = forward_call(
        n_dp, block_input, w_gate, w_up, seg_row, pos_row, rotary_rows(),
        norm1_gain[None, :], norm2_gain[None, :], q_norm_gain[None, :], k_norm_gain[None, :],
        w_q, w_k, w_v, w_o.T.astype(BF16),
    )
    first, second, dn2, mlp, down = mlp_call(n_dp, n2, cotangent, w1, hq, pack_down)
    output_rows = lax.psum(mlp, "tensor")
    dh, dm, dwo, gate_one, up_one, small_two = middle_call(
        n_dp, first, dn2, h, cotangent, w0, ctx, gains
    )
    grad_input, gate_two, up_two, grad_o, grad_qkv, small = last_call(
        n_dp, second, dwo, dm, qm, kb, vb, lse, qk, n1, w0, block_input, dh,
        cosine, sine, seg_row, gains, small_two,
    )
    return (
        output_rows,
        grad_input,
        small[0, :rows],
        small[2, :small_gain],
        small[3, :small_gain],
        grad_qkv[:, :q_cols],
        grad_qkv[:, q_cols : q_cols + kv_cols],
        grad_qkv[:, q_cols + kv_cols :],
        grad_o.T,
        small[1, :rows],
        jnp.concatenate([gate_one, gate_two], axis=1),
        jnp.concatenate([up_one, up_two], axis=1),
        down[:, :ff_cols].T,
    )


def solution(mesh):
    placed = (
        P("dp", None),
        P("dp"),
        P("dp"),
        P("dp"),
        P("dp"),
        P("dp"),
        P("dp", "tensor"),
        P("dp", "tensor"),
        P("dp", "tensor"),
        P("tensor", "dp"),
        P("dp"),
        P("dp", "tensor"),
        P("dp", "tensor"),
        P("tensor", "dp"),
        P("dp", None),
    )
    return jax.shard_map(
        functools.partial(shards, n_dp=mesh.shape["dp"], n_tensor=mesh.shape["tensor"]),
        mesh=mesh,
        in_specs=placed,
        out_specs=(
            P("dp", None),
            P("dp", None),
            P("dp"),
            P("dp"),
            P("dp"),
            P("dp", "tensor"),
            P("dp", "tensor"),
            P("dp", "tensor"),
            P("tensor", "dp"),
            P("dp"),
            P("dp", "tensor"),
            P("dp", "tensor"),
            P("tensor", "dp"),
        ),
        check_vma=False,
    )
```

```python
import functools

import jax
import jax.numpy as jnp
import numpy as np
from jax import lax
from jax.experimental import pallas as pl
from jax.experimental.pallas import tpu as pltpu
from jax.sharding import PartitionSpec as P

EPSILON = 1e-05
ROPE_BASE = 1000000.0
MASKED = -1e30


MESH = pl.DeviceIdType.MESH
NEAR = 2
HALF = 64
LANES = 128
HIGHEST = lax.Precision.HIGHEST
BF16 = jnp.bfloat16
F32 = jnp.float32


def whole_block():
    return pl.BlockSpec(memory_space=pltpu.VMEM)


def in_place():
    return pl.BlockSpec(memory_space=pl.ANY)


def remote(src, dst, send, recv, dp, tensor):
    return pltpu.make_async_remote_copy(
        src_ref=src,
        dst_ref=dst,
        send_sem=send,
        recv_sem=recv,
        device_id=(dp, tensor),
        device_id_type=MESH,
    )


def begin(src, dst, sem):
    copy = pltpu.make_async_copy(src, dst, sem)
    copy.start()
    return copy


def dot_nn(left, right):
    return jnp.dot(left, right, preferred_element_type=F32)


def dot_nt(left, right):
    return lax.dot_general(left, right, (((1,), (1,)), ((), ())), preferred_element_type=F32)


def dot_tn(left, right):
    return lax.dot_general(left, right, (((0,), (0,)), ((), ())), preferred_element_type=F32)


class Place:
    def __init__(self, count):
        self.count = count
        self.depth = count // NEAR
        self.me = lax.axis_index("dp")
        self.tensor = lax.axis_index("tensor")
        self.far = self.me // NEAR
        self.near = lax.rem(self.me, NEAR)
        self.core = lax.rem(self.tensor, 2)
        self.mate = self.tensor + 1 - 2 * self.core
        self.across = lax.rem(self.tensor + 2, 4)
        self.beside = self.me + 1 - 2 * self.near

    def ahead(self, step):
        return lax.rem(self.far + step, self.depth)

    def behind(self, step):
        return lax.rem(self.far + self.depth - step, self.depth)

    def greet(self, everyone, tensor):
        barrier = pltpu.get_barrier_semaphore()
        peers = []
        if everyone:
            peers += [(lax.rem(self.me + d, self.count), self.tensor) for d in range(1, self.count)]
        else:
            peers += [
                (self.ahead(step) * NEAR + self.near, self.tensor) for step in range(1, self.depth)
            ]
            peers.append((self.beside, self.tensor))
        if tensor:
            peers += [(self.me, lax.rem(self.tensor + t, 4)) for t in range(1, 4)]
        for peer in peers:
            pl.semaphore_signal(barrier, 1, device_id=peer, device_id_type=MESH)
        pl.semaphore_wait(barrier, len(peers))


class Gather:
    def __init__(self, place, shard, full, late, sems):
        self.place, self.shard, self.full = place, shard, full
        self.rows = shard.shape[0]
        self.cuts = [(0, self.rows - late)] + ([(self.rows - late, late)] if late else [])
        self.zsend, self.zrecv, self.ysend, self.yrecv, self.own = sems
        self.sent = []

    @staticmethod
    def sems(count):
        depth = count // NEAR
        dma = pltpu.SemaphoreType.DMA
        return [dma((2, depth - 1, 3)), dma((2, depth - 1, 3)), dma((2 * depth - 1, 2)), dma((2 * depth - 1, 2)), dma]

    def spot(self, block, cut):
        start, size = self.cuts[cut]
        return self.full.at[pl.ds(pl.multiple_of(block * self.rows + start, 16), size), :]

    def mine(self, cut):
        start, size = self.cuts[cut]
        return self.shard.at[pl.ds(start, size), :]

    def block(self, way, step, other):
        far = self.place.far - step if way == 0 else self.place.far + step
        return far * NEAR + (1 - self.place.near if other else self.place.near)

    def valid(self, way, step):
        return self.place.far >= step if way == 0 else self.place.far + step < self.place.depth

    def emit(self, make):
        copy, when = make()
        if when is None:
            copy.start()
        else:
            pl.when(when)(copy.start)
        self.sent.append(make)

    def along(self, way, step, cut, other, turn=None):
        place = self.place
        if step >= place.depth - 1:
            return

        def make():
            more = place.far < place.depth - 1 if way == 0 else place.far > 0
            spot = self.spot(self.block(way, step, other), cut)
            copy = remote(
                self.mine(cut) if step == 0 and not other else spot, spot,
                self.zsend.at[way, step, cut + other], self.zrecv.at[way, step, cut + other],
                place.me + (NEAR if way == 0 else -NEAR), place.tensor,
            )
            when = more if step == 0 else more & self.valid(way, step)
            return copy, when if turn is None else when & turn()

        self.emit(make)

    def crossing(self, way, step, cut, other):
        place = self.place
        spot = self.spot(self.block(way, step, other), cut)
        slot = step if way == 0 else step + place.depth - 1
        return remote(
            self.mine(cut) if step == 0 and not other else spot, spot,
            self.ysend.at[slot, cut], self.yrecv.at[slot, cut], place.beside, place.tensor,
        ), (self.valid(way, step) if step else None)

    def over(self, way, step, cut):
        self.emit(lambda: self.crossing(way, step, cut, 0))

    def came_over(self, way, step, cut):
        copy, when = self.crossing(way, step, cut, 1)
        if when is None:
            copy.wait_recv()
        else:
            pl.when(when)(copy.wait_recv)

    def start(self):
        place = self.place
        self.local = lambda: pltpu.make_async_copy(
            self.shard, self.full.at[pl.ds(pl.multiple_of(place.me * self.rows, 16), self.rows), :], self.own
        )
        self.local().start()
        for cut in reversed(range(len(self.cuts))):
            self.over(0, 0, cut)
        for way in range(2):
            self.along(way, 0, 0, 0)
            if len(self.cuts) > 1:
                self.along(way, 0, 1, 0, lambda way=way: jnp.logical_not(self.valid(way, 1)))

    def ends(self, way, step):
        return self.valid(way, step) & jnp.logical_not(self.valid(way, step + 1))

    def arrive(self, way, step, cut, other):
        place = self.place
        spot = self.spot(self.block(way, step, other), cut)
        copy = remote(
            spot, spot, self.zsend.at[way, step - 1, cut + other], self.zrecv.at[way, step - 1, cut + other],
            place.me, place.tensor,
        )
        pl.when(self.valid(way, step))(copy.wait_recv)
        self.along(way, step, cut, other)

    def steps(self):
        late = len(self.cuts) > 1
        if late:
            self.came_over(0, 0, 1)
            for way in range(2):
                self.along(way, 0, 1, 1, lambda way=way: jnp.logical_not(self.valid(way, 1)))
            yield
        for step in range(1, self.place.depth):
            for way in range(2):
                self.arrive(way, step, 0, 0)
                self.over(way, step, 0)
                if late:
                    for other in range(2):
                        self.along(way, 0, 1, other, lambda way=way, step=step: self.ends(way, step))
                yield
        if late:
            for step in range(1, self.place.depth):
                for other in range(2):
                    for way in range(2):
                        self.arrive(way, step, 1, other)
                    yield

    def finish(self):
        self.came_over(0, 0, 0)
        for step in range(1, self.place.depth):
            for way in range(2):
                self.came_over(way, step, 0)
        self.local().wait()

    def settle(self):
        for make in self.sent:
            copy, when = make()
            if when is None:
                copy.wait_send()
            else:
                pl.when(when)(copy.wait_send)


def late_share(rows, share):
    return int(rows * share) // 16 * 16


class TensorSum:
    def __init__(self, place, part, total, tiles, scratch):
        self.place, self.part, self.total, self.tiles = place, part, total, tiles
        self.tile = part.shape[0] // tiles
        self.half = self.tile // 2
        self.near, self.chip, self.far, self.sems = scratch
        self.sent = []

    @staticmethod
    def scratch(rows, width, tiles, kind):
        half = (rows // 2, width)
        return [
            pltpu.VMEM(half, kind), pltpu.VMEM(half, BF16), pltpu.VMEM(half, BF16), pltpu.SemaphoreType.DMA((6, tiles))
        ]

    def half_rows(self, index, which):
        return pl.ds(pl.multiple_of(index * self.tile + which * self.half, 16), self.half)

    def slot(self, index):
        return pl.ds(index * self.half, self.half)

    def core_copy(self, index):
        place = self.place
        return remote(
            self.part.at[self.half_rows(index, 1 - place.core), :], self.near.at[self.slot(index), :],
            self.sems.at[0, index], self.sems.at[1, index], place.me, place.mate,
        )

    def across_copy(self, index):
        place = self.place
        return remote(
            self.chip.at[self.slot(index), :], self.far.at[self.slot(index), :],
            self.sems.at[2, index], self.sems.at[3, index], place.me, place.across,
        )

    def back_copy(self, index, which):
        place = self.place
        rows = self.half_rows(index, which)
        return remote(
            self.total.at[rows, :], self.total.at[rows, :],
            self.sems.at[4, index], self.sems.at[5, index], place.me, place.mate,
        )

    def send_core(self, index):
        self.core_copy(index).start()
        self.sent.append(lambda: self.core_copy(index))

    def send_across(self, index):
        place = self.place
        self.core_copy(index).wait_recv()
        mine = self.part[self.half_rows(index, place.core), :].astype(F32)
        self.chip[self.slot(index), :] = (mine + self.near[self.slot(index), :].astype(F32)).astype(BF16)
        self.across_copy(index).start()
        self.sent.append(lambda: self.across_copy(index))

    def send_back(self, index):
        place = self.place
        self.across_copy(index).wait_recv()
        both = self.chip[self.slot(index), :].astype(F32) + self.far[self.slot(index), :].astype(F32)
        self.total[self.half_rows(index, place.core), :] = both.astype(self.total.dtype)
        self.back_copy(index, place.core).start()

    def finish(self, index):
        self.back_copy(index, 1 - self.place.core).wait_recv()
        self.back_copy(index, self.place.core).wait_send()

    def steps(self):
        for index in range(2):
            self.send_across(index)
            yield
        for index in range(self.tiles):
            self.send_back(index)
            if index + 2 < self.tiles:
                self.send_across(index + 2)
            yield

    def settle(self):
        for make in self.sent:
            make().wait_send()


def lane_ids(width=LANES):
    return lax.broadcasted_iota(jnp.int32, (1, width), 1)


def head_mean(values):
    row = lax.broadcasted_iota(jnp.int32, (LANES, LANES), 0)
    col = lax.broadcasted_iota(jnp.int32, (LANES, LANES), 1)
    groups = jnp.where(row // HALF == col // HALF, 1.0 / HALF, 0.0).astype(F32)
    return jnp.dot(values, groups, precision=HIGHEST, preferred_element_type=F32)


def turn(values, cosine, sine):
    ahead = pltpu.roll(values, LANES - HALF // 2, 1)
    back = pltpu.roll(values, HALF // 2, 1)
    first = lax.rem(lane_ids(), HALF) < HALF // 2
    return values * cosine + jnp.where(first, ahead, back) * sine


def column_of(row_ref, column):
    for index in range(row_ref.shape[1] // LANES):
        spot = pl.ds(index * LANES, LANES)
        row = row_ref[:, spot].astype(F32)
        column[spot, :] = jnp.broadcast_to(row, (LANES, LANES)).T


def bias_block(seg_col, seg_row, bias, first, tile):
    last = first + tile
    rows = lax.broadcasted_iota(jnp.int32, (tile, last), 0) + first
    cols = lax.broadcasted_iota(jnp.int32, (tile, last), 1)
    same = seg_col[pl.ds(first, tile), pl.ds(0, 1)] == seg_row[:, pl.ds(0, last)].astype(F32)
    allowed = same & (rows >= cols)
    bias[:, pl.ds(0, last)] = jnp.where(allowed, 0.0, MASKED)


def drain(*moves):
    for one in moves:
        for _ in one:
            pass


def ahead(moves, count=1):
    for _ in range(count):
        next(moves, None)


def polled(count, body, *polls):
    def step(index, carry):
        body(index)
        for at in range(count):
            due = [(moves, times[at]) for moves, times in polls if at in times]
            if due:

                @pl.when(index == at)
                def _(due=due):
                    for moves, times in due:
                        ahead(moves, times)

        return carry

    lax.fori_loop(0, count, step, 0)


def every(count, times=1, first=0):
    return {index: times for index in range(first, count)}


def blocks(total, size, body):
    def step(index, carry):
        body(pl.multiple_of(index * size, size))
        return carry

    lax.fori_loop(0, total // size, step, 0)


def forward_kernel(count, *refs):
    (
        x_hbm, gate_hbm, up_hbm, seg_row, pos_row, turn_ref, g1_ref, g2_ref, gq_ref, gk_ref,
        wq_ref, wk_ref, wv_ref, wot_ref,
        full_attn, full_gates, n1_out, qk_out, qm_out, kb_out, vb_out, lse_out, ctx_out, h_out, n2_out, cos_out, sin_out, hq_out,
        gains_out,
        x_ref, w0, n1_ref, qk_ref, qm_ref, kb_ref, vb_ref, lse_ref, ctx_ref, h_ref, n2_ref, cos_ref, sin_ref, hq_ref,
        column, pack_attn, pack_gates, gate_ref, up_ref, bias, gain_slots, part, total, tmp_near, tmp_chip, tmp_far, sum_sems, gain_send, gain_recv, copy_sems,
        *gather_sems,
    ) = refs
    place = Place(count)
    seq, width = x_ref.shape
    q_cols = ctx_ref.shape[1]
    kv_cols = kb_ref.shape[1]
    pairs = q_cols // LANES
    group = (q_cols // HALF) // (kv_cols // HALF)
    tile = seq // 4
    load = begin(x_hbm, x_ref, copy_sems.at[0])
    weights = [begin(gate_hbm, gate_ref, copy_sems.at[11]), begin(up_hbm, up_ref, copy_sems.at[12])]
    spot = 0
    for ref in (wq_ref, wk_ref, wv_ref, wot_ref):
        pack_attn[:, pl.ds(spot, ref.shape[1])] = ref[...].astype(BF16)
        spot += ref.shape[1]
    gain_slots[place.me] = jnp.zeros(gain_slots.shape[1:], F32)
    for row, ref in enumerate((g1_ref, g2_ref, gq_ref, gk_ref)):
        gain_slots[place.me, pl.ds(row, 1), pl.ds(0, ref.shape[1])] = ref[...].astype(BF16).astype(F32)
    place.greet(True, True)
    first = Gather(place, pack_attn, w0, late_share(pack_attn.shape[0], 1 / 6), gather_sems[:5])
    second = Gather(place, pack_gates, full_gates, late_share(pack_gates.shape[0], 1 / 6), gather_sems[5:])
    first.start()
    gain_copies = []
    for step in range(1, count):
        copy = remote(
            gain_slots.at[place.me], gain_slots.at[place.me], gain_send.at[step], gain_recv.at[step],
            lax.rem(place.me + step, count), place.tensor,
        )
        copy.start()
        gain_copies.append(copy)
    for weight in weights:
        weight.wait()
    even = gate_ref.shape[1] // LANES

    def lay(index, carry):
        cols = pl.ds(pl.multiple_of(index * LANES, LANES), LANES)
        for side, ref in enumerate((gate_ref, up_ref)):
            spot = pl.multiple_of((2 * index + side) * LANES, LANES)
            pack_gates[:, pl.ds(spot, LANES)] = ref[:, cols].astype(BF16)
        return carry

    lax.fori_loop(0, even, lay, 0)
    rest = pl.ds(even * LANES, HALF)
    pack_gates[:, pl.ds(2 * even * LANES, LANES)] = jnp.concatenate(
        [gate_ref[:, rest], up_ref[:, rest]], axis=1
    ).astype(BF16)
    column_of(pos_row, column)

    def angles(index, carry):
        rows = pl.ds(pl.multiple_of(index * LANES, LANES), LANES)
        angle = column[rows, pl.ds(0, 1)] * turn_ref[pl.ds(0, 1), :]
        cos_ref[rows, :] = jnp.cos(angle)
        sin_ref[rows, :] = jnp.sin(angle) * turn_ref[pl.ds(1, 1), :]
        return carry

    lax.fori_loop(0, seq // LANES, angles, 0)
    column_of(seg_row, column)
    for qb in range(4):
        bias_block(column, seg_row, bias.at[qb], qb * tile, tile)
    for step in range(1, count):
        whose = gain_slots.at[lax.rem(place.me + count - step, count)]
        remote(whose, whose, gain_send.at[step], gain_recv.at[step], place.me, place.tensor).wait_recv()
    gains_out[...] = jnp.zeros_like(gains_out)
    own = width // count
    for row in range(2):
        gains_out[pl.ds(row, 1), :] = jnp.concatenate(
            [gain_slots[d, pl.ds(row, 1), pl.ds(0, own)] for d in range(count)], axis=1
        )
    for row in range(2, 4):
        gains_out[pl.ds(row, 1), pl.ds(0, LANES)] = jnp.concatenate(
            [gain_slots[d, pl.ds(row, 1), pl.ds(0, HALF // count)] for d in range(count)] * 2, axis=1
        )
    moves_first = first.steps()
    ahead(moves_first, 2)
    g1 = gains_out[pl.ds(0, 1), :]
    g2 = gains_out[pl.ds(1, 1), :]
    load.wait()

    def norm_one(index, carry):
        rows = pl.ds(pl.multiple_of(index * LANES, LANES), LANES)
        x = x_ref[rows, :].astype(F32)
        inverse = lax.rsqrt(jnp.mean(x * x, axis=1, keepdims=True) + EPSILON)
        n1_ref[rows, :] = (x * inverse * g1).astype(BF16)
        return carry

    lax.fori_loop(0, seq // LANES, norm_one, 0)
    saves = [
        begin(n1_ref, n1_out, copy_sems.at[1]),
        begin(cos_ref, cos_out, copy_sems.at[13]),
        begin(sin_ref, sin_out, copy_sems.at[14]),
    ]
    drain(moves_first)
    second.start()
    moves = second.steps()
    first.finish()
    saves.append(begin(w0, full_attn, copy_sems.at[2]))
    gq = gains_out[pl.ds(2, 1), pl.ds(0, LANES)]
    gk = gains_out[pl.ds(3, 1), pl.ds(0, LANES)]
    lanes = lane_ids()

    def project(index, carry):
        rows = pl.ds(pl.multiple_of(index * tile, tile), tile)
        qkv = dot_nn(n1_ref[rows, :], w0[:, pl.ds(0, q_cols + 2 * kv_cols)])
        qk_ref[rows, :] = qkv[:, : q_cols + kv_cols]
        vb_ref[rows, :] = qkv[:, q_cols + kv_cols :].astype(BF16)
        cosine, sine = cos_ref[rows, :], sin_ref[rows, :]
        for pair in range(pairs + 1):
            raw = qkv[:, pair * LANES : (pair + 1) * LANES]
            inverse = lax.rsqrt(head_mean(raw * raw) + EPSILON)
            turned = turn(raw * inverse * (gk if pair == pairs else gq), cosine, sine)
            if pair == pairs:
                kb_ref[rows, :] = turned.astype(BF16)
                continue
            swapped = pltpu.roll(turned, HALF, 1)
            for side in range(2):
                head = 2 * pair + side
                kv = head // group
                keep = (turned if side == kv else swapped).astype(BF16) * 0.125
                qm_ref[head, rows, :] = jnp.where(lanes // HALF == kv, keep, jnp.zeros_like(keep))
        return carry

    lax.fori_loop(0, 4, project, 0)
    for index, (src, dst) in enumerate(((qk_ref, qk_out), (qm_ref, qm_out), (kb_ref, kb_out), (vb_ref, vb_out))):
        saves.append(begin(src, dst, copy_sems.at[3 + index]))
    next(moves, None)

    for qb in range(4):
        last = (qb + 1) * tile
        rows = pl.ds(qb * tile, tile)

        def attend(pair, carry, last=last, rows=rows, qb=qb):
            halves, sums = [], []
            for side in range(2):
                head = 2 * pair + side
                kv = head // group
                logits = dot_nt(qm_ref[head, rows, :], kb_ref[pl.ds(0, last), :]) + bias[qb, :, pl.ds(0, last)]
                top = jnp.max(logits, axis=1, keepdims=True)
                expo = jnp.exp(logits - top)
                summed = jnp.sum(expo, axis=1, keepdims=True)
                probs = (expo * (1.0 / summed)).astype(BF16)
                got = dot_nn(probs, vb_ref[pl.ds(0, last), :])
                halves.append(jnp.where(kv == side, got, pltpu.roll(got, HALF, 1)))
                sums.append(top + jnp.log(summed))
            ctx_ref[rows, pl.ds(pl.multiple_of(pair * LANES, LANES), LANES)] = jnp.where(
                lanes < HALF, halves[0], halves[1]
            ).astype(BF16)
            carry = jnp.where(lanes == 2 * pair, sums[0], carry)
            return jnp.where(lanes == 2 * pair + 1, sums[1], carry)

        lse_ref[rows, :] = lax.fori_loop(0, pairs, attend, jnp.zeros((tile, LANES), F32))
        if qb > 1:
            next(moves, None)
    saves.append(begin(lse_ref, lse_out, copy_sems.at[7]))
    saves.append(begin(ctx_ref, ctx_out, copy_sems.at[8]))

    summed = TensorSum(place, part, total, 4, (tmp_near, tmp_chip, tmp_far, sum_sems))
    for index in range(4):
        rows = pl.ds(index * tile, tile)
        part[rows, :] = dot_nt(ctx_ref[rows, :], w0[:, pl.ds(q_cols + 2 * kv_cols, q_cols)])
        summed.send_core(index)
    summed.send_across(0)
    summed.send_across(1)
    next(moves, None)
    for index in range(4):
        summed.send_back(index)
        if index < 2:
            summed.send_across(index + 2)
        next(moves, None)
        summed.finish(index)

        def norm_two(sub, carry, index=index):
            rows = pl.ds(pl.multiple_of(index * tile + sub * LANES, LANES), LANES)
            h = x_ref[rows, :].astype(F32) + total[rows, :]
            h_ref[rows, :] = h
            hq_ref[rows, :] = (h * 0.25).astype(BF16)
            inverse = lax.rsqrt(jnp.mean(h * h, axis=1, keepdims=True) + EPSILON)
            n2_ref[rows, :] = (h * inverse * g2).astype(BF16)
            return carry

        lax.fori_loop(0, tile // LANES, norm_two, 0)
        next(moves, None)
    saves.append(begin(h_ref, h_out, copy_sems.at[9]))
    saves.append(begin(n2_ref, n2_out, copy_sems.at[10]))
    saves.append(begin(hq_ref, hq_out, copy_sems.at[15]))
    drain(moves)
    second.finish()
    for save in saves:
        save.wait()
    for copy in gain_copies:
        copy.wait_send()
    first.settle()
    second.settle()
    summed.settle()


def forward_call(count, x, gate, up, seg_row, pos_row, turns, g1, g2, gq, gk, wq, wk, wv, wot):
    seq, width = x.shape
    rows = wq.shape[0]
    q_cols, kv_cols = wq.shape[1], LANES
    attn_cols = wq.shape[1] + wk.shape[1] + wv.shape[1] + wot.shape[1]
    kept = [
        ((seq, width), BF16),
        ((seq, q_cols + kv_cols), F32),
        ((q_cols // HALF, seq, LANES), BF16),
        ((seq, LANES), BF16),
        ((seq, LANES), BF16),
        ((seq, LANES), F32),
        ((seq, q_cols), BF16),
        ((seq, width), F32),
        ((seq, width), BF16),
        ((seq, LANES), F32),
        ((seq, LANES), F32),
        ((seq, width), BF16),
    ]
    attn = ((count * rows, attn_cols), BF16)
    outs = [attn, ((count * rows, 2 * gate.shape[1]), BF16), *kept, ((8, width), F32)]
    dma = pltpu.SemaphoreType.DMA
    return pl.pallas_call(
        functools.partial(forward_kernel, count),
        out_shape=[jax.ShapeDtypeStruct(*out) for out in outs],
        in_specs=[in_place()] * 3 + [whole_block()] * 11,
        out_specs=[in_place()] * 14 + [whole_block()],
        scratch_shapes=[
            pltpu.VMEM((seq, width), BF16),
            pltpu.VMEM(*attn),
            *[pltpu.VMEM(*one) for one in kept],
            pltpu.VMEM((seq, LANES), F32),
            pltpu.VMEM((rows, attn_cols), BF16),
            pltpu.VMEM((rows, 2 * gate.shape[1]), BF16),
            pltpu.VMEM(gate.shape, F32),
            pltpu.VMEM(up.shape, F32),
            pltpu.VMEM((4, seq // 4, seq), F32),
            pltpu.VMEM((count, 8, 2 * LANES), F32),
            pltpu.VMEM((seq, width), F32),
            pltpu.VMEM((seq, width), F32),
            *TensorSum.scratch(seq, width, 4, F32),
            dma((count,)),
            dma((count,)),
            dma((16,)),
            *Gather.sems(count),
            *Gather.sems(count),
        ],
        compiler_params=pltpu.CompilerParams(
            collective_id=1, has_side_effects=True, vmem_limit_bytes=61 << 20
        ),
    )(x, gate, up, seg_row, pos_row, turns, g1, g2, gq, gk, wq, wk, wv, wot)


def store(ref, rows, value):
    ref[rows, :] = value


def store_apart(gate, up, rows, value):
    even = gate.shape[1] // LANES
    for index in range(even):
        cols = pl.ds(index * LANES, LANES)
        gate[rows, cols] = value[:, 2 * index * LANES : (2 * index + 1) * LANES]
        up[rows, cols] = value[:, (2 * index + 1) * LANES : (2 * index + 2) * LANES]
    if gate.shape[1] % LANES:
        rest = value[:, 2 * even * LANES :]
        cols = pl.ds(even * LANES, HALF)
        gate[rows, cols] = rest[:, :HALF]
        up[rows, cols] = pltpu.roll(rest, HALF, 1)[:, :HALF]


class Scatter:
    def __init__(self, place, partial, result, late, scratch, flight=2, source=None):
        self.place, self.partial = place, partial
        self.flight = flight
        self.source = partial if source is None else source
        self.put = result if callable(result) else functools.partial(store, result)
        self.rows = partial.shape[0] // place.count
        self.late = late
        early = self.rows - late
        half = (early // 2 + 15) // 16 * 16
        self.cuts = [(0, half), (half, early - half)] if early > half else [(0, early)]
        self.tail = (early, late)
        self.over_in, self.far_in, self.far_other, self.late_in = scratch[:4]
        self.zsend, self.zrecv, self.ysend, self.yrecv, self.lsend, self.lrecv = scratch[4:]
        self.sent = []
        depth = place.depth
        orders = [
            sorted(range(depth), key=lambda goal, far=far: (-abs(goal - far), -goal)) for far in range(depth)
        ]
        self.goals = []
        for index in range(depth):
            goal = jnp.int32(0)
            for far in range(depth):
                goal = goal + orders[far][index] * (place.far == far).astype(jnp.int32)
            self.goals.append(goal)
        self.pieces = [(index, cut) for index in range(depth) for cut in range(len(self.cuts))]

    @staticmethod
    def scratch(count, rows, width, late):
        depth = count // NEAR
        dma = pltpu.SemaphoreType.DMA
        return [
            pltpu.VMEM((depth, rows - late, width), BF16),
            pltpu.VMEM((depth + 2, rows, width), BF16),
            pltpu.VMEM((depth + 2, max(late, 16), width), BF16),
            pltpu.VMEM((max(late, 16), width), BF16),
            dma((depth - 1, 4)),
            dma((depth + 2, 4)),
            dma((depth, 2)),
            dma((depth, 2)),
            dma,
            dma,
        ]

    def spot(self, goal, other, start, size):
        near = 1 - self.place.near if other else self.place.near
        return pl.ds(pl.multiple_of((goal * NEAR + near) * self.rows + start, 16), size)

    def over(self, number):
        place = self.place
        index, cut = self.pieces[number]
        start, size = self.cuts[cut]
        return remote(
            self.source.at[self.spot(self.goals[index], True, start, size), :],
            self.over_in.at[index, pl.ds(start, size), :],
            self.ysend.at[index, cut], self.yrecv.at[index, cut], place.beside, place.tensor,
        )

    def cross(self, number):
        if number < len(self.pieces):
            self.over(number).start()
            self.sent.append(lambda: self.over(number))

    def start(self):
        self.start_far()
        self.start_near()

    def start_near(self):
        for number in range(self.flight):
            self.cross(number)

    def start_far(self):
        if self.late:
            for index in range(self.place.depth - 1):
                for item in (2, 3):
                    pl.when(jnp.logical_not(self.fed(index)))(lambda index=index, item=item: self.hop(index, item).start())

    def add(self, spot, sources):
        size = sources[0].shape[0]
        part = 32 if size % 32 == 0 else 16

        def body(index, carry):
            start = pl.multiple_of(index * part, 16)
            rows = pl.ds(pl.multiple_of(spot.start + start, 16), part)
            total = self.partial[rows, :].astype(F32)
            for source in sources:
                total = total + source[pl.ds(start, part), :].astype(F32)
            self.partial[rows, :] = total.astype(BF16)
            return carry

        lax.fori_loop(0, size // part, body, 0)

    def item(self, item):
        return (0, *self.cuts[item]) if item < 2 else (item - 2, *self.tail)

    def into(self, slot, item):
        other, start, size = self.item(item)
        return self.far_other.at[slot] if other else self.far_in.at[slot, pl.ds(start, size), :]

    def wait_far(self, slot, item):
        place = self.place
        into = self.into(slot, item)
        remote(
            into, into, self.zsend.at[0, item], self.zrecv.at[slot, item], place.me, place.tensor
        ).wait_recv()
        return into

    def hop(self, index, item):
        place = self.place
        goal = self.goals[index]
        sign = 2 * (goal > place.far).astype(jnp.int32) - 1
        ends = ((goal - place.far) * sign == 1).astype(jnp.int32)
        slot = goal + ends * (place.depth + (1 - sign) // 2 - goal)
        return remote(
            self.partial.at[self.spot(goal, *self.item(item)), :], self.into(slot, item),
            self.zsend.at[index, item], self.zrecv.at[slot, item], place.me + sign * NEAR, place.tensor,
        )

    def arrived(self, index, cut):
        number = index * len(self.cuts) + cut
        self.over(number).wait_recv()
        self.cross(number + self.flight)
        start, size = self.cuts[cut]
        return self.over_in.at[index, pl.ds(start, size), :]

    def fed(self, index):
        place = self.place
        up = self.goals[index] > place.far
        return (up & (place.far > 0)) | (jnp.logical_not(up) & (place.far < place.depth - 1))

    def pass_on(self, index, item, base):
        self.add(self.spot(self.goals[index], *self.item(item)), base)
        self.hop(index, item).start()

    def first(self, number):
        index, cut = self.pieces[number]
        came = self.arrived(index, cut)
        if index < self.place.depth - 1:
            pl.when(jnp.logical_not(self.fed(index)))(lambda: self.pass_on(index, cut, [came]))

    def then(self, index, item):
        base = [self.over_in.at[index, pl.ds(*self.cuts[item]), :]] if item < 2 else []
        pl.when(self.fed(index))(
            lambda: self.pass_on(index, item, base + [self.wait_far(self.goals[index], item)])
        )
        self.sent.append(lambda: self.hop(index, item))

    def close(self, item):
        place = self.place
        spot = self.spot(place.far, *self.item(item))
        for way, comes in enumerate((place.far > 0, place.far < place.depth - 1)):

            @pl.when(comes)
            def _(way=way):
                self.add(spot, [self.wait_far(place.depth + way, item)])

    def last(self):
        place = self.place
        return remote(
            self.partial.at[self.spot(place.far, True, *self.tail), :], self.late_in,
            self.lsend, self.lrecv, place.beside, place.tensor,
        )

    def far_steps(self):
        for index in range(self.place.depth - 1 if self.late else 0):
            for item in (2, 3):
                self.then(index, item)
            yield

    def steps(self, far=True):
        place = self.place
        cuts = len(self.cuts)
        passing = cuts * (place.depth - 1)
        for number in range(len(self.pieces) + cuts):
            if number < len(self.pieces):
                self.first(number)
            index = (number - 1) // cuts
            if far and self.late and number and (number - 1) % cuts == 0 and index < place.depth - 1:
                self.then(index, 2)
                self.then(index, 3)
            if cuts <= number < passing + cuts:
                self.then(*self.pieces[number - cuts])
            if number == len(self.pieces) - 1 and self.late:
                self.close(3)
                self.last().start()
                self.sent.append(self.last)
                self.close(2)
            if number >= passing + cuts:
                cut = number - passing - cuts
                start, size = self.cuts[cut]
                own = self.spot(place.far, 0, start, size)
                self.add(own, [self.over_in.at[place.depth - 1, pl.ds(start, size), :]])
                self.close(cut)
                self.put(pl.ds(start, size), self.partial[own, :].astype(F32))
            yield
        if self.late:
            start, size = self.tail
            self.last().wait_recv()
            self.put(
                pl.ds(start, size),
                self.partial[self.spot(place.far, 0, start, size), :].astype(F32) + self.late_in[...].astype(F32),
            )
            yield

    def settle(self):
        for make in self.sent:
            make().wait_send()


def mlp_kernel(count, shares, *refs):
    (
        n2_hbm, cot_hbm, gates_hbm, hq_hbm, pack_down,
        first_out, second_out, dn2_out, part_out, down_ref,
        n2_ref, cot_ref, dn2_part, dn2_ref, w1, w2, ab, hid, partial, near, chip, far, sum_sems, copy_sems, *rest,
    ) = refs
    place = Place(count)
    seq, width = n2_ref.shape
    both = w1.shape[1]
    even = both // (2 * LANES)
    split = first_out.shape[1]
    tile = seq // 4
    lanes = lane_ids()
    loads = [
        begin(src, dst, copy_sems.at[index])
        for index, (src, dst) in enumerate(((n2_hbm, n2_ref), (gates_hbm, w1), (cot_hbm, cot_ref)))
    ]
    place.greet(False, True)
    gather = Gather(place, pack_down, w2, shares[0], rest[:5])
    scatter = Scatter(place, partial, down_ref, shares[1], rest[5:])
    summed = TensorSum(place, dn2_part, dn2_ref, 4, (near, chip, far, sum_sems))
    gather.start()
    moves, sums, tensor = gather.steps(), scatter.steps(False), summed.steps()
    loads[0].wait()
    loads[1].wait()

    def gate_up(index):
        cols = pl.ds(pl.multiple_of(index * 2 * LANES, 2 * LANES), 2 * LANES)
        got = dot_nn(n2_ref[...], w1[:, cols])
        gate, up = got[:, :LANES], got[:, LANES:]
        sig = jax.nn.sigmoid(gate)
        act = gate * sig
        hid[:, pl.ds(pl.multiple_of(index * LANES, LANES), LANES)] = (act * up).astype(BF16)
        slope = up * sig * (1.0 + gate * (1.0 - sig))
        ab[:, cols] = jnp.concatenate([slope, act], axis=1).astype(BF16)

    polled(even, gate_up, (moves, {8: 1, 12: 1}))
    tail = pl.ds(2 * even * LANES, LANES)
    got = dot_nn(n2_ref[...], w1[:, tail])
    up = pltpu.roll(got, HALF, 1)
    sig = jax.nn.sigmoid(got)
    act = got * sig
    hid[:, pl.ds(even * LANES, LANES)] = jnp.where(lanes < HALF, act * up, 0.0).astype(BF16)
    slope = up * sig * (1.0 + got * (1.0 - sig))
    ab[:, tail] = jnp.where(lanes < HALF, slope, pltpu.roll(act, HALF, 1)).astype(BF16)
    loads[2].wait()

    def down_grad(index):
        rows = pl.ds(pl.multiple_of(index * 384, 384), 384)
        partial[rows, :] = dot_tn(cot_ref[:, rows], hid[...]).astype(BF16)

    polled(width // 384, down_grad, (moves, {1: 1, 3: 1}))
    scatter.start_far()
    drain(moves)
    drain(scatter.far_steps())
    gather.finish()
    scatter.start_near()

    def inner_grad(index):
        got = dot_nn(cot_ref[...], w2[:, pl.ds(pl.multiple_of(index * 2 * LANES, 2 * LANES), 2 * LANES)])
        for side in range(2):
            piece = got[:, side * LANES : (side + 1) * LANES]
            cols = pl.ds(pl.multiple_of(index * 4 * LANES + side * 2 * LANES, 2 * LANES), 2 * LANES)
            ab[:, cols] = (ab[:, cols].astype(F32) * jnp.concatenate([piece, piece], axis=1)).astype(BF16)

    polled(even // 2, inner_grad)
    got = dot_nn(cot_ref[...], w2[:, pl.ds((even - 1) * LANES, 2 * LANES)])
    piece = got[:, :LANES]
    cols = pl.ds(2 * (even - 1) * LANES, 2 * LANES)
    ab[:, cols] = (ab[:, cols].astype(F32) * jnp.concatenate([piece, piece], axis=1)).astype(BF16)
    piece = got[:, LANES:]
    piece = jnp.where(lanes < HALF, piece, pltpu.roll(piece, HALF, 1))
    ab[:, tail] = (ab[:, tail].astype(F32) * piece).astype(BF16)

    base = begin(hq_hbm, cot_ref, copy_sems.at[2])

    def normed_grad(index):
        rows = pl.ds(pl.multiple_of(index * tile, tile), tile)
        dn2_part[rows, :] = dot_nt(ab[rows, :], w1[...]).astype(BF16)
        for at in range(4):

            @pl.when(index == at)
            def _(at=at):
                summed.send_core(at)
                ahead(sums, 1)
                if at:
                    ahead(tensor, 1)

    lax.fori_loop(0, 4, lambda index, carry: (normed_grad(index), carry)[1], 0)

    def output_part(index):
        rows = pl.ds(pl.multiple_of(index * 256, 256), 256)
        cot_ref[:, rows] = (dot_nt(hid[...], w2[rows, :]) + cot_ref[:, rows].astype(F32)).astype(BF16)

    base.wait()
    polled(width // 256, output_part, (sums, {2: 1, 5: 1}), (tensor, {5: 1}))
    saves = [begin(cot_ref, part_out, copy_sems.at[4])]

    def gates_grad(index):
        rows = pl.ds(pl.multiple_of(index * 384, 384), 384)
        for low, high in ((0, split), (split, both)):
            w1[rows, pl.ds(low, high - low)] = dot_tn(n2_ref[:, rows], ab[:, pl.ds(low, high - low)]).astype(BF16)

    polled(width // 384, gates_grad, (sums, every(4)), (tensor, {1: 1, 3: 1}))
    saves.append(begin(w1.at[:, pl.ds(0, split)], first_out, copy_sems.at[5]))
    saves.append(begin(w1.at[:, pl.ds(split, both - split)], second_out, copy_sems.at[6]))
    drain(tensor, sums)
    for index in range(4):
        summed.finish(index)
    saves.append(begin(dn2_ref, dn2_out, copy_sems.at[3]))
    for save in saves:
        save.wait()
    gather.settle()
    scatter.settle()
    summed.settle()


def mlp_call(count, n2, cot, full_gates, hq, pack_down):
    seq, width = n2.shape
    rows, down = pack_down.shape
    shares = late_share(rows, 1 / 6), late_share(rows, 1 / 4)
    both = full_gates.shape[1]
    split = 14 * LANES
    shape = jax.ShapeDtypeStruct
    dma = pltpu.SemaphoreType.DMA
    return pl.pallas_call(
        functools.partial(mlp_kernel, count, shares),
        out_shape=[
            shape((width, split), BF16),
            shape((width, both - split), BF16),
            shape((seq, width), BF16),
            shape((seq, width), BF16),
            shape((rows, down), F32),
        ],
        in_specs=[in_place()] * 5,
        out_specs=[in_place()] * 4 + [whole_block()],
        scratch_shapes=[
            *[pltpu.VMEM((seq, width), BF16)] * 4,
            pltpu.VMEM((width, both), BF16),
            pltpu.VMEM((width, down), BF16),
            pltpu.VMEM((seq, both), BF16),
            pltpu.VMEM((seq, down), BF16),
            pltpu.VMEM((width, down), BF16),
            *TensorSum.scratch(seq, width, 4, BF16),
            dma((7,)),
            *Gather.sems(count),
            *Scatter.scratch(count, rows, down, shares[1]),
        ],
        compiler_params=pltpu.CompilerParams(
            collective_id=2, has_side_effects=True, vmem_limit_bytes=61 << 20
        ),
    )(n2, cot, full_gates, hq, pack_down)


def middle_kernel(count, *refs):
    (
        part_in, dn2_hbm, h_hbm, cot_hbm, w0_hbm, ctx_hbm, gain_ref,
        dh_out, dm_out, dwo_out, gate_ref, up_ref, small_ref,
        partial, dn2_ref, h_ref, cot_ref, wo, ctx_ref, dh_ref, dm_ref, dwo_ref, dhb, copy_sems, *rest,
    ) = refs
    place = Place(count)
    seq, width = dn2_ref.shape
    q_cols = ctx_ref.shape[1]
    heads = q_cols // HALF
    group = heads // 2
    tile = seq // 4
    lanes = lane_ids()
    load = begin(part_in, partial, copy_sems.at[0])
    place.greet(False, False)
    put = functools.partial(store_apart, gate_ref, up_ref)
    scatter = Scatter(place, partial, put, late_share(gate_ref.shape[0], 1 / 6), rest, 3, part_in)
    scatter.start_near()
    load.wait()
    scatter.start_far()
    loads = [
        begin(src, dst, copy_sems.at[index + 1])
        for index, (src, dst) in enumerate(
            (
                (dn2_hbm, dn2_ref), (h_hbm, h_ref), (cot_hbm, cot_ref),
                (w0_hbm.at[:, pl.ds(w0_hbm.shape[1] - q_cols, q_cols)], wo), (ctx_hbm, ctx_ref),
            )
        )
    ]
    sums = scatter.steps()
    g2 = gain_ref[pl.ds(1, 1), :]
    for load in loads:
        load.wait()
    small_ref[...] = jnp.zeros_like(small_ref)

    def residual_grad(index, carry):
        rows = pl.ds(pl.multiple_of(index * 64, 64), 64)
        grad = dn2_ref[rows, :].astype(F32)
        h = h_ref[rows, :]
        inverse = lax.rsqrt(jnp.mean(h * h, axis=1, keepdims=True) + EPSILON)
        scaled = grad * g2
        inner = jnp.mean(scaled * h, axis=1, keepdims=True)
        dh = cot_ref[rows, :].astype(F32) + inverse * scaled - h * (inverse * inverse * inverse * inner)
        dh_ref[rows, :] = dh
        dhb[rows, :] = dh.astype(BF16)
        return carry + jnp.sum((grad * h * inverse).reshape(8, 8, width), axis=0)

    def back(index):
        small_ref[...] += lax.fori_loop(
            index * (tile // 64), (index + 1) * (tile // 64), residual_grad, jnp.zeros((8, width), F32)
        )
        rows = pl.ds(pl.multiple_of(index * tile, tile), tile)
        dctx = dot_nn(dhb[rows, :], wo[...])
        for pair in range(heads // 2):
            value = dctx[:, pair * LANES : (pair + 1) * LANES]
            swapped = pltpu.roll(value, HALF, 1)
            for side in range(2):
                head = 2 * pair + side
                keep = value if side == head // group else swapped
                dm_ref[head, rows, :] = jnp.where(lanes // HALF == head // group, keep, 0.0).astype(BF16)

    polled(4, back, (sums, {1: 1, 2: 1, 3: 1}))
    saves = [
        begin(dh_ref, dh_out, copy_sems.at[7]),
        begin(dm_ref, dm_out, copy_sems.at[8]),
    ]

    def out_grad(index):
        rows = pl.ds(pl.multiple_of(index * 384, 384), 384)
        dwo_ref[rows, :] = dot_tn(dhb[:, rows], ctx_ref[...]).astype(BF16)

    polled(width // 384, out_grad, (sums, {1: 1, 3: 1}))
    saves.append(begin(dwo_ref, dwo_out, copy_sems.at[10]))
    drain(sums)
    for save in saves:
        save.wait()
    scatter.settle()


def middle_call(count, part, dn2, h, cot, w0, ctx, gains):
    seq, width = dn2.shape
    q_cols = ctx.shape[1]
    rows = width // count
    shape = jax.ShapeDtypeStruct
    dma = pltpu.SemaphoreType.DMA
    return pl.pallas_call(
        functools.partial(middle_kernel, count),
        out_shape=[
            shape((seq, width), F32),
            shape((q_cols // HALF, seq, LANES), BF16),
            shape((width, q_cols), BF16),
            shape((rows, part.shape[1] // 2), F32),
            shape((rows, part.shape[1] // 2), F32),
            shape((8, width), F32),
        ],
        in_specs=[in_place()] * 6 + [whole_block()],
        out_specs=[in_place()] * 3 + [whole_block()] * 3,
        scratch_shapes=[
            pltpu.VMEM(part.shape, BF16),
            pltpu.VMEM((seq, width), BF16),
            pltpu.VMEM((seq, width), F32),
            pltpu.VMEM((seq, width), BF16),
            pltpu.VMEM((width, q_cols), BF16),
            pltpu.VMEM((seq, q_cols), BF16),
            pltpu.VMEM((seq, width), F32),
            pltpu.VMEM((q_cols // HALF, seq, LANES), BF16),
            pltpu.VMEM((width, q_cols), BF16),
            pltpu.VMEM((seq, width), BF16),
            dma((11,)),
            *Scatter.scratch(count, rows, part.shape[1], late_share(rows, 1 / 6)),
        ],
        compiler_params=pltpu.CompilerParams(
            collective_id=3, has_side_effects=True, vmem_limit_bytes=61 << 20
        ),
    )(part, dn2, h, cot, w0, ctx, gains)


def last_kernel(count, *refs):
    (
        part_in, dwo_in, dm_hbm, qm_hbm, kb_hbm, vb_hbm, lse_hbm, qk_hbm, n1_hbm, w0_hbm, x_hbm, dh_hbm,
        cos_hbm, sin_hbm, seg_row, gain_ref, two_ref,
        grad_out, gate_ref, up_ref, out_ref, qkv_ref, small_ref,
        partial, partial_o, dm_ref, qm_ref, kb_ref, vb_ref, lse_ref, qk_ref, n1_ref, wqkv, x_ref, dh_ref, cos_ref, sin_ref,
        column, partial_qkv, bias, dk, dv, head_sums, dlow, part, dn1_ref, small, slots, head_slots,
        near, chip, far, sum_sems, small_send, small_recv, copy_sems, *rest,
    ) = refs
    place = Place(count)
    seq, width = n1_ref.shape
    kv_cols = kb_ref.shape[1]
    q_cols = qk_ref.shape[1] - kv_cols
    pairs = q_cols // LANES
    group = (q_cols // HALF) // (kv_cols // HALF)
    tile = seq // 4
    own = width // count
    few = HALF // count
    lanes = lane_ids()
    sources = (
        (part_in, partial), (dwo_in, partial_o), (qm_hbm, qm_ref), (kb_hbm, kb_ref), (lse_hbm, lse_ref),
        (dm_hbm, dm_ref), (vb_hbm, vb_ref), (qk_hbm, qk_ref), (cos_hbm, cos_ref), (sin_hbm, sin_ref),
        (w0_hbm.at[:, pl.ds(0, wqkv.shape[1])], wqkv), (n1_hbm, n1_ref), (x_hbm, x_ref), (dh_hbm, dh_ref),
    )
    loads = [begin(src, dst, copy_sems.at[index]) for index, (src, dst) in enumerate(sources[:2])]
    place.greet(True, True)
    third = len(rest) // 3
    late = late_share(gate_ref.shape[0], 1 / 6)
    scatter = Scatter(place, partial, functools.partial(store_apart, gate_ref, up_ref), late, rest[:third], 3, part_in)
    scatter_o = Scatter(place, partial_o, out_ref, late, rest[third : 2 * third], 8)
    scatter_qkv = Scatter(place, partial_qkv, qkv_ref, late, rest[2 * third :], 8)
    final = TensorSum(place, part, dn1_ref, 4, (near, chip, far, sum_sems))
    scatter.start_near()
    for load in loads:
        load.wait()
    scatter.start_far()
    loads = [begin(src, dst, copy_sems.at[index + 2]) for index, (src, dst) in enumerate(sources[2:])]
    column_of(seg_row, column)
    sums, sums_o = scatter.steps(), scatter_o.steps()
    dk[...] = jnp.zeros_like(dk)
    dv[...] = jnp.zeros_like(dv)
    gq = gain_ref[pl.ds(2, 1), pl.ds(0, LANES)]
    gk = gain_ref[pl.ds(3, 1), pl.ds(0, LANES)]
    for load in loads[:9]:
        load.wait()

    def head_back(grad, raw, cosine, sine, gain):
        back = turn(grad, cosine, -sine)
        inverse = lax.rsqrt(head_mean(raw * raw) + EPSILON)
        scaled = back * gain
        inner = head_mean(scaled * raw)
        low = inverse * scaled - raw * (inverse * inverse * inverse * inner)
        return low.astype(BF16), jnp.sum((back * raw * inverse).reshape(-1, 8, LANES), axis=0)

    head_sums[...] = jnp.zeros_like(head_sums)
    turns = {3: every(3), 2: every(3), 1: {0: 1, 2: 1}, 0: {2: 1}}
    for qb in reversed(range(4)):
        last = (qb + 1) * tile
        rows = pl.ds(qb * tile, tile)
        bias_block(column, seg_row, bias, qb * tile, tile)

        def attend_back(pair, last=last, rows=rows):
            keys = pl.ds(0, last)
            sides = []
            for side in range(2):
                head = 2 * pair + side
                kv = head // group
                query, grad = qm_ref[head, rows, :], dm_ref[head, rows, :]
                logsum = jnp.sum(jnp.where(lanes == head, lse_ref[rows, :], 0.0), axis=1, keepdims=True)
                logits = dot_nt(query, kb_ref[keys, :]) + bias[:, keys]
                probs = jnp.exp(logits - logsum)
                dprob = dot_nt(grad, vb_ref[keys, :])
                inner = jnp.sum(probs * dprob, axis=1, keepdims=True)
                ds = (probs * (dprob - inner)).astype(BF16)
                got = dot_nn(ds, kb_ref[keys, :]) * 0.125
                sides.append(jnp.where(kv == side, got, pltpu.roll(got, HALF, 1)))
                dk[keys, :] += dot_tn(ds, query)
                dv[keys, :] += dot_tn(probs.astype(BF16), grad)
            cols = pl.ds(pl.multiple_of(pair * LANES, LANES), LANES)
            low, terms = head_back(
                jnp.where(lanes < HALF, sides[0], sides[1]), qk_ref[rows, cols], cos_ref[rows, :], sin_ref[rows, :], gq
            )
            dlow[rows, cols] = low
            head_sums[pl.ds(0, 8), :] += terms

        polled(pairs, attend_back, (sums, turns[qb]))
        low, terms = head_back(
            dk[rows, :], qk_ref[rows, pl.ds(q_cols, LANES)], cos_ref[rows, :], sin_ref[rows, :], gk
        )
        dlow[rows, pl.ds(q_cols, LANES)] = low
        dlow[rows, pl.ds(q_cols + LANES, LANES)] = dv[rows, :].astype(BF16)
        head_sums[pl.ds(8, 8), :] += terms
        part[rows, :] = dot_nt(dlow[rows, :], wqkv[...]).astype(BF16)
        final.send_core(qb)
        if qb < 3:
            final.send_back(qb + 1)
        final.send_across(qb)
        if qb == 2:
            scatter_o.start()
        if qb < 2:
            ahead(sums_o, 2)
    mine = head_slots.at[place.tensor]
    mine[...] = head_sums[...]
    head_copies = []
    for step in range(1, 4):
        copy = remote(
            mine, mine, small_send.at[step - 1], small_recv.at[step - 1], place.me, lax.rem(place.tensor + step, 4)
        )
        copy.start()
        head_copies.append(copy)
    for load in loads[9:]:
        load.wait()

    def qkv_grad(start):
        partial_qkv[pl.ds(start, 384), :] = dot_tn(n1_ref[:, pl.ds(start, 384)], dlow[...]).astype(BF16)

    blocks(width, 384, qkv_grad)
    scatter_qkv.start()
    sums_qkv = scatter_qkv.steps()
    for step, copy in enumerate(head_copies):
        whose = head_slots.at[lax.rem(place.tensor + 3 - step, 4)]
        remote(whose, whose, small_send.at[step], small_recv.at[step], place.me, place.tensor).wait_recv()
    heads = head_slots[0] + head_slots[1] + head_slots[2] + head_slots[3]
    ahead(sums_o, 2)
    g1 = gain_ref[pl.ds(0, 1), :]
    gain_one = jnp.zeros((8, width), F32)
    saves = []
    for index in reversed(range(4)):
        if index == 0:
            final.send_back(0)
        ahead(sums, 1)
        ahead(sums_o, 1)
        ahead(sums_qkv, 1)
        final.finish(index)

        def input_grad(sub, carry, index=index):
            rows = pl.ds(pl.multiple_of(index * tile + sub * 64, 64), 64)
            grad = dn1_ref[rows, :].astype(F32)
            x = x_ref[rows, :].astype(F32)
            inverse = lax.rsqrt(jnp.mean(x * x, axis=1, keepdims=True) + EPSILON)
            scaled = grad * g1
            inner = jnp.mean(scaled * x, axis=1, keepdims=True)
            dh_ref[rows, :] = dh_ref[rows, :] + inverse * scaled - x * (inverse * inverse * inverse * inner)
            return carry + jnp.sum((grad * x * inverse).reshape(8, 8, width), axis=0)

        gain_one = lax.fori_loop(0, tile // 64, input_grad, gain_one)
        rows = pl.ds(index * tile, tile)
        saves.append(begin(dh_ref.at[rows, :], grad_out.at[rows, :], copy_sems.at[index]))
    one = jnp.sum(gain_one, axis=0, keepdims=True)
    two = jnp.sum(two_ref[...], axis=0, keepdims=True)
    small[...] = jnp.zeros_like(small)
    q_sum = jnp.sum(heads[:8], axis=0, keepdims=True)
    k_sum = jnp.sum(heads[8:], axis=0, keepdims=True)
    q_sum = q_sum + pltpu.roll(q_sum, HALF, 1)
    k_sum = k_sum + pltpu.roll(k_sum, HALF, 1)

    def small_copy(d):
        return remote(
            small.at[d], slots.at[place.me], small_send.at[3 + d], small_recv.at[3 + place.me], d, place.tensor
        )

    for d in range(count):
        for row, (values, size) in enumerate(((one, own), (two, own), (q_sum, few), (k_sum, few))):
            small[d, pl.ds(row, 1), pl.ds(0, size)] = values[:, d * size : (d + 1) * size]
        pl.when(place.me != d)(lambda d=d: small_copy(d).start())
    slots[place.me] = small[place.me]
    drain(sums, sums_o, sums_qkv)
    for d in range(count):

        @pl.when(place.me != d)
        def _(d=d):
            remote(
                slots.at[d], slots.at[d], small_send.at[3 + d], small_recv.at[3 + d], d, place.tensor
            ).wait_recv()

    total = slots[0]
    for d in range(1, count):
        total = total + slots[d]
    small_ref[...] = total
    for d in range(count):
        pl.when(place.me != d)(lambda d=d: small_copy(d).wait_send())
    for save in saves:
        save.wait()
    for copy in head_copies:
        copy.wait_send()
    for each in (scatter, scatter_o, scatter_qkv, final):
        each.settle()


def last_call(count, part, dwo, dm, qm, kb, vb, lse, qk, n1, w0, x, dh, cosine, sine, seg_row, gains, two):
    seq, width = n1.shape
    rows = width // count
    q_cols = dwo.shape[1]
    low = qk.shape[1] + LANES
    shape = jax.ShapeDtypeStruct
    dma = pltpu.SemaphoreType.DMA
    loaded = [part, dwo, dm, qm, kb, vb, lse, qk, n1, jax.ShapeDtypeStruct((width, low), BF16), x, dh, cosine, sine]
    small = (8, 2 * LANES)
    return pl.pallas_call(
        functools.partial(last_kernel, count),
        out_shape=[
            shape((seq, width), F32),
            shape((rows, part.shape[1] // 2), F32),
            shape((rows, part.shape[1] // 2), F32),
            shape((rows, q_cols), F32),
            shape((rows, low), F32),
            shape(small, F32),
        ],
        in_specs=[in_place()] * 14 + [whole_block()] * 3,
        out_specs=[in_place()] + [whole_block()] * 5,
        scratch_shapes=[
            *[pltpu.VMEM(one.shape, one.dtype) for one in loaded],
            pltpu.VMEM((seq, LANES), F32),
            pltpu.VMEM((width, low), BF16),
            pltpu.VMEM((seq // 4, seq), F32),
            pltpu.VMEM((seq, LANES), F32),
            pltpu.VMEM((seq, LANES), F32),
            pltpu.VMEM((16, LANES), F32),
            pltpu.VMEM((seq, low), BF16),
            pltpu.VMEM((seq, width), BF16),
            pltpu.VMEM((seq, width), BF16),
            pltpu.VMEM((count,) + small, F32),
            pltpu.VMEM((count,) + small, F32),
            pltpu.VMEM((4, 16, LANES), F32),
            *TensorSum.scratch(seq, width, 4, BF16),
            dma((count + 3,)),
            dma((count + 3,)),
            dma((14,)),
            *Scatter.scratch(count, rows, part.shape[1], late_share(rows, 1 / 6)),
            *Scatter.scratch(count, rows, q_cols, late_share(rows, 1 / 6)),
            *Scatter.scratch(count, rows, low, late_share(rows, 1 / 6)),
        ],
        compiler_params=pltpu.CompilerParams(
            collective_id=4, has_side_effects=True, vmem_limit_bytes=61 << 20
        ),
    )(part, dwo, dm, qm, kb, vb, lse, qk, n1, w0, x, dh, cosine, sine, seg_row, gains, two)


def rotary_rows():
    lane = np.arange(LANES)
    frequency = ROPE_BASE ** (-(lane % (HALF // 2)) * 2.0 / HALF)
    sign = np.where(lane % HALF < HALF // 2, -1.0, 1.0)
    return jnp.asarray(np.concatenate([frequency[None], sign[None], np.zeros((6, LANES))]).astype(np.float32))


def shards(
    block_input,
    segments,
    positions,
    norm1_gain,
    q_norm_gain,
    k_norm_gain,
    w_q,
    w_k,
    w_v,
    w_o,
    norm2_gain,
    w_gate,
    w_up,
    w_down,
    cotangent,
    *,
    n_dp,
    n_tensor,
):
    rows = w_q.shape[0]
    q_cols, kv_cols, ff_cols = w_q.shape[1], w_k.shape[1], w_gate.shape[1]
    small_gain = q_norm_gain.shape[0]
    seg_row, pos_row = segments[None, :], positions[None, :]
    pack_down = jnp.pad(w_down.T.astype(BF16), ((0, 0), (0, -ff_cols % LANES)))
    w0, w1, n1, qk, qm, kb, vb, lse, ctx, h, n2, cosine, sine, hq, gains = forward_call(
        n_dp, block_input, w_gate, w_up, seg_row, pos_row, rotary_rows(),
        norm1_gain[None, :], norm2_gain[None, :], q_norm_gain[None, :], k_norm_gain[None, :],
        w_q, w_k, w_v, w_o.T.astype(BF16),
    )
    first, second, dn2, mlp, down = mlp_call(n_dp, n2, cotangent, w1, hq, pack_down)
    output_rows = lax.psum(mlp, "tensor")
    dh, dm, dwo, gate_one, up_one, small_two = middle_call(
        n_dp, first, dn2, h, cotangent, w0, ctx, gains
    )
    grad_input, gate_two, up_two, grad_o, grad_qkv, small = last_call(
        n_dp, second, dwo, dm, qm, kb, vb, lse, qk, n1, w0, block_input, dh,
        cosine, sine, seg_row, gains, small_two,
    )
    return (
        output_rows,
        grad_input,
        small[0, :rows],
        small[2, :small_gain],
        small[3, :small_gain],
        grad_qkv[:, :q_cols],
        grad_qkv[:, q_cols : q_cols + kv_cols],
        grad_qkv[:, q_cols + kv_cols :],
        grad_o.T,
        small[1, :rows],
        jnp.concatenate([gate_one, gate_two], axis=1),
        jnp.concatenate([up_one, up_two], axis=1),
        down[:, :ff_cols].T,
    )


def solution(mesh):
    placed = (
        P("dp", None),
        P("dp"),
        P("dp"),
        P("dp"),
        P("dp"),
        P("dp"),
        P("dp", "tensor"),
        P("dp", "tensor"),
        P("dp", "tensor"),
        P("tensor", "dp"),
        P("dp"),
        P("dp", "tensor"),
        P("dp", "tensor"),
        P("tensor", "dp"),
        P("dp", None),
    )
    return jax.shard_map(
        functools.partial(shards, n_dp=mesh.shape["dp"], n_tensor=mesh.shape["tensor"]),
        mesh=mesh,
        in_specs=placed,
        out_specs=(
            P("dp", None),
            P("dp", None),
            P("dp"),
            P("dp"),
            P("dp"),
            P("dp", "tensor"),
            P("dp", "tensor"),
            P("dp", "tensor"),
            P("tensor", "dp"),
            P("dp"),
            P("dp", "tensor"),
            P("dp", "tensor"),
            P("tensor", "dp"),
        ),
        check_vma=False,
    )
```
